32 devices in a mesh: lon: 8 (over z, y), lat: 2 (over core), mem: 2 (over x).
Axes of the slice: x: 2, y: 2, z: 4, core: 2. Of those that a mesh axis runs over, the one named last changes fastest.
Arguments:
- inputs: bfloat16 [2, 48, 896, 512], P('mem', 'lat', 'lon'), may hold values from -6 to 6
- cotangent: bfloat16 [2, 48, 896, 512], P('mem', 'lat', 'lon'), may hold values from -6 to 6
- dw_kernel: bfloat16 [2, 9, 512], replicated, may hold values from -4 to 4
- pw_weight: bfloat16 [2, 512, 512], replicated, may hold values from -0.25 to 0.25
Outputs:
- input_grad: bfloat16 [2, 48, 896, 512], P('mem', 'lat', 'lon')
- kernel_grad: float32 [2, 9, 512], P(None, None, 'mem')
- weight_grad: float32 [2, 512, 512], P(None, None, 'mem')
The draws below stay inside these ranges and needn't reach their ends.
All inputs are finite; a program needn't handle non-finite values.
Results may differ from the reference program's by a relative error of at most 0.015.
Values may be sent and summed in bfloat16 or wider, within the bound.
A program may use at most 128 MiB of HBM per device.

```python
import math
import jax
import jax.numpy as jnp
from jax import lax

C = 512
KERNEL_SPACING = 4
TAPS = 9
LAYERS = 2
MEMBERS = 2
LAT = 48
LON = 896
SAMPLES = 86016


def draw_dw_kernel(key, part):
    key_scale, key_base = jax.random.split(jax.random.fold_in(key, 17))
    channel_scale = jnp.exp(jax.random.uniform(key_scale, (LAYERS, 1, C), jnp.float32, math.log(0.3), math.log(3.0)))
    base = jnp.clip(jax.random.normal(key_base, (LAYERS, TAPS, C), jnp.float32), -4.0, 4.0)
    return jnp.clip(base * channel_scale / 3.0, -4.0, 4.0).astype(jnp.bfloat16)


def block_levels(rng, extent, cuts, smallest, high):
    level = 1.0
    for position, parts in cuts:
        draws = jax.random.uniform(jax.random.fold_in(jax.random.fold_in(rng, 6), position), (parts,), jnp.float32, smallest / len(cuts), high / len(cuts))
        level = level * jnp.repeat(jnp.exp(draws), extent[position] // parts).reshape((-1,) + (1,) * (len(extent) - 1 - position))
    return level


def scatter_about(rng, extent, deviation, most, pieces=(), kind=jnp.bfloat16):
    entries = deviation * jax.random.normal(rng, extent, jnp.float32)
    if pieces:
        entries = entries * block_levels(rng, extent, pieces, -0.22, 0.18)
    return jnp.clip(entries, -most, most).astype(kind)


def setup_inputs(seed: int = 0) -> dict:
    splits = jax.random.split(jax.random.key(seed), 5)
    return {
        "inputs": scatter_about(splits[0], (MEMBERS, LAT, LON, C), 1.0, 6.0, ((0, 2), (1, 2), (2, 8))),
        "cotangent": scatter_about(splits[1], (MEMBERS, LAT, LON, C), 1.0, 6.0, ((0, 2), (1, 2), (2, 8))),
        "dw_kernel": draw_dw_kernel(jax.random.fold_in(splits[4], 71), 0),
        "pw_weight": scatter_about(splits[3], (LAYERS, C, C), C ** -0.5, 0.25),
    }


def widen(grid_field):
    periodic_field = jnp.concatenate([grid_field[:, -KERNEL_SPACING:], grid_field, grid_field[:, :KERNEL_SPACING]], axis=1)
    return jnp.pad(periodic_field, ((KERNEL_SPACING, KERNEL_SPACING), (0, 0), (0, 0)))

def stencil(padded_field, kernel, reversed_kernel):
    latitude_row_count = padded_field.shape[-3] - 2 * KERNEL_SPACING
    longitude_column_count = padded_field.shape[-2] - 2 * KERNEL_SPACING
    summed = jnp.zeros(padded_field.shape[:-3] + (latitude_row_count, longitude_column_count, padded_field.shape[-1]), jnp.float32)
    for padding_amount in range(3):
        for tap_position in range(3):
            row_shift = KERNEL_SPACING * (2 - padding_amount) if reversed_kernel else KERNEL_SPACING * padding_amount
            column_shift = KERNEL_SPACING * (2 - tap_position) if reversed_kernel else KERNEL_SPACING * tap_position
            stencil_window = padded_field[..., row_shift:row_shift + latitude_row_count, column_shift:column_shift + longitude_column_count, :].astype(jnp.float32)
            summed = summed + stencil_window * kernel[3 * padding_amount + tap_position].astype(jnp.float32)
    return summed

def normalize(conv_out):
    mean_sq = lax.optimization_barrier(jnp.mean(conv_out * conv_out, axis=-1, keepdims=True)) + 1e-06
    recip = lax.rsqrt(mean_sq)
    return (conv_out * recip, recip)

def forward_block(padded_field, kernel, weight):
    conv_out = stencil(padded_field, kernel, False)
    normed, recip = normalize(conv_out)
    hidden = normed.astype(jnp.bfloat16)
    width_c = hidden.shape[-1]
    pre_act = jnp.dot(hidden.reshape(-1, width_c), weight, preferred_element_type=jnp.float32).reshape(hidden.shape)
    interior_region = padded_field[..., KERNEL_SPACING:-KERNEL_SPACING, KERNEL_SPACING:-KERNEL_SPACING, :]
    output = (interior_region.astype(jnp.float32) + jax.nn.gelu(pre_act)).astype(jnp.bfloat16)
    return (output, hidden, pre_act, normed, recip)

def backward_block(padded_field, kernel, weight, saved, upstream, widen_fn):
    hidden, pre_act, normed, recip = saved
    _, pullback = jax.vjp(jax.nn.gelu, pre_act)
    grad_pre = pullback(upstream.astype(jnp.float32))[0].astype(jnp.bfloat16)
    width_c = hidden.shape[-1]
    flat_hidden = hidden.reshape(-1, width_c)
    flat_grad = grad_pre.reshape(-1, width_c)
    weight_term = lax.dot_general(flat_hidden, flat_grad, (((0,), (0,)), ((), ())), preferred_element_type=jnp.float32)
    grad_norm = lax.dot_general(flat_grad, weight, (((1,), (1,)), ((), ())), preferred_element_type=jnp.float32).reshape(hidden.shape)
    grad_conv = recip * (grad_norm - normed * lax.optimization_barrier(jnp.mean(grad_norm * normed, axis=-1, keepdims=True)))
    grad_conv = grad_conv.astype(jnp.bfloat16)
    latitude_row_count, longitude_column_count = (hidden.shape[-3], hidden.shape[-2])
    grad_wide = grad_conv.astype(jnp.float32)
    tap_sums = []
    for padding_amount in range(3):
        for tap_position in range(3):
            stencil_window = padded_field[..., KERNEL_SPACING * padding_amount:KERNEL_SPACING * padding_amount + latitude_row_count, KERNEL_SPACING * tap_position:KERNEL_SPACING * tap_position + longitude_column_count, :].astype(jnp.float32)
            tap_sums.append(lax.optimization_barrier(jnp.sum((stencil_window * grad_wide).reshape(-1, width_c), axis=0)))
    kernel_term = jnp.stack(tap_sums)
    back_in = upstream.astype(jnp.float32) + stencil(widen_fn(grad_conv), kernel, True)
    return (back_in.astype(jnp.bfloat16), kernel_term, weight_term)

def reference(inputs, cotangent, dw_kernel, pw_weight):

    def per_member(pair):
        member_in, member_cot = pair
        padded_in = widen(member_in)
        first = forward_block(padded_in, dw_kernel[0], pw_weight[0])
        padded_mid = widen(first[0])
        second = forward_block(padded_mid, dw_kernel[1], pw_weight[1])
        grad_mid, kernel_b, weight_b = backward_block(padded_mid, dw_kernel[1], pw_weight[1], second[1:], member_cot, widen)
        grad_in, kernel_a, weight_a = backward_block(padded_in, dw_kernel[0], pw_weight[0], first[1:], grad_mid, widen)
        return (grad_in, jnp.stack([kernel_a, kernel_b]), jnp.stack([weight_a, weight_b]))
    input_grad, kernel_terms, weight_terms = lax.map(per_member, (inputs, cotangent))
    factor = 1.0 / math.sqrt(SAMPLES)
    return (input_grad, lax.optimization_barrier(jnp.sum(kernel_terms, axis=0)) * factor, lax.optimization_barrier(jnp.sum(weight_terms, axis=0)) * factor)
```

```python
import functools
import math

import jax
import jax.numpy as jnp
from jax import lax
from jax.experimental import pallas as pl
from jax.experimental.pallas import tpu as pltpu
from jax.sharding import PartitionSpec as P

S = 4
F32 = jnp.float32
BF16 = jnp.bfloat16
MESH = pl.DeviceIdType.MESH
ROOT = math.sqrt(2.0 / math.pi)
CUBE = 0.044715


def gelu_both(x):
    xx = x * x
    t = jnp.tanh(x * (ROOT + (ROOT * CUBE) * xx))
    h = 0.5 + 0.5 * t
    g = x * h
    return g, h + g * (1.0 - t) * (ROOT + (3.0 * ROOT * CUBE) * xx)


def kernel(n, factor, scoped, *refs):
    pl.run_scoped(lambda *inner: work(n, factor, *refs, *inner), *scoped)


def work(
    n, factor,
    x_hbm, cot_hbm, dw_ref, w_ref,
    out_hbm, kgrad, wgrad,
    raw, cotraw, perm, unperm, kacc, wacc,
    w0s, w0r, w1s, w1r, w2s, w2r, w3s, w3r, kv, kr0, ks1, kr1, ks2, kr2,
    in_sem, out_sem, rim_s, rim_r, red_s, red_r,
    u0p, u1p, g1p, g0p, g1, hid0, hid1, gp, d0, rc0, rc1, pre, gn, kb,
):
    R, A, T, C = hid0.shape
    M = A * T
    H = C // 2
    CH = max(c for c in (1, 2, 4) if A % c == 0)
    WIDE = max(c for c in (1, 2, 4, 7) if A % c == 0)
    groups = [slice(g, g + 128) for g in range(0, C, 128)]
    me, lat, mem = lax.axis_index("lon"), lax.axis_index("lat"), lax.axis_index("mem")
    other, omem = 1 - lat, 1 - mem

    def lon_at(d):
        return lax.rem(me + (d % n), n)

    def dev(lon_i, lat_i, mem_i):
        return {"lon": lon_i, "lat": lat_i, "mem": mem_i}

    def planned(src, dst, ssem, rsem, where):
        return pltpu.make_async_remote_copy(
            src_ref=src, dst_ref=dst, send_sem=ssem, recv_sem=rsem, device_id=where, device_id_type=MESH
        )

    def in_copy(i, r):
        src, dst = ((x_hbm, raw), (cot_hbm, cotraw))[i]
        return pltpu.make_async_copy(src.at[0, pl.ds(S * r, S)], dst.at[pl.ds(S * r, S)], in_sem.at[i, r])

    for i in range(2):
        for r in range(R):
            in_copy(i, r).start()

    barrier = pltpu.get_barrier_semaphore()
    for d in range(n):
        for la in (lat, other):
            if d == 0 and la is lat:
                continue
            pl.semaphore_signal(barrier, inc=1, device_id=dev(lon_at(d), la, mem), device_id_type=MESH)
    pl.semaphore_signal(barrier, inc=1, device_id=dev(me, lat, omem), device_id_type=MESH)

    def one_hot(rows_dim):
        o = lax.broadcasted_iota(jnp.int32, (M, M), rows_dim)
        i = lax.broadcasted_iota(jnp.int32, (M, M), 1 - rows_dim)
        a, s, b = o >> 4, (o >> 2) & 3, o & 3
        return jnp.where(i == s * (A * S) + a * S + b, 1.0, 0.0).astype(BF16)

    perm[...] = one_hot(0)
    unperm[...] = one_hot(1)
    for l in range(2):
        taps_f = dw_ref[l].astype(F32)
        for t in range(9):
            kb[l, t] = jnp.broadcast_to(taps_f[t : t + 1, :], (T, C)).astype(BF16)
    kacc[...] = jnp.zeros_like(kacc)
    kv[...] = jnp.zeros_like(kv)
    edge = lat * (R + 1)
    for ref in (u0p, u1p, g1p, g0p):
        ref[edge] = jnp.zeros(ref.shape[1:], BF16)

    def rows_loop(lo, hi, fn):
        def step(r, c):
            fn(r)
            return c

        lax.fori_loop(lo, hi, step, 0)

    def regroup(src, r):
        rows = src[pl.ds(S * r, S)].reshape(M, C)
        return jnp.dot(perm[...], rows, preferred_element_type=F32).astype(BF16).reshape(A, T, C)

    def load0(r):
        in_copy(0, r).wait()
        u0p[1 + r, 1 : A + 1] = regroup(raw, r)

    rows_loop(0, R, load0)

    pl.semaphore_wait(barrier, 2 * n)

    right, left = lon_at(1), lon_at(-1)

    def send_rims(e, first, moves):
        return [
            planned(s, d, rim_s.at[e, i + first], rim_r.at[e, i + first], w) for i, (s, d, w) in enumerate(moves)
        ]

    def lon_rims(ref, e):
        moves = (
            (ref.at[pl.ds(1, R), pl.ds(A, 1)], ref.at[pl.ds(1, R), pl.ds(0, 1)], dev(right, lat, mem)),
            (ref.at[pl.ds(1, R), pl.ds(1, 1)], ref.at[pl.ds(1, R), pl.ds(A + 1, 1)], dev(left, lat, mem)),
        )
        return send_rims(e, 0, moves)

    def lat_rims(ref, e):
        row = R - lat * (R - 1)
        moves = (
            (ref.at[row, pl.ds(1, A)], ref.at[edge, pl.ds(1, A)], dev(me, other, mem)),
            (ref.at[row, pl.ds(A, 1)], ref.at[edge, pl.ds(0, 1)], dev(right, other, mem)),
            (ref.at[row, pl.ds(1, 1)], ref.at[edge, pl.ds(A + 1, 1)], dev(left, other, mem)),
        )
        return send_rims(e, 2, moves)

    def inward(i):
        return i + other * (R - 1 - 2 * i)

    def start(copies):
        for c in copies:
            c.start()

    def finish(copies):
        for c in copies:
            c.wait()

    def products(ref, r, a, ch, lanes, other_factor):
        for p in range(3):
            row = ref[r + p, pl.ds(a, ch + 2), :, lanes]
            yield [row[q : q + ch] * other_factor(p, q) for q in range(3)]

    def conv(ref, l, r, a, ch, lanes, rev):
        def tap(p, q):
            return kb[l, 3 * (2 - p) + 2 - q if rev else 3 * p + q, :, lanes]

        s0, s1, s2 = [v[0] + v[1] + v[2] for v in products(ref, r, a, ch, lanes, tap)]
        return s0 + s1 + s2

    def chunks(fn, ch, unroll=False):
        def step(i, c):
            fn(i * ch)
            return c

        lax.fori_loop(0, A // ch, step, 0, unroll=unroll)

    def tree(v):
        v = [v[i] for i in range(v.shape[0])]
        while len(v) > 1:
            v = [a + b for a, b in zip(v[::2], v[1::2])] + v[len(v) - len(v) % 2 :]
        return v[0]

    def add_taps(k, t, lanes, prod):
        both = tree(prod).astype(F32).reshape(2, 8, 128)
        kacc[k, t, :, lanes] += both[0] + both[1]

    def lane_mean(v, ch):
        m = jnp.sum(v.astype(F32), axis=-1, keepdims=True) * (1.0 / C)
        return jnp.broadcast_to(m, (ch, T, 128))

    def conv_norm(src, l, r, hid, rc, rr):
        ch = CH

        def go(a):
            convs = [conv(src, l, r, a, ch, lanes, False) for lanes in groups]
            c0, c1, c2, c3 = [c * c for c in convs]
            recip = lax.rsqrt(lane_mean((c0 + c1) + (c2 + c3), ch) + 1e-6)
            rc[rr, pl.ds(a, ch)] = recip
            for lanes, c in zip(groups, convs):
                hid[r, pl.ds(a, ch), :, lanes] = (c.astype(F32) * recip).astype(BF16)

        chunks(go, ch, True)

    def mix(v, l):
        return jnp.dot(v.reshape(M, C), w_ref[l], preferred_element_type=F32).reshape(A, T, C)

    def mix_back(v, l):
        return lax.dot_general(
            v.reshape(M, C), w_ref[l], (((1,), (1,)), ((), ())), preferred_element_type=F32
        ).astype(BF16).reshape(A, T, C)

    def norm_back(dst, hid, rc, r, rr):
        ch = CH

        def go(a):
            ns = [hid[r, pl.ds(a, ch), :, lanes] for lanes in groups]
            gs = [gn[pl.ds(a, ch), :, lanes] for lanes in groups]
            d0_, d1_, d2_, d3_ = [g * v for g, v in zip(gs, ns)]
            mean = lane_mean((d0_ + d1_) + (d2_ + d3_), ch)
            recip = rc[rr, pl.ds(a, ch)]
            for lanes, g, v in zip(groups, gs, ns):
                back = recip * (g.astype(F32) - v.astype(F32) * mean)
                dst[1 + r, pl.ds(1 + a, ch), :, lanes] = back.astype(BF16)

        chunks(go, ch, True)

    def weight_sum(l, hid):
        wacc[l] = jnp.zeros((C, C), F32)

        def go(r):
            wacc[l] += lax.dot_general(
                hid[r].reshape(M, C), gp[r].reshape(M, C), (((0,), (0,)), ((), ())), preferred_element_type=F32
            )

        rows_loop(0, R, go)

    own_rows = pl.ds(pl.multiple_of(lat * H, H), H)
    other_rows = pl.ds(pl.multiple_of(other * H, H), H)
    own_cols = pl.ds(pl.multiple_of(mem * H, H), H)
    other_cols = pl.ds(pl.multiple_of(omem * H, H), H)
    piece = H // n
    wire = w2s.dtype

    def red(l, stage, i, src, dst, where):
        c = planned(src, dst, red_s.at[l, stage, i], red_r.at[l, stage, i], where)
        c.start()
        return c

    def stage0(l):
        w0s[l] = wacc[l, other_rows, :].astype(BF16)
        return [red(l, 0, 0, w0s.at[l], w0r.at[l], dev(me, other, mem))]

    def taps_stage0():
        for k in range(2):
            for t in range(9):
                kv[k, t : t + 1, :] = jnp.sum(kacc[k, t], axis=0, keepdims=True)
        return [red(0, 0, 1, kv, kr0, dev(me, other, mem))]

    def taps_stage1():
        kv[...] += kr0[...]
        ks1[...] = kv[:, :, other_cols]
        return [red(0, 1, 1, ks1, kr1, dev(me, lat, omem))]

    def taps_stage2():
        both = (kv[:, :, own_cols] + kr1[...]).astype(BF16)
        ks2[...] = both
        kr2[me] = both
        return [red(0, 2, n + d, ks2, kr2.at[me], dev(lon_at(d), lat, mem)) for d in range(1, n)]

    def taps_stage3():
        ks = kr2[0].astype(F32)
        for j in range(1, n):
            ks = ks + kr2[j].astype(F32)
        for k in range(2):
            kgrad[k] = ks[k, :9, :] * factor
        return []

    def stage1(l):
        wacc[l, own_rows, :] += w0r[l].astype(F32)
        w1s[l] = wacc[l, own_rows, other_cols].astype(BF16)
        return [red(l, 1, 0, w1s.at[l], w1r.at[l], dev(me, lat, omem))]

    def stage2(l):
        total = wacc[l, own_rows, own_cols] + w1r[l].astype(F32)
        wacc[l, own_rows, own_cols] = total
        w2s[l] = total.reshape(n, piece, H).astype(wire)
        return [
            red(l, 2, d, w2s.at[l, lon_at(d)], w2r.at[l, me], dev(lon_at(d), lat, mem)) for d in range(1, n)
        ]

    def stage3(l):
        start = pl.multiple_of(lat * H + me * piece, piece)
        total = wacc[l, pl.ds(start, piece), own_cols]
        for d in range(1, n):
            total = total + w2r[l, lon_at(d)].astype(F32)
        done = (total * factor).astype(wire)
        w3s[l] = done
        w3r[l, lat, me] = done
        out = []
        for d in range(n):
            for k, la in enumerate((lat, other)):
                if d or k:
                    out.append(red(l, 3, k * n + d, w3s.at[l], w3r.at[l, lat, me], dev(lon_at(d), la, mem)))
        return out

    def stage4(l):
        wgrad[l] = w3r[l].reshape(C, H).astype(F32)

    moving = lat_rims(u0p, 0) + lon_rims(u0p, 0)
    start(moving)

    def load1(r):
        in_copy(1, r).wait()
        g1[r] = regroup(cotraw, r)

    rows_loop(0, R, load1)
    finish(moving)

    lats1 = lat_rims(u1p, 1)

    def block0(i):
        r = inward(i)
        conv_norm(u0p, 0, r, hid0, rc0, r)
        pre[...] = mix(hid0[r], 0)

        def go(a):
            for lanes in groups:
                gel, slope = gelu_both(pre[pl.ds(a, CH), :, lanes])
                d0[r, pl.ds(a, CH), :, lanes] = slope.astype(BF16)
                u = u0p[1 + r, pl.ds(1 + a, CH), :, lanes]
                u1p[1 + r, pl.ds(1 + a, CH), :, lanes] = u + gel.astype(BF16)

        chunks(go, CH)

        @pl.when(i == 0)
        def _():
            start(lats1)

    rows_loop(0, R, block0)
    lons = lon_rims(u1p, 1)
    start(lons)
    finish(lats1)
    finish(lons)

    lats2 = lat_rims(g1p, 2)

    def block1(i):
        r = inward(i)
        conv_norm(u1p, 1, r, hid1, rc1, 0)
        pre[...] = mix(hid1[r], 1)

        def go(a):
            for lanes in groups:
                slope = gelu_both(pre[pl.ds(a, CH), :, lanes])[1]
                g = g1[r, pl.ds(a, CH), :, lanes].astype(F32)
                gp[r, pl.ds(a, CH), :, lanes] = (g * slope).astype(BF16)

        chunks(go, CH)
        gn[...] = mix_back(gp[r], 1)
        norm_back(g1p, hid1, rc1, r, 0)

        @pl.when(i == 0)
        def _():
            start(lats2)

    rows_loop(0, R, block1)
    lons = lon_rims(g1p, 2)
    start(lons)
    weight_sum(1, hid1)
    sums = stage0(1)
    finish(lats2)
    finish(lons)

    def back0(i):
        r = inward(i)

        def go(a):
            for lanes in groups:
                u = u1p[1 + r, pl.ds(1 + a, CH), :, lanes]
                s = conv(g1p, 1, r, a, CH, lanes, True) + g1[r, pl.ds(a, CH), :, lanes]
                for p, row in enumerate(products(g1p, r, a, CH, lanes, lambda p, q: u)):
                    for q, v in enumerate(row):
                        add_taps(1, 3 * (2 - p) + 2 - q, lanes, v)
                g1[r, pl.ds(a, CH), :, lanes] = s
                gp[r, pl.ds(a, CH), :, lanes] = s * d0[r, pl.ds(a, CH), :, lanes]

        chunks(go, CH)
        gn[...] = mix_back(gp[r], 0)
        norm_back(g0p, hid0, rc0, r, r)

    cuts = [(R * i) // 3 for i in range(4)]
    lats3 = lat_rims(g0p, 3)
    rows_loop(0, 1, back0)
    start(lats3)
    for i, stage in enumerate((stage1, stage2, stage3)):
        rows_loop(max(cuts[i], 1), cuts[i + 1], back0)
        finish(sums)
        sums = stage(1)
    lons = lon_rims(g0p, 3)
    start(lons)
    weight_sum(0, hid0)
    finish(sums)
    sums = stage0(0)

    def taps0(r):
        def go(a):
            for lanes in groups:
                g = g0p[1 + r, pl.ds(1 + a, WIDE), :, lanes]
                for p, row in enumerate(products(u0p, r, a, WIDE, lanes, lambda p, q: g)):
                    for q, v in enumerate(row):
                        add_taps(0, 3 * p + q, lanes, v)

        chunks(go, WIDE)

    rows_loop(0, R, taps0)
    tap_sums = taps_stage0()
    finish(sums)
    sums = stage1(0)
    stage4(1)
    finish(lats3)
    finish(lons)

    def last(r):
        def go(a):
            for lanes in groups:
                s = conv(g0p, 0, r, a, WIDE, lanes, True) + g1[r, pl.ds(a, WIDE), :, lanes]
                hid1[r, pl.ds(a, WIDE), :, lanes] = s

        chunks(go, WIDE)
        rows = jnp.dot(unperm[...], hid1[r].reshape(M, C), preferred_element_type=F32).astype(BF16)
        raw[pl.ds(S * r, S)] = rows.reshape(S, S * A, C)

    out_copies = []
    tap_stages = (taps_stage1, taps_stage2, taps_stage3)
    for i, stage in enumerate((stage2, stage3, None)):
        rows_loop(cuts[i], cuts[i + 1], last)
        for r in range(cuts[i], cuts[i + 1]):
            c = pltpu.make_async_copy(raw.at[pl.ds(S * r, S)], out_hbm.at[0, pl.ds(S * r, S)], out_sem.at[r])
            c.start()
            out_copies.append(c)
        finish(sums)
        sums = stage(0) if stage else []
        finish(tap_sums)
        tap_sums = tap_stages[i]()
    stage4(0)
    finish(out_copies)


def body(inputs, cotangent, dw_kernel, pw_weight):
    _, rows, cols, C = inputs.shape
    n = lax.axis_size("lon")
    R, A, T, H = rows // S, cols // S, S * S, C // 2
    piece = H // n
    wire = BF16 if piece % 16 == 0 else F32
    samples = inputs.size // C * n * lax.axis_size("lat") * lax.axis_size("mem")
    anywhere = pl.BlockSpec(memory_space=pl.ANY)
    local = pl.BlockSpec(memory_space=pltpu.VMEM)
    padded = pltpu.VMEM((R + 2, A + 2, T, C), BF16)
    cells = pltpu.VMEM((R, A, T, C), BF16)
    scoped = [
        padded, padded, padded, padded,
        cells, cells, cells, cells, cells,
        pltpu.VMEM((R, A, T, 128), F32),
        pltpu.VMEM((1, A, T, 128), F32),
        pltpu.VMEM((A, T, C), F32),
        pltpu.VMEM((A, T, C), BF16),
        pltpu.VMEM((2, 9, T, C), BF16),
    ]
    scratch = [
        pltpu.VMEM((rows, cols, C), BF16),
        pltpu.VMEM((rows, cols, C), BF16),
        pltpu.VMEM((A * T, A * T), BF16),
        pltpu.VMEM((A * T, A * T), BF16),
        pltpu.VMEM((2, 9, 8, C), F32),
        pltpu.VMEM((2, C, C), F32),
        pltpu.VMEM((2, H, C), BF16), pltpu.VMEM((2, H, C), BF16),
        pltpu.VMEM((2, H, H), BF16), pltpu.VMEM((2, H, H), BF16),
        pltpu.VMEM((2, n, piece, H), wire), pltpu.VMEM((2, n, piece, H), wire),
        pltpu.VMEM((2, piece, H), wire), pltpu.VMEM((2, 2, n, piece, H), wire),
        pltpu.VMEM((2, 16, C), F32), pltpu.VMEM((2, 16, C), F32),
        pltpu.VMEM((2, 16, H), F32), pltpu.VMEM((2, 16, H), F32),
        pltpu.VMEM((2, 16, H), BF16), pltpu.VMEM((n, 2, 16, H), BF16),
        pltpu.SemaphoreType.DMA((2, R)), pltpu.SemaphoreType.DMA((R,)),
        pltpu.SemaphoreType.DMA((4, 5)), pltpu.SemaphoreType.DMA((4, 5)),
        pltpu.SemaphoreType.DMA((2, 4, 2 * n)), pltpu.SemaphoreType.DMA((2, 4, 2 * n)),
    ]
    return pl.pallas_call(
        functools.partial(kernel, n, 1.0 / math.sqrt(samples), scoped),
        out_shape=(
            jax.ShapeDtypeStruct(inputs.shape, BF16),
            jax.ShapeDtypeStruct((2, 9, H), F32),
            jax.ShapeDtypeStruct((2, C, H), F32),
        ),
        in_specs=[anywhere, anywhere, local, local],
        out_specs=(anywhere, local, local),
        scratch_shapes=scratch,
        name="blocks",
        compiler_params=pltpu.CompilerParams(
            collective_id=0, has_side_effects=True, vmem_limit_bytes=60 * 1024 * 1024
        ),
    )(inputs, cotangent, dw_kernel, pw_weight)


def solution(mesh):
    placed = (P("mem", "lat", "lon", None), P("mem", "lat", "lon", None), P(), P())
    return jax.shard_map(
        body,
        mesh=mesh,
        in_specs=placed,
        out_specs=(P("mem", "lat", "lon", None), P(None, None, "mem"), P(None, None, "mem")),
        check_vma=False,
    )
```

```python
import functools
import math

import jax
import jax.numpy as jnp
from jax import lax
from jax.experimental import pallas as pl
from jax.experimental.pallas import tpu as pltpu
from jax.sharding import PartitionSpec as P

S = 4
F32 = jnp.float32
BF16 = jnp.bfloat16
MESH = pl.DeviceIdType.MESH
ROOT = math.sqrt(2.0 / math.pi)
CUBE = 0.044715


def gelu_both(x):
    xx = x * x
    t = jnp.tanh(x * (ROOT + (ROOT * CUBE) * xx))
    h = 0.5 + 0.5 * t
    g = x * h
    return g, h + g * (1.0 - t) * (ROOT + (3.0 * ROOT * CUBE) * xx)


def kernel(n, factor, scoped, *refs):
    pl.run_scoped(lambda *inner: work(n, factor, *refs, *inner), *scoped)


def work(
    n, factor,
    x_hbm, cot_hbm, dw_ref, w_ref,
    out_hbm, kgrad, wgrad,
    raw, cotraw, perm, unperm, kacc, wacc,
    w0s, w0r, w1s, w1r, w2s, w2r, w3s, w3r, kv, kown, koth, kin, ks2, kr2,
    in_sem, out_sem, rim_s, rim_r, red_s, red_r,
    u0p, u1p, g1p, g0p, g1, hid0, d0, rc0, hid1, rc1, gp, pre, gn, row_buf, kb,
):
    R, A, T, C = hid0.shape
    M = A * T
    H = C // 2
    CH = gp.shape[1]
    NK = A // CH
    MC = R * CH * T
    WIDE = max(c for c in (1, 2, 4, 7) if A % c == 0)
    groups = [slice(g, g + 128) for g in range(0, C, 128)]
    me, lat, mem = lax.axis_index("lon"), lax.axis_index("lat"), lax.axis_index("mem")
    other, omem = 1 - lat, 1 - mem

    def lon_at(d):
        return lax.rem(me + (d % n), n)

    def dev(lon_i, lat_i, mem_i):
        return {"lon": lon_i, "lat": lat_i, "mem": mem_i}

    def planned(src, dst, ssem, rsem, where):
        return pltpu.make_async_remote_copy(
            src_ref=src, dst_ref=dst, send_sem=ssem, recv_sem=rsem, device_id=where, device_id_type=MESH
        )

    def in_copy(i, r):
        src, dst = ((x_hbm, raw), (cot_hbm, cotraw))[i]
        return pltpu.make_async_copy(src.at[0, pl.ds(S * r, S)], dst.at[pl.ds(S * r, S)], in_sem.at[i, r])

    for i in range(2):
        for r in range(R):
            in_copy(i, r).start()

    barrier = pltpu.get_barrier_semaphore()
    for d in range(n):
        for la in (lat, other):
            if d == 0 and la is lat:
                continue
            pl.semaphore_signal(barrier, inc=1, device_id=dev(lon_at(d), la, mem), device_id_type=MESH)
    for la in (lat, other):
        pl.semaphore_signal(barrier, inc=1, device_id=dev(me, la, omem), device_id_type=MESH)

    def one_hot(rows_dim):
        o = lax.broadcasted_iota(jnp.int32, (M, M), rows_dim)
        i = lax.broadcasted_iota(jnp.int32, (M, M), 1 - rows_dim)
        a, s, b = o >> 4, (o >> 2) & 3, o & 3
        return jnp.where(i == s * (A * S) + a * S + b, 1.0, 0.0).astype(BF16)

    perm[...] = one_hot(0)
    unperm[...] = one_hot(1)
    for l in range(2):
        taps_f = dw_ref[l].astype(F32)
        for t in range(9):
            kb[l, t] = jnp.broadcast_to(taps_f[t : t + 1, :], (T, C)).astype(BF16)
    kacc[...] = jnp.zeros_like(kacc)
    kv[...] = jnp.zeros_like(kv)
    edge = lat * (R + 1)
    for ref in (u0p, u1p, g1p, g0p):
        ref[edge] = jnp.zeros(ref.shape[1:], BF16)

    def rows_loop(lo, hi, fn):
        def step(r, c):
            fn(r)
            return c

        lax.fori_loop(lo, hi, step, 0)

    def regroup(src, r):
        rows = src[pl.ds(S * r, S)].reshape(M, C)
        return jnp.dot(perm[...], rows, preferred_element_type=F32).astype(BF16).reshape(A, T, C)

    wacc[...] = jnp.zeros_like(wacc)

    def load0(r):
        in_copy(0, r).wait()
        u0p[1 + r, 1 : A + 1] = regroup(raw, r)

    rows_loop(0, R, load0)

    pl.semaphore_wait(barrier, 2 * n + 1)

    right, left = lon_at(1), lon_at(-1)

    def rim(ref, e, i, src, dst, where):
        return planned(ref.at[src], ref.at[dst], rim_s.at[e, i], rim_r.at[e, i], where)

    seam = R - lat * (R - 1)
    inner = pl.ds(1, R)

    def rim_right(ref, e):
        last, first = pl.ds(A, 1), pl.ds(0, 1)
        return [
            rim(ref, e, 0, (inner, last), (inner, first), dev(right, lat, mem)),
            rim(ref, e, 2, (seam, last), (edge, first), dev(right, other, mem)),
        ]

    def rim_left(ref, e):
        first, last = pl.ds(1, 1), pl.ds(A + 1, 1)
        return [
            rim(ref, e, 1, (inner, first), (inner, last), dev(left, lat, mem)),
            rim(ref, e, 3, (seam, first), (edge, last), dev(left, other, mem)),
        ]

    def rim_lat(ref, e, k):
        at = pl.ds(1 + k * CH, CH)
        return [rim(ref, e, 4 + k, (seam, at), (edge, at), dev(me, other, mem))]

    def rim_lat_all(ref, e):
        at = pl.ds(1, A)
        return [rim(ref, e, 4, (seam, at), (edge, at), dev(me, other, mem))]

    def chunk_at(i):
        half, odd = i // 2, i % 2
        return odd * half + (1 - odd) * (NK - 1 - half)

    def next_piece(i):
        half, odd = i // 2, i % 2
        return odd * (half + 1) + (1 - odd) * (NK - 2 - half)

    def send_after(ref, e, i, k):
        start(rim_lat(ref, e, k))

        @pl.when(i == 0)
        def _():
            start(rim_right(ref, e))

        @pl.when(i == 1)
        def _():
            start(rim_left(ref, e))

    def wait_before(ref, e, i):
        @pl.when(i == 0)
        def _():
            finish(rim_lat(ref, e, NK - 1) + rim_lat(ref, e, NK - 2) + rim_left(ref, e))

        @pl.when(i == 1)
        def _():
            finish(rim_lat(ref, e, 0) + rim_lat(ref, e, 1) + rim_right(ref, e))

        @pl.when(jnp.logical_and(i > 1, i < NK - 2))
        def _():
            finish(rim_lat(ref, e, next_piece(i)))

    def wait_all(ref, e):
        for k in range(NK):
            finish(rim_lat(ref, e, k))
        finish(rim_left(ref, e) + rim_right(ref, e))

    def start(copies):
        for c in copies:
            c.start()

    def finish(copies):
        for c in copies:
            c.wait()

    def products(ref, r, a, ch, lanes, other_factor):
        for p in range(3):
            row = ref[r + p, pl.ds(a, ch + 2), :, lanes]
            yield [row[q : q + ch] * other_factor(p, q) for q in range(3)]

    def conv(ref, l, r, a, ch, lanes, rev):
        def tap(p, q):
            return kb[l, 3 * (2 - p) + 2 - q if rev else 3 * p + q, :, lanes]

        s0, s1, s2 = [v[0] + v[1] + v[2] for v in products(ref, r, a, ch, lanes, tap)]
        return s0 + s1 + s2

    def chunks(fn, ch, unroll=False):
        def step(i, c):
            fn(i * ch)
            return c

        lax.fori_loop(0, A // ch, step, 0, unroll=unroll)

    def each_row(fn):
        def step(r, c):
            fn(r)
            return c

        lax.fori_loop(0, R, step, 0, unroll=True)

    def tree(v):
        v = [v[i] for i in range(v.shape[0])]
        while len(v) > 1:
            v = [a + b for a, b in zip(v[::2], v[1::2])] + v[len(v) - len(v) % 2 :]
        return v[0]

    def add_taps(k, t, lanes, prod):
        both = tree(prod).astype(F32).reshape(2, 8, 128)
        kacc[k, t, :, lanes] += both[0] + both[1]

    def lane_mean(v, ch):
        m = jnp.sum(v.astype(F32), axis=-1, keepdims=True) * (1.0 / C)
        return jnp.broadcast_to(m, (ch, T, 128))

    def conv_norm(src, l, a, hid, rc, at):
        def go(r):
            convs = [conv(src, l, r, a, CH, lanes, False) for lanes in groups]
            c0, c1, c2, c3 = [c * c for c in convs]
            recip = lax.rsqrt(lane_mean((c0 + c1) + (c2 + c3), CH) + 1e-6)
            rc[r, at] = recip
            for lanes, c in zip(groups, convs):
                hid[r, at, :, lanes] = (c.astype(F32) * recip).astype(BF16)

        each_row(go)

    def mix(v, l):
        return jnp.dot(v.reshape(MC, C), w_ref[l], preferred_element_type=F32).reshape(R, CH, T, C)

    def mix_back(v, l):
        return lax.dot_general(
            v.reshape(MC, C), w_ref[l], (((1,), (1,)), ((), ())), preferred_element_type=F32
        ).astype(BF16).reshape(R, CH, T, C)

    def norm_back(dst, hid, rc, a, at):
        def go(r):
            ns = [hid[r, at, :, lanes] for lanes in groups]
            gs = [gn[r, :, :, lanes] for lanes in groups]
            d0_, d1_, d2_, d3_ = [g * v for g, v in zip(gs, ns)]
            mean = lane_mean((d0_ + d1_) + (d2_ + d3_), CH)
            recip = rc[r, at]
            for lanes, g, v in zip(groups, gs, ns):
                back = recip * (g.astype(F32) - v.astype(F32) * mean)
                dst[1 + r, pl.ds(1 + a, CH), :, lanes] = back.astype(BF16)

        each_row(go)

    def weight_sum(l, hid):
        wacc[l] += lax.dot_general(
            hid.reshape(MC, C), gp[...].reshape(MC, C), (((0,), (0,)), ((), ())), preferred_element_type=F32
        )

    own_rows = pl.ds(pl.multiple_of(lat * H, H), H)
    other_rows = pl.ds(pl.multiple_of(other * H, H), H)
    own_cols = pl.ds(pl.multiple_of(mem * H, H), H)
    other_cols = pl.ds(pl.multiple_of(omem * H, H), H)
    piece = H // n
    wire = w2s.dtype

    def red(l, stage, i, src, dst, where):
        return planned(src, dst, red_s.at[l, stage, i], red_r.at[l, stage, i], where)

    def plan(l, stage):
        if stage == 0:
            return [red(l, 0, 0, w0s.at[l], w0r.at[l], dev(me, other, mem))]
        if stage == 1:
            return [red(l, 1, 0, w1s.at[l], w1r.at[l], dev(me, lat, omem))]
        if stage == 2:
            return [
                red(l, 2, d, w2s.at[l, lon_at(d)], w2r.at[l, me], dev(lon_at(d), lat, mem)) for d in range(1, n)
            ]
        return [
            red(l, 3, k * n + d, w3s.at[l], w3r.at[l, lat, me], dev(lon_at(d), la, mem))
            for d in range(n) for k, la in enumerate((lat, other)) if d or k
        ]

    def stage(l, step):
        if step:
            finish(plan(l, step - 1))
        if step == 0:
            w0s[l] = wacc[l, other_rows, :].astype(BF16)
        elif step == 1:
            wacc[l, own_rows, :] += w0r[l].astype(F32)
            w1s[l] = wacc[l, own_rows, other_cols].astype(BF16)
        elif step == 2:
            total = wacc[l, own_rows, own_cols] + w1r[l].astype(F32)
            wacc[l, own_rows, own_cols] = total
            w2s[l] = total.reshape(n, piece, H).astype(wire)
        elif step == 3:
            at = pl.multiple_of(lat * H + me * piece, piece)
            total = wacc[l, pl.ds(at, piece), own_cols]
            for d in range(1, n):
                total = total + w2r[l, lon_at(d)].astype(F32)
            done = (total * factor).astype(wire)
            w3s[l] = done
            w3r[l, lat, me] = done
        else:
            wgrad[l] = w3r[l].reshape(C, H).astype(F32)
            return
        start(plan(l, step))

    def tap_plan(step):
        if step == 0:
            return [
                red(0, 0, 1, kown, kin.at[0], dev(me, other, mem)),
                red(0, 0, 2, koth, kin.at[1], dev(me, lat, omem)),
                red(0, 0, 3, koth, kin.at[2], dev(me, other, omem)),
            ]
        return [red(0, 2, n + d, ks2, kr2.at[me], dev(lon_at(d), lat, mem)) for d in range(1, n)]

    def tap_stage(step):
        if step:
            finish(tap_plan(step - 1))
        if step == 0:
            for k in range(2):
                for t in range(9):
                    kv[k, t : t + 1, :] = jnp.sum(kacc[k, t], axis=0, keepdims=True)
            kown[...] = kv[:, :, own_cols].astype(BF16)
            koth[...] = kv[:, :, other_cols].astype(BF16)
        elif step == 1:
            total = kv[:, :, own_cols]
            for j in range(3):
                total = total + kin[j].astype(F32)
            both = total.astype(BF16)
            ks2[...] = both
            kr2[me] = both
        else:
            ks = kr2[0].astype(F32)
            for j in range(1, n):
                ks = ks + kr2[j].astype(F32)
            for k in range(2):
                kgrad[k] = ks[k, :9, :] * factor
            return
        start(tap_plan(step))

    rims0 = rim_lat_all(u0p, 0) + rim_right(u0p, 0) + rim_left(u0p, 0)
    start(rims0)

    def load1(r):
        in_copy(1, r).wait()
        g1[r] = regroup(cotraw, r)

    rows_loop(0, R, load1)
    finish(rims0)
    here = pl.ds(0, CH)

    def block0(i):
        k = chunk_at(i)
        a = k * CH
        at = pl.ds(a, CH)
        conv_norm(u0p, 0, a, hid0, rc0, at)
        pre[...] = mix(hid0[:, at], 0)

        def go(r):
            for lanes in groups:
                gel, slope = gelu_both(pre[r, :, :, lanes])
                d0[r, at, :, lanes] = slope.astype(BF16)
                u = u0p[1 + r, pl.ds(1 + a, CH), :, lanes]
                u1p[1 + r, pl.ds(1 + a, CH), :, lanes] = u + gel.astype(BF16)

        each_row(go)
        send_after(u1p, 1, i, k)

    rows_loop(0, NK, block0)

    def block1(i):
        wait_before(u1p, 1, i)
        k = chunk_at(i)
        a = k * CH
        at = pl.ds(a, CH)
        conv_norm(u1p, 1, a, hid1, rc1, here)
        pre[...] = mix(hid1[...], 1)

        def go(r):
            for lanes in groups:
                slope = gelu_both(pre[r, :, :, lanes])[1]
                g = g1[r, at, :, lanes].astype(F32)
                gp[r, :, :, lanes] = (g * slope).astype(BF16)

        each_row(go)
        gn[...] = mix_back(gp[...], 1)
        weight_sum(1, hid1[...])
        norm_back(g1p, hid1, rc1, a, here)
        send_after(g1p, 2, i, k)

    rows_loop(0, NK, block1)
    stage(1, 0)

    def back0(i):
        wait_before(g1p, 2, i)
        k = chunk_at(i)
        a = k * CH
        at = pl.ds(a, CH)

        def go(r):
            for lanes in groups:
                s = conv(g1p, 1, r, a, CH, lanes, True) + g1[r, at, :, lanes]
                g1[r, at, :, lanes] = s
                gp[r, :, :, lanes] = s * d0[r, at, :, lanes]

        each_row(go)
        gn[...] = mix_back(gp[...], 0)
        weight_sum(0, hid0[:, at])
        norm_back(g0p, hid0, rc0, a, at)
        send_after(g0p, 3, i, k)
        for step in range(1, 4):
            @pl.when(i == (NK * step) // 3 - 1)
            def _(step=step):
                stage(1, step)

    rows_loop(0, NK, back0)
    stage(0, 0)

    def tap_sums(k, moved, still, rev):
        def row(r):
            def go(a):
                for lanes in groups:
                    v = still[1 + r, pl.ds(1 + a, WIDE), :, lanes]
                    for p, prods in enumerate(products(moved, r, a, WIDE, lanes, lambda p, q: v)):
                        for q, prod in enumerate(prods):
                            add_taps(k, 3 * (2 - p) + 2 - q if rev else 3 * p + q, lanes, prod)

            chunks(go, WIDE)

        rows_loop(0, R, row)

    tap_sums(1, g1p, u1p, True)
    stage(0, 1)
    tap_sums(0, u0p, g0p, False)
    tap_stage(0)
    stage(0, 2)
    stage(1, 4)
    wait_all(g0p, 3)

    def out_copy(r):
        return pltpu.make_async_copy(raw.at[pl.ds(S * r, S)], out_hbm.at[0, pl.ds(S * r, S)], out_sem.at[r])

    def last(r):
        def go(a):
            for lanes in groups:
                s = conv(g0p, 0, r, a, WIDE, lanes, True) + g1[r, pl.ds(a, WIDE), :, lanes]
                row_buf[pl.ds(a, WIDE), :, lanes] = s

        chunks(go, WIDE)
        rows = jnp.dot(unperm[...], row_buf[...].reshape(M, C), preferred_element_type=F32).astype(BF16)
        raw[pl.ds(S * r, S)] = rows.reshape(S, S * A, C)
        out_copy(r).start()

    rows_loop(0, R // 2, last)
    tap_stage(1)
    stage(0, 3)
    rows_loop(R // 2, R, last)
    tap_stage(2)
    stage(0, 4)
    finish([out_copy(r) for r in range(R)])


def body(inputs, cotangent, dw_kernel, pw_weight):
    _, rows, cols, C = inputs.shape
    n = lax.axis_size("lon")
    R, A, T, H = rows // S, cols // S, S * S, C // 2
    piece = H // n
    wire = BF16 if piece % 16 == 0 else F32
    samples = inputs.size // C * n * lax.axis_size("lat") * lax.axis_size("mem")
    anywhere = pl.BlockSpec(memory_space=pl.ANY)
    local = pl.BlockSpec(memory_space=pltpu.VMEM)
    padded = pltpu.VMEM((R + 2, A + 2, T, C), BF16)
    cells = pltpu.VMEM((R, A, T, C), BF16)
    CH = max(c for c in (1, 2, 4) if A % c == 0)
    chunk = pltpu.VMEM((R, CH, T, C), BF16)
    scoped = [
        padded, padded, padded, padded,
        cells, cells, cells,
        pltpu.VMEM((R, A, T, 128), F32),
        chunk,
        pltpu.VMEM((R, CH, T, 128), F32),
        chunk,
        pltpu.VMEM((R, CH, T, C), F32),
        chunk,
        pltpu.VMEM((A, T, C), BF16),
        pltpu.VMEM((2, 9, T, C), BF16),
    ]
    scratch = [
        pltpu.VMEM((rows, cols, C), BF16),
        pltpu.VMEM((rows, cols, C), BF16),
        pltpu.VMEM((A * T, A * T), BF16),
        pltpu.VMEM((A * T, A * T), BF16),
        pltpu.VMEM((2, 9, 8, C), F32),
        pltpu.VMEM((2, C, C), F32),
        pltpu.VMEM((2, H, C), BF16), pltpu.VMEM((2, H, C), BF16),
        pltpu.VMEM((2, H, H), BF16), pltpu.VMEM((2, H, H), BF16),
        pltpu.VMEM((2, n, piece, H), wire), pltpu.VMEM((2, n, piece, H), wire),
        pltpu.VMEM((2, piece, H), wire), pltpu.VMEM((2, 2, n, piece, H), wire),
        pltpu.VMEM((2, 16, C), F32),
        pltpu.VMEM((2, 16, H), BF16), pltpu.VMEM((2, 16, H), BF16), pltpu.VMEM((3, 2, 16, H), BF16),
        pltpu.VMEM((2, 16, H), BF16), pltpu.VMEM((n, 2, 16, H), BF16),
        pltpu.SemaphoreType.DMA((2, R)), pltpu.SemaphoreType.DMA((R,)),
        pltpu.SemaphoreType.DMA((4, 4 + A // CH)), pltpu.SemaphoreType.DMA((4, 4 + A // CH)),
        pltpu.SemaphoreType.DMA((2, 4, 2 * n)), pltpu.SemaphoreType.DMA((2, 4, 2 * n)),
    ]
    return pl.pallas_call(
        functools.partial(kernel, n, 1.0 / math.sqrt(samples), scoped),
        out_shape=(
            jax.ShapeDtypeStruct(inputs.shape, BF16),
            jax.ShapeDtypeStruct((2, 9, H), F32),
            jax.ShapeDtypeStruct((2, C, H), F32),
        ),
        in_specs=[anywhere, anywhere, local, local],
        out_specs=(anywhere, local, local),
        scratch_shapes=scratch,
        name="blocks",
        compiler_params=pltpu.CompilerParams(
            collective_id=0, has_side_effects=True, vmem_limit_bytes=60 * 1024 * 1024
        ),
    )(inputs, cotangent, dw_kernel, pw_weight)


def solution(mesh):
    placed = (P("mem", "lat", "lon", None), P("mem", "lat", "lon", None), P(), P())
    return jax.shard_map(
        body,
        mesh=mesh,
        in_specs=placed,
        out_specs=(P("mem", "lat", "lon", None), P(None, None, "mem"), P(None, None, "mem")),
        check_vma=False,
    )
```

```python
import functools
import math

import jax
import jax.numpy as jnp
from jax import lax
from jax.experimental import pallas as pl
from jax.experimental.pallas import tpu as pltpu
from jax.sharding import PartitionSpec as P

S = 4
F32 = jnp.float32
BF16 = jnp.bfloat16
MESH = pl.DeviceIdType.MESH
ROOT = math.sqrt(2.0 / math.pi)
CUBE = 0.044715


def gelu_both(x):
    xx = x * x
    t = jnp.tanh(x * (ROOT + (ROOT * CUBE) * xx))
    h = 0.5 + 0.5 * t
    g = x * h
    return g, h + g * (1.0 - t) * (ROOT + (3.0 * ROOT * CUBE) * xx)


def kernel(n, factor, scoped, *refs):
    pl.run_scoped(lambda *inner: work(n, factor, *refs, *inner), *scoped)


def work(
    n, factor,
    x_hbm, cot_hbm, dw_ref, w_ref,
    out_hbm, kgrad, wgrad,
    raw, cotraw, perm, unperm, kacc, wacc,
    w0s, w0r, w1s, w1r, w2s, w2r, w3s, w3r, kv, kown, koth, kin, ks2, kr2,
    in_sem, out_sem, rim_s, rim_r, red_s, red_r,
    u0p, u1p, g1p, g0p, g1, hid0, d0, rc0, hid1, rc1, gp, pre, gn, row_buf, kb,
):
    R, A, T, C = hid0.shape
    M = A * T
    H = C // 2
    CH = gn.shape[1]
    NK = A // CH
    MC = R * CH * T
    WIDE = max(c for c in (1, 2, 4, 7) if A % c == 0)
    groups = [slice(g, g + 128) for g in range(0, C, 128)]
    me, lat, mem = lax.axis_index("lon"), lax.axis_index("lat"), lax.axis_index("mem")
    other, omem = 1 - lat, 1 - mem

    def lon_at(d):
        return lax.rem(me + (d % n), n)

    def dev(lon_i, lat_i, mem_i):
        return {"lon": lon_i, "lat": lat_i, "mem": mem_i}

    def planned(src, dst, ssem, rsem, where):
        return pltpu.make_async_remote_copy(
            src_ref=src, dst_ref=dst, send_sem=ssem, recv_sem=rsem, device_id=where, device_id_type=MESH
        )

    def in_copy(i, r):
        src, dst = ((x_hbm, raw), (cot_hbm, cotraw))[i]
        return pltpu.make_async_copy(src.at[0, pl.ds(S * r, S)], dst.at[pl.ds(S * r, S)], in_sem.at[i, r])

    for i in range(2):
        for r in range(R):
            in_copy(i, r).start()

    barrier = pltpu.get_barrier_semaphore()
    for d in range(n):
        for la in (lat, other):
            if d == 0 and la is lat:
                continue
            pl.semaphore_signal(barrier, inc=1, device_id=dev(lon_at(d), la, mem), device_id_type=MESH)
    for la in (lat, other):
        pl.semaphore_signal(barrier, inc=1, device_id=dev(me, la, omem), device_id_type=MESH)

    def one_hot(rows_dim):
        o = lax.broadcasted_iota(jnp.int32, (M, M), rows_dim)
        i = lax.broadcasted_iota(jnp.int32, (M, M), 1 - rows_dim)
        a, s, b = o >> 4, (o >> 2) & 3, o & 3
        return jnp.where(i == s * (A * S) + a * S + b, 1.0, 0.0).astype(BF16)

    perm[...] = one_hot(0)
    unperm[...] = one_hot(1)
    for t in range(9):
        taps_f = dw_ref[t].astype(F32)
        for l in range(2):
            kb[l, t] = jnp.broadcast_to(taps_f[l : l + 1, :], (T, C)).astype(BF16)
    kacc[...] = jnp.zeros_like(kacc)
    kv[...] = jnp.zeros_like(kv)
    edge = lat * (R + 1)
    for ref in (u0p, u1p, g1p, g0p):
        ref[edge] = jnp.zeros(ref.shape[1:], BF16)

    def rows_loop(lo, hi, fn):
        def step(r, c):
            fn(r)
            return c

        lax.fori_loop(lo, hi, step, 0)

    def regroup(src, r):
        rows = src[pl.ds(S * r, S)].reshape(M, C)
        return jnp.dot(perm[...], rows, preferred_element_type=F32).astype(BF16).reshape(A, T, C)

    wacc[...] = jnp.zeros_like(wacc)

    def load0(r):
        in_copy(0, r).wait()
        u0p[1 + r, 1 : A + 1] = regroup(raw, r)

    rows_loop(0, R, load0)

    pl.semaphore_wait(barrier, 2 * n + 1)

    right, left = lon_at(1), lon_at(-1)

    def rim(ref, e, i, src, dst, where):
        return planned(ref.at[src], ref.at[dst], rim_s.at[e, i], rim_r.at[e, i], where)

    seam = R - lat * (R - 1)
    inner = pl.ds(1, R)

    def rim_right(ref, e):
        last, first = pl.ds(A, 1), pl.ds(0, 1)
        return [
            rim(ref, e, 0, (inner, last), (inner, first), dev(right, lat, mem)),
            rim(ref, e, 2, (seam, last), (edge, first), dev(right, other, mem)),
        ]

    def rim_left(ref, e):
        first, last = pl.ds(1, 1), pl.ds(A + 1, 1)
        return [
            rim(ref, e, 1, (inner, first), (inner, last), dev(left, lat, mem)),
            rim(ref, e, 3, (seam, first), (edge, last), dev(left, other, mem)),
        ]

    def rim_lat(ref, e, k):
        at = pl.ds(1 + k * CH, CH)
        return [rim(ref, e, 4 + k, (seam, at), (edge, at), dev(me, other, mem))]

    def rim_lat_all(ref, e):
        at = pl.ds(1, A)
        return [rim(ref, e, 4, (seam, at), (edge, at), dev(me, other, mem))]

    def interior_first(m):
        return [*range(1, 1 + m), NK - 1, 0, *range(1 + m, NK - 1)]

    def pick(order, i):
        return sum(k * ((i + NK - j) // NK - (i + NK - j - 1) // NK) for j, k in enumerate(order))

    def send_after(ref, e, i, k, order):
        start(rim_lat(ref, e, k))

        @pl.when(i == order.index(NK - 1))
        def _():
            start(rim_right(ref, e))

        @pl.when(i == order.index(0))
        def _():
            start(rim_left(ref, e))

    def wait_before(ref, e, i, order):
        done = set()
        for j, k in enumerate(order):
            need = [p for p in (k - 1, k, k + 1) if 0 <= p < NK and p not in done]
            done.update(need)
            if e == 0:
                need = [0] if j == 0 else []
            if not need and 0 < k < NK - 1:
                continue

            @pl.when(i == j)
            def _(k=k, need=need):
                for p in need:
                    finish(rim_lat(ref, e, p) if e else rim_lat_all(ref, e))
                if k == NK - 1:
                    finish(rim_left(ref, e))
                if k == 0:
                    finish(rim_right(ref, e))

    def wait_all(ref, e):
        for k in range(NK):
            finish(rim_lat(ref, e, k))
        finish(rim_left(ref, e) + rim_right(ref, e))

    def start(copies):
        for c in copies:
            c.start()

    def finish(copies):
        for c in copies:
            c.wait()

    def products(ref, r, a, ch, lanes, other_factor):
        for p in range(3):
            row = ref[r + p, pl.ds(a, ch + 2), :, lanes]
            yield [row[q : q + ch] * other_factor(p, q) for q in range(3)]

    def conv(ref, l, r, a, ch, lanes, rev):
        def tap(p, q):
            return kb[l, 3 * (2 - p) + 2 - q if rev else 3 * p + q, :, lanes]

        s0, s1, s2 = [v[0] + v[1] + v[2] for v in products(ref, r, a, ch, lanes, tap)]
        return s0 + s1 + s2

    def chunks(fn, ch, unroll=False):
        def step(i, c):
            fn(i * ch)
            return c

        lax.fori_loop(0, A // ch, step, 0, unroll=unroll)

    def each_row(fn):
        def step(r, c):
            fn(r)
            return c

        lax.fori_loop(0, R, step, 0, unroll=True)

    def tree(v):
        v = [v[i] for i in range(v.shape[0])]
        while len(v) > 1:
            v = [a + b for a, b in zip(v[::2], v[1::2])] + v[len(v) - len(v) % 2 :]
        return v[0]

    def add_taps(k, t, lanes, prod):
        both = tree(prod).astype(F32).reshape(2, 8, 128)
        kacc[k, t, :, lanes] += both[0] + both[1]

    def lane_mean(v, ch):
        m = jnp.sum(v.astype(F32), axis=-1, keepdims=True) * (1.0 / C)
        return jnp.broadcast_to(m, (ch, T, 128))

    def conv_norm(src, l, a, hid, rc, at):
        def go(r):
            convs = [conv(src, l, r, a, CH, lanes, False) for lanes in groups]
            c0, c1, c2, c3 = [c * c for c in convs]
            recip = lax.rsqrt(lane_mean((c0 + c1) + (c2 + c3), CH) + 1e-6)
            rc[r, at] = recip
            for lanes, c in zip(groups, convs):
                hid[r, at, :, lanes] = (c.astype(F32) * recip).astype(BF16)

        each_row(go)

    def mix(v, l):
        return jnp.dot(v.reshape(MC, C), w_ref[l], preferred_element_type=F32).reshape(R, CH, T, C)

    def mix_back(v, l):
        return lax.dot_general(
            v.reshape(MC, C), w_ref[l], (((1,), (1,)), ((), ())), preferred_element_type=F32
        ).astype(BF16).reshape(R, CH, T, C)

    def norm_back(dst, hid, rc, a, at):
        def go(r):
            ns = [hid[r, at, :, lanes] for lanes in groups]
            gs = [gn[r, :, :, lanes] for lanes in groups]
            d0_, d1_, d2_, d3_ = [g * v for g, v in zip(gs, ns)]
            mean = lane_mean((d0_ + d1_) + (d2_ + d3_), CH)
            recip = rc[r, at]
            for lanes, g, v in zip(groups, gs, ns):
                back = recip * (g.astype(F32) - v.astype(F32) * mean)
                dst[1 + r, pl.ds(1 + a, CH), :, lanes] = back.astype(BF16)

        each_row(go)

    def weight_sum(l, hid, at):
        wacc[l] += lax.dot_general(
            hid[:, at].reshape(MC, C), gp[:, at].reshape(MC, C), (((0,), (0,)), ((), ())), preferred_element_type=F32
        )

    own_rows = pl.ds(pl.multiple_of(lat * H, H), H)
    other_rows = pl.ds(pl.multiple_of(other * H, H), H)
    own_cols = pl.ds(pl.multiple_of(mem * H, H), H)
    other_cols = pl.ds(pl.multiple_of(omem * H, H), H)
    piece = H // n
    wire = w2s.dtype

    def red(l, stage, i, src, dst, where):
        return planned(src, dst, red_s.at[l, stage, i], red_r.at[l, stage, i], where)

    def plan(l, stage):
        if stage == 0:
            return [red(l, 0, 0, w0s.at[l], w0r.at[l], dev(me, other, mem))]
        if stage == 1:
            return [red(l, 1, 0, w1s.at[l], w1r.at[l], dev(me, lat, omem))]
        if stage == 2:
            return [
                red(l, 2, d, w2s.at[l, lon_at(d)], w2r.at[l, me], dev(lon_at(d), lat, mem)) for d in range(1, n)
            ]
        if stage == 3:
            return [red(l, 3, d, w3s.at[l], w3r.at[l, lat, me], dev(lon_at(d), lat, mem)) for d in range(1, n)]
        return [red(l, 4, 0, w3r.at[l, lat], w3r.at[l, lat], dev(me, other, mem))]

    def stage(l, step):
        if step:
            finish(plan(l, step - 1))
        if step == 0:
            w0s[l] = wacc[l, other_rows, :].astype(BF16)
        elif step == 1:
            wacc[l, own_rows, :] += w0r[l].astype(F32)
            w1s[l] = wacc[l, own_rows, other_cols].astype(BF16)
        elif step == 2:
            total = wacc[l, own_rows, own_cols] + w1r[l].astype(F32)
            wacc[l, own_rows, own_cols] = total
            w2s[l] = total.reshape(n, piece, H).astype(wire)
        elif step == 3:
            at = pl.multiple_of(lat * H + me * piece, piece)
            total = wacc[l, pl.ds(at, piece), own_cols]
            for d in range(1, n):
                total = total + w2r[l, lon_at(d)].astype(F32)
            done = (total * factor).astype(wire)
            w3s[l] = done
            w3r[l, lat, me] = done
        elif step == 5:
            wgrad[l] = w3r[l].reshape(C, H).astype(F32)
            return
        start(plan(l, step))

    def tap_plan(step):
        if step == 0:
            return [
                red(0, 0, 1, kown, kin.at[0], dev(me, other, mem)),
                red(0, 0, 2, koth, kin.at[1], dev(me, lat, omem)),
                red(0, 0, 3, koth, kin.at[2], dev(me, other, omem)),
            ]
        return [red(0, 2, n + d, ks2, kr2.at[me], dev(lon_at(d), lat, mem)) for d in range(1, n)]

    def tap_stage(step):
        if step:
            finish(tap_plan(step - 1))
        if step == 0:
            for k in range(2):
                for t in range(9):
                    kv[k, t : t + 1, :] = jnp.sum(kacc[k, t], axis=0, keepdims=True)
            kown[...] = kv[:, :, own_cols].astype(BF16)
            koth[...] = kv[:, :, other_cols].astype(BF16)
        elif step == 1:
            total = kv[:, :, own_cols]
            for j in range(3):
                total = total + kin[j].astype(F32)
            both = total.astype(BF16)
            ks2[...] = both
            kr2[me] = both
        else:
            ks = kr2[0].astype(F32)
            for j in range(1, n):
                ks = ks + kr2[j].astype(F32)
            for k in range(2):
                kgrad[:, k, :] = ks[k, :9, :] * factor
            return
        start(tap_plan(step))

    rims0 = rim_lat_all(u0p, 0) + rim_right(u0p, 0) + rim_left(u0p, 0)
    start(rims0)

    def load1(r):
        in_copy(1, r).wait()
        g1[r] = regroup(cotraw, r)

    rows_loop(0, R, load1)
    mixed, inward, outward = [interior_first(m) for m in (min(3, NK - 2), NK - 2, 0)]

    def block0(i):
        wait_before(u0p, 0, i, mixed)
        k = pick(mixed, i)
        a = k * CH
        at = pl.ds(a, CH)
        conv_norm(u0p, 0, a, hid0, rc0, at)
        pre[...] = mix(hid0[:, at], 0)

        def go(r):
            for lanes in groups:
                gel, slope = gelu_both(pre[r, :, :, lanes])
                d0[r, at, :, lanes] = slope.astype(BF16)
                u = u0p[1 + r, pl.ds(1 + a, CH), :, lanes]
                u1p[1 + r, pl.ds(1 + a, CH), :, lanes] = u + gel.astype(BF16)

        each_row(go)
        send_after(u1p, 1, i, k, mixed)

    rows_loop(0, NK, block0)

    def block1(i):
        wait_before(u1p, 1, i, inward)
        k = pick(inward, i)
        a = k * CH
        at = pl.ds(a, CH)
        conv_norm(u1p, 1, a, hid1, rc1, at)
        pre[...] = mix(hid1[:, at], 1)

        def go(r):
            for lanes in groups:
                slope = gelu_both(pre[r, :, :, lanes])[1]
                g = g1[r, at, :, lanes].astype(F32)
                gp[r, at, :, lanes] = (g * slope).astype(BF16)

        each_row(go)
        weight_sum(1, hid1, at)

    rows_loop(0, NK, block1)
    stage(1, 0)

    def back1(i):
        k = pick(outward, i)
        a = k * CH
        at = pl.ds(a, CH)
        gn[...] = mix_back(gp[:, at], 1)
        norm_back(g1p, hid1, rc1, a, at)
        send_after(g1p, 2, i, k, outward)

        @pl.when(i == 3)
        def _():
            stage(1, 1)

    rows_loop(0, NK, back1)

    def back0(i):
        wait_before(g1p, 2, i, inward)
        k = pick(inward, i)
        a = k * CH
        at = pl.ds(a, CH)

        def go(r):
            for lanes in groups:
                s = conv(g1p, 1, r, a, CH, lanes, True) + g1[r, at, :, lanes]
                g1[r, at, :, lanes] = s
                gp[r, at, :, lanes] = s * d0[r, at, :, lanes]

        each_row(go)
        weight_sum(0, hid0, at)

    rows_loop(0, NK, back0)
    stage(0, 0)
    stage(1, 2)

    def norm0(i):
        k = pick(outward, i)
        a = k * CH
        at = pl.ds(a, CH)
        gn[...] = mix_back(gp[:, at], 0)
        norm_back(g0p, hid0, rc0, a, at)
        send_after(g0p, 3, i, k, outward)

        @pl.when(i == 3)
        def _():
            stage(0, 1)

    rows_loop(0, NK, norm0)

    def tap_sums(k, moved, still, rev, lo, hi):
        def row(r):
            def go(a):
                for lanes in groups:
                    v = still[1 + r, pl.ds(1 + a, WIDE), :, lanes]
                    for p, prods in enumerate(products(moved, r, a, WIDE, lanes, lambda p, q: v)):
                        for q, prod in enumerate(prods):
                            add_taps(k, 3 * (2 - p) + 2 - q if rev else 3 * p + q, lanes, prod)

            chunks(go, WIDE)

        rows_loop(lo, hi, row)

    tap_sums(1, g1p, u1p, True, 0, R)
    stage(1, 3)
    tap_sums(0, u0p, g0p, False, 0, R // 2)
    stage(0, 2)
    tap_sums(0, u0p, g0p, False, R // 2, R)
    tap_stage(0)
    wait_all(g0p, 3)

    def out_copy(r):
        return pltpu.make_async_copy(raw.at[pl.ds(S * r, S)], out_hbm.at[0, pl.ds(S * r, S)], out_sem.at[r])

    def last(r):
        def go(a):
            for lanes in groups:
                s = conv(g0p, 0, r, a, WIDE, lanes, True) + g1[r, pl.ds(a, WIDE), :, lanes]
                row_buf[pl.ds(a, WIDE), :, lanes] = s

        chunks(go, WIDE)
        rows = jnp.dot(unperm[...], row_buf[...].reshape(M, C), preferred_element_type=F32).astype(BF16)
        raw[pl.ds(S * r, S)] = rows.reshape(S, S * A, C)
        out_copy(r).start()

    rows_loop(0, R, last)
    stage(1, 4)
    tap_stage(1)
    stage(0, 3)
    stage(1, 5)
    tap_stage(2)
    stage(0, 4)
    stage(0, 5)
    finish([out_copy(r) for r in range(R)])


def hand_over(pieces, *refs):
    srcs, dsts, sem = refs[:3], refs[3:6], refs[6]
    step = srcs[0].shape[1] // pieces
    copies = [
        pltpu.make_async_copy(srcs[0].at[:, pl.ds(i * step, step)], dsts[0].at[:, pl.ds(i * step, step)], sem.at[i])
        for i in range(pieces)
    ]
    copies += [pltpu.make_async_copy(srcs[j], dsts[j], sem.at[pieces + j]) for j in (1, 2)]
    for c in copies:
        c.start()
    for c in copies:
        c.wait()


def body(inputs, cotangent, dw_kernel, pw_weight):
    _, rows, cols, C = inputs.shape
    n = lax.axis_size("lon")
    R, A, T, H = rows // S, cols // S, S * S, C // 2
    piece = H // n
    wire = BF16 if piece % 16 == 0 else F32
    samples = inputs.size // C * n * lax.axis_size("lat") * lax.axis_size("mem")
    anywhere = pl.BlockSpec(memory_space=pl.ANY)
    local = pl.BlockSpec(memory_space=pltpu.VMEM)
    padded = pltpu.VMEM((R + 2, A + 2, T, C), BF16)
    cells = pltpu.VMEM((R, A, T, C), BF16)
    CH = max(c for c in (1, 2, 4) if A % c == 0)
    chunk = pltpu.VMEM((R, CH, T, C), BF16)
    scoped = [
        padded, padded, padded, padded,
        cells, cells, cells,
        pltpu.VMEM((R, A, T, 128), F32),
        cells,
        pltpu.VMEM((R, A, T, 128), F32),
        cells,
        pltpu.VMEM((R, CH, T, C), F32),
        chunk,
        pltpu.VMEM((A, T, C), BF16),
        pltpu.VMEM((2, 9, T, C), BF16),
    ]
    scratch = [
        pltpu.VMEM((rows, cols, C), BF16),
        pltpu.VMEM((rows, cols, C), BF16),
        pltpu.VMEM((A * T, A * T), BF16),
        pltpu.VMEM((A * T, A * T), BF16),
        pltpu.VMEM((2, 9, 8, C), F32),
        pltpu.VMEM((2, C, C), F32),
        pltpu.VMEM((2, H, C), BF16), pltpu.VMEM((2, H, C), BF16),
        pltpu.VMEM((2, H, H), BF16), pltpu.VMEM((2, H, H), BF16),
        pltpu.VMEM((2, n, piece, H), wire), pltpu.VMEM((2, n, piece, H), wire),
        pltpu.VMEM((2, piece, H), wire), pltpu.VMEM((2, 2, n, piece, H), wire),
        pltpu.VMEM((2, 16, C), F32),
        pltpu.VMEM((2, 16, H), BF16), pltpu.VMEM((2, 16, H), BF16), pltpu.VMEM((3, 2, 16, H), BF16),
        pltpu.VMEM((2, 16, H), BF16), pltpu.VMEM((n, 2, 16, H), BF16),
        pltpu.SemaphoreType.DMA((2, R)), pltpu.SemaphoreType.DMA((R,)),
        pltpu.SemaphoreType.DMA((4, 4 + A // CH)), pltpu.SemaphoreType.DMA((4, 4 + A // CH)),
        pltpu.SemaphoreType.DMA((2, 5, 2 * n)), pltpu.SemaphoreType.DMA((2, 5, 2 * n)),
    ]
    made = pl.pallas_call(
        functools.partial(kernel, n, 1.0 / math.sqrt(samples), scoped),
        out_shape=(
            jax.ShapeDtypeStruct(inputs.shape, BF16),
            jax.ShapeDtypeStruct((9, 2, H), F32),
            jax.ShapeDtypeStruct((2, C, H), F32),
        ),
        in_specs=[anywhere, anywhere, local, local],
        out_specs=(anywhere, local, local),
        scratch_shapes=scratch,
        name="blocks",
        compiler_params=pltpu.CompilerParams(
            collective_id=0, has_side_effects=True, vmem_limit_bytes=60 * 1024 * 1024
        ),
    )(inputs, cotangent, jnp.transpose(dw_kernel, (1, 0, 2)), pw_weight)
    pieces = max(p for p in (1, 2, 3, 4, 6, 8) if rows % p == 0)
    out, kgrad, wgrad = pl.pallas_call(
        functools.partial(hand_over, pieces),
        out_shape=tuple(jax.ShapeDtypeStruct(v.shape, v.dtype) for v in made),
        in_specs=[anywhere] * 3,
        out_specs=(anywhere,) * 3,
        scratch_shapes=[pltpu.SemaphoreType.DMA((pieces + 3,))],
        name="hand_over",
    )(*made)
    return out, jnp.transpose(kgrad, (1, 0, 2)), wgrad


def solution(mesh):
    placed = (P("mem", "lat", "lon", None), P("mem", "lat", "lon", None), P(), P())
    return jax.shard_map(
        body,
        mesh=mesh,
        in_specs=placed,
        out_specs=(P("mem", "lat", "lon", None), P(None, None, "mem"), P(None, None, "mem")),
        check_vma=False,
    )
```

```python
import functools
import math

import jax
import jax.numpy as jnp
from jax import lax
from jax.experimental import pallas as pl
from jax.experimental.pallas import tpu as pltpu
from jax.sharding import PartitionSpec as P

S = 4
F32 = jnp.float32
BF16 = jnp.bfloat16
MESH = pl.DeviceIdType.MESH
ROOT = math.sqrt(2.0 / math.pi)
CUBE = 0.044715


def gelu_both(x):
    xx = x * x
    t = jnp.tanh(x * (ROOT + (ROOT * CUBE) * xx))
    h = 0.5 + 0.5 * t
    g = x * h
    return g, h + g * (1.0 - t) * (ROOT + (3.0 * ROOT * CUBE) * xx)


def kernel(n, factor, scoped, *refs):
    pl.run_scoped(lambda *inner: work(n, factor, *refs, *inner), *scoped)


def work(
    n, factor,
    x_hbm, cot_hbm, dw_ref, w_ref,
    out_hbm, kgrad, wgrad,
    raw, cotraw, perm, unperm, kacc, wacc,
    w0s, w0r, w1s, w1r, w2s, w2r, w3s, w3r, kv, kown, koth, kin, ks2, kr2,
    in_sem, out_sem, rim_s, rim_r, red_s, red_r,
    u0p, u1p, g1p, g0p, g1, hid0, d0, rc0, hid1_0, hid1_1, rc1_0, rc1_1, gp_0, gp_1, pre, gn, row_buf, kb,
):
    R, A, T, C = hid0.shape
    M = A * T
    H = C // 2
    CH = gn.shape[1]
    NK = A // CH
    MC = R * CH * T
    WIDE = max(c for c in (1, 2, 4, 7) if A % c == 0)
    groups = [slice(g, g + 128) for g in range(0, C, 128)]
    me, lat, mem = lax.axis_index("lon"), lax.axis_index("lat"), lax.axis_index("mem")
    other, omem = 1 - lat, 1 - mem

    def lon_at(d):
        return lax.rem(me + (d % n), n)

    def dev(lon_i, lat_i, mem_i):
        return {"lon": lon_i, "lat": lat_i, "mem": mem_i}

    def planned(src, dst, ssem, rsem, where):
        return pltpu.make_async_remote_copy(
            src_ref=src, dst_ref=dst, send_sem=ssem, recv_sem=rsem, device_id=where, device_id_type=MESH
        )

    def in_copy(i, r):
        src, dst = ((x_hbm, raw), (cot_hbm, cotraw))[i]
        return pltpu.make_async_copy(src.at[0, pl.ds(S * r, S)], dst.at[pl.ds(S * r, S)], in_sem.at[i, r])

    for i in range(2):
        for r in range(R):
            in_copy(i, r).start()

    barrier = pltpu.get_barrier_semaphore()
    for d in range(n):
        for la in (lat, other):
            if d == 0 and la is lat:
                continue
            pl.semaphore_signal(barrier, inc=1, device_id=dev(lon_at(d), la, mem), device_id_type=MESH)
    for la in (lat, other):
        pl.semaphore_signal(barrier, inc=1, device_id=dev(me, la, omem), device_id_type=MESH)

    def one_hot(rows_dim):
        o = lax.broadcasted_iota(jnp.int32, (M, M), rows_dim)
        i = lax.broadcasted_iota(jnp.int32, (M, M), 1 - rows_dim)
        a, s, b = o >> 4, (o >> 2) & 3, o & 3
        return jnp.where(i == s * (A * S) + a * S + b, 1.0, 0.0).astype(BF16)

    perm[...] = one_hot(0)
    unperm[...] = one_hot(1)
    for t in range(9):
        taps_f = dw_ref[t].astype(F32)
        for l in range(2):
            kb[l, t] = jnp.broadcast_to(taps_f[l : l + 1, :], (T, C)).astype(BF16)
    kacc[...] = jnp.zeros_like(kacc)
    kv[...] = jnp.zeros_like(kv)
    edge = lat * (R + 1)
    for ref in (u0p, u1p, g1p, g0p):
        ref[edge] = jnp.zeros(ref.shape[1:], BF16)

    def rows_loop(lo, hi, fn):
        def step(r, c):
            fn(r)
            return c

        lax.fori_loop(lo, hi, step, 0)

    def regroup(src, r):
        rows = src[pl.ds(S * r, S)].reshape(M, C)
        return jnp.dot(perm[...], rows, preferred_element_type=F32).astype(BF16).reshape(A, T, C)

    wacc[...] = jnp.zeros_like(wacc)

    def load0(r):
        in_copy(0, r).wait()
        u0p[1 + r, 1 : A + 1] = regroup(raw, r)

    rows_loop(0, R, load0)

    pl.semaphore_wait(barrier, 2 * n + 1)

    right, left = lon_at(1), lon_at(-1)

    def rim(ref, e, i, src, dst, where):
        return planned(ref.at[src], ref.at[dst], rim_s.at[e, i], rim_r.at[e, i], where)

    seam = R - lat * (R - 1)
    inner = pl.ds(1, R)

    def rim_right(ref, e):
        last, first = pl.ds(A, 1), pl.ds(0, 1)
        return [
            rim(ref, e, 0, (inner, last), (inner, first), dev(right, lat, mem)),
            rim(ref, e, 2, (seam, last), (edge, first), dev(right, other, mem)),
        ]

    def rim_left(ref, e):
        first, last = pl.ds(1, 1), pl.ds(A + 1, 1)
        return [
            rim(ref, e, 1, (inner, first), (inner, last), dev(left, lat, mem)),
            rim(ref, e, 3, (seam, first), (edge, last), dev(left, other, mem)),
        ]

    def rim_lat(ref, e, k):
        at = pl.ds(1 + k * CH, CH)
        return [rim(ref, e, 4 + k, (seam, at), (edge, at), dev(me, other, mem))]

    def rim_lat_all(ref, e):
        at = pl.ds(1, A)
        return [rim(ref, e, 4, (seam, at), (edge, at), dev(me, other, mem))]

    def interior_first(m):
        return [*range(1, 1 + m), NK - 1, 0, *range(1 + m, NK - 1)]

    def pick(order, i):
        return sum(k * ((i + NK - j) // NK - (i + NK - j - 1) // NK) for j, k in enumerate(order))

    def send_after(ref, e, i, k, order):
        start(rim_lat(ref, e, k))

        @pl.when(i == order.index(NK - 1))
        def _():
            start(rim_right(ref, e))

        @pl.when(i == order.index(0))
        def _():
            start(rim_left(ref, e))

    def wait_before(ref, e, i, order):
        done = set()
        for j, k in enumerate(order):
            need = [p for p in (k - 1, k, k + 1) if 0 <= p < NK and p not in done]
            done.update(need)
            if e == 0:
                need = [0] if j == 0 else []
            if not need and 0 < k < NK - 1:
                continue

            @pl.when(i == j)
            def _(k=k, need=need):
                for p in need:
                    finish(rim_lat(ref, e, p) if e else rim_lat_all(ref, e))
                if k == NK - 1:
                    finish(rim_left(ref, e))
                if k == 0:
                    finish(rim_right(ref, e))

    def wait_all(ref, e):
        for k in range(NK):
            finish(rim_lat(ref, e, k))
        finish(rim_left(ref, e) + rim_right(ref, e))

    def start(copies):
        for c in copies:
            c.start()

    def finish(copies):
        for c in copies:
            c.wait()

    def products(ref, r, a, ch, lanes, other_factor):
        for p in range(3):
            row = ref[r + p, pl.ds(a, ch + 2), :, lanes]
            yield [row[q : q + ch] * other_factor(p, q) for q in range(3)]

    def conv(ref, l, r, a, ch, lanes, rev):
        def tap(p, q):
            return kb[l, 3 * (2 - p) + 2 - q if rev else 3 * p + q, :, lanes]

        s0, s1, s2 = [v[0] + v[1] + v[2] for v in products(ref, r, a, ch, lanes, tap)]
        return s0 + s1 + s2

    def chunks(fn, ch, unroll=False):
        def step(i, c):
            fn(i * ch)
            return c

        lax.fori_loop(0, A // ch, step, 0, unroll=unroll)

    def each_row(fn):
        def step(r, c):
            fn(r)
            return c

        lax.fori_loop(0, R, step, 0, unroll=True)

    def tree(v):
        v = [v[i] for i in range(v.shape[0])]
        while len(v) > 1:
            v = [a + b for a, b in zip(v[::2], v[1::2])] + v[len(v) - len(v) % 2 :]
        return v[0]

    def add_taps(k, t, lanes, prod):
        both = tree(prod).astype(F32).reshape(2, 8, 128)
        kacc[k, t, :, lanes] += both[0] + both[1]

    def lane_mean(v, ch):
        m = jnp.sum(v.astype(F32), axis=-1, keepdims=True) * (1.0 / C)
        return jnp.broadcast_to(m, (ch, T, 128))

    def conv_norm(src, l, a, hid, rc):
        def go(r):
            convs = [conv(src, l, r, a, CH, lanes, False) for lanes in groups]
            c0, c1, c2, c3 = [c * c for c in convs]
            recip = lax.rsqrt(lane_mean((c0 + c1) + (c2 + c3), CH) + 1e-6)
            rc[r] = recip
            for lanes, c in zip(groups, convs):
                hid[r, :, :, lanes] = (c.astype(F32) * recip).astype(BF16)

        each_row(go)

    def mix(v, l):
        return jnp.dot(v.reshape(MC, C), w_ref[l], preferred_element_type=F32).reshape(R, CH, T, C)

    def mix_back(v, l):
        return lax.dot_general(
            v.reshape(MC, C), w_ref[l], (((1,), (1,)), ((), ())), preferred_element_type=F32
        ).astype(BF16).reshape(R, CH, T, C)

    def norm_back(dst, hid, rc, a):
        def go(r):
            ns = [hid[r, :, :, lanes] for lanes in groups]
            gs = [gn[r, :, :, lanes] for lanes in groups]
            d0_, d1_, d2_, d3_ = [g * v for g, v in zip(gs, ns)]
            mean = lane_mean((d0_ + d1_) + (d2_ + d3_), CH)
            recip = rc[r]
            for lanes, g, v in zip(groups, gs, ns):
                back = recip * (g.astype(F32) - v.astype(F32) * mean)
                dst[1 + r, pl.ds(1 + a, CH), :, lanes] = back.astype(BF16)

        each_row(go)

    def weight_sum(l, hid, gp):
        wacc[l] += lax.dot_general(
            hid[...].reshape(MC, C), gp[...].reshape(MC, C), (((0,), (0,)), ((), ())), preferred_element_type=F32
        )

    def slot(pair, i, odd):
        return pair[odd].at[i // 2]

    def pipeline(before, first, second, after):
        before(0)
        first(0, 0)
        pairs = (NK - 1) // 2

        def both(i, odd):
            second(i - 1, 1 - odd)
            first(i, odd)

        def step(j, c):
            before(2 * j + 1)
            before(2 * j + 2)
            both(2 * j + 1, 1)
            both(2 * j + 2, 0)
            after(2 * j)
            after(2 * j + 1)
            return c

        lax.fori_loop(0, pairs, step, 0)
        if NK % 2 == 0:
            before(NK - 1)
            both(NK - 1, 1)
            after(NK - 2)


    own_rows = pl.ds(pl.multiple_of(lat * H, H), H)
    other_rows = pl.ds(pl.multiple_of(other * H, H), H)
    own_cols = pl.ds(pl.multiple_of(mem * H, H), H)
    other_cols = pl.ds(pl.multiple_of(omem * H, H), H)
    piece = H // n
    wire = w2s.dtype

    def red(l, stage, i, src, dst, where):
        return planned(src, dst, red_s.at[l, stage, i], red_r.at[l, stage, i], where)

    def plan(l, stage):
        if stage == 0:
            return [red(l, 0, 0, w0s.at[l], w0r.at[l], dev(me, other, mem))]
        if stage == 1:
            return [red(l, 1, 0, w1s.at[l], w1r.at[l], dev(me, lat, omem))]
        if stage == 2:
            return [
                red(l, 2, d, w2s.at[l, lon_at(d)], w2r.at[l, me], dev(lon_at(d), lat, mem)) for d in range(1, n)
            ]
        if stage == 3:
            return [red(l, 3, d, w3s.at[l], w3r.at[l, lat, me], dev(lon_at(d), lat, mem)) for d in range(1, n)]
        return [red(l, 4, 0, w3r.at[l, lat], w3r.at[l, lat], dev(me, other, mem))]

    def stage(l, step):
        if step:
            finish(plan(l, step - 1))
        if step == 0:
            w0s[l] = wacc[l, other_rows, :].astype(BF16)
        elif step == 1:
            wacc[l, own_rows, :] += w0r[l].astype(F32)
            w1s[l] = wacc[l, own_rows, other_cols].astype(BF16)
        elif step == 2:
            total = wacc[l, own_rows, own_cols] + w1r[l].astype(F32)
            wacc[l, own_rows, own_cols] = total
            w2s[l] = total.reshape(n, piece, H).astype(wire)
        elif step == 3:
            at = pl.multiple_of(lat * H + me * piece, piece)
            total = wacc[l, pl.ds(at, piece), own_cols]
            for d in range(1, n):
                total = total + w2r[l, lon_at(d)].astype(F32)
            done = (total * factor).astype(wire)
            w3s[l] = done
            w3r[l, lat, me] = done
        elif step == 5:
            wgrad[l] = w3r[l].reshape(C, H).astype(F32)
            return
        start(plan(l, step))

    def tap_plan(step):
        if step == 0:
            return [
                red(0, 0, 1, kown, kin.at[0], dev(me, other, mem)),
                red(0, 0, 2, koth, kin.at[1], dev(me, lat, omem)),
                red(0, 0, 3, koth, kin.at[2], dev(me, other, omem)),
            ]
        return [red(0, 2, n + d, ks2, kr2.at[me], dev(lon_at(d), lat, mem)) for d in range(1, n)]

    def tap_stage(step):
        if step:
            finish(tap_plan(step - 1))
        if step == 0:
            for k in range(2):
                for t in range(9):
                    kv[k, t : t + 1, :] = jnp.sum(kacc[k, t], axis=0, keepdims=True)
            kown[...] = kv[:, :, own_cols].astype(BF16)
            koth[...] = kv[:, :, other_cols].astype(BF16)
        elif step == 1:
            total = kv[:, :, own_cols]
            for j in range(3):
                total = total + kin[j].astype(F32)
            both = total.astype(BF16)
            ks2[...] = both
            kr2[me] = both
        else:
            ks = kr2[0].astype(F32)
            for j in range(1, n):
                ks = ks + kr2[j].astype(F32)
            for k in range(2):
                kgrad[:, k, :] = ks[k, :9, :] * factor
            return
        start(tap_plan(step))

    rims0 = rim_lat_all(u0p, 0) + rim_right(u0p, 0) + rim_left(u0p, 0)
    start(rims0)

    def load1(r):
        in_copy(1, r).wait()
        g1[r] = regroup(cotraw, r)

    rows_loop(0, R, load1)
    mixed, inward = interior_first(min(3, NK - 2)), interior_first(NK - 2)

    def block0(i):
        wait_before(u0p, 0, i, mixed)
        k = pick(mixed, i)
        a = k * CH
        at = pl.ds(a, CH)
        conv_norm(u0p, 0, a, hid0.at[:, at], rc0.at[:, at])
        pre[...] = mix(hid0[:, at], 0)

        def go(r):
            for lanes in groups:
                gel, slope = gelu_both(pre[r, :, :, lanes])
                d0[r, at, :, lanes] = slope.astype(BF16)
                u = u0p[1 + r, pl.ds(1 + a, CH), :, lanes]
                u1p[1 + r, pl.ds(1 + a, CH), :, lanes] = u + gel.astype(BF16)

        each_row(go)
        send_after(u1p, 1, i, k, mixed)

    rows_loop(0, NK, block0)

    hid1, rc1, gp = (hid1_0, hid1_1), (rc1_0, rc1_1), (gp_0, gp_1)

    def block1(i, odd):
        k = pick(mixed, i)
        a = k * CH
        at = pl.ds(a, CH)
        hid, out = slot(hid1, i, odd), slot(gp, i, odd)
        conv_norm(u1p, 1, a, hid, slot(rc1, i, odd))
        pre[...] = mix(hid[...], 1)

        def go(r):
            for lanes in groups:
                slope = gelu_both(pre[r, :, :, lanes])[1]
                g = g1[r, at, :, lanes].astype(F32)
                out[r, :, :, lanes] = (g * slope).astype(BF16)

        each_row(go)
        weight_sum(1, hid, out)

    def back1(i, odd):
        gn[...] = mix_back(slot(gp, i, odd)[...], 1)
        norm_back(g1p, slot(hid1, i, odd), slot(rc1, i, odd), pick(mixed, i) * CH)

    def send1(i):
        send_after(g1p, 2, i, pick(mixed, i), mixed)

    pipeline(lambda i: wait_before(u1p, 1, i, mixed), block1, back1, send1)
    stage(1, 0)
    back1(NK - 1, (NK - 1) % 2)
    send1(NK - 1)

    def back0(i, odd):
        a = pick(inward, i) * CH
        at = pl.ds(a, CH)
        out = slot(gp, i, odd)

        def go(r):
            for lanes in groups:
                s = conv(g1p, 1, r, a, CH, lanes, True) + g1[r, at, :, lanes]
                g1[r, at, :, lanes] = s
                out[r, :, :, lanes] = s * d0[r, at, :, lanes]

        each_row(go)

    def sum0(i, odd):
        weight_sum(0, hid0.at[:, pl.ds(pick(inward, i) * CH, CH)], slot(gp, i, odd))

    def chain1(i):
        @pl.when(i == 3)
        def _():
            stage(1, 1)

    pipeline(lambda i: wait_before(g1p, 2, i, inward), back0, sum0, chain1)
    sum0(NK - 1, (NK - 1) % 2)
    stage(0, 0)

    def norm0(i, odd):
        k = pick(inward, i)
        a = k * CH
        at = pl.ds(a, CH)
        gn[...] = mix_back(slot(gp, i, odd)[...], 0)
        norm_back(g0p, hid0.at[:, at], rc0.at[:, at], a)
        send_after(g0p, 3, i, k, inward)

    def norm0_pair(j):
        norm0(2 * j, 0)
        norm0(2 * j + 1, 1)

        @pl.when(j == 1)
        def _():
            stage(0, 1)

    rows_loop(0, NK // 2, norm0_pair)
    if NK % 2:
        norm0(NK - 1, 0)
    stage(1, 2)

    def tap_sums(k, moved, still, rev, lo, hi):
        def row(r):
            def go(a):
                for lanes in groups:
                    v = still[1 + r, pl.ds(1 + a, WIDE), :, lanes]
                    for p, prods in enumerate(products(moved, r, a, WIDE, lanes, lambda p, q: v)):
                        for q, prod in enumerate(prods):
                            add_taps(k, 3 * (2 - p) + 2 - q if rev else 3 * p + q, lanes, prod)

            chunks(go, WIDE)

        rows_loop(lo, hi, row)

    tap_sums(1, g1p, u1p, True, 0, R)
    stage(1, 3)
    tap_sums(0, u0p, g0p, False, 0, R // 2)
    stage(0, 2)
    tap_sums(0, u0p, g0p, False, R // 2, R)
    tap_stage(0)
    wait_all(g0p, 3)

    def out_copy(r):
        return pltpu.make_async_copy(raw.at[pl.ds(S * r, S)], out_hbm.at[0, pl.ds(S * r, S)], out_sem.at[r])

    def last(r):
        def go(a):
            for lanes in groups:
                s = conv(g0p, 0, r, a, WIDE, lanes, True) + g1[r, pl.ds(a, WIDE), :, lanes]
                row_buf[pl.ds(a, WIDE), :, lanes] = s

        chunks(go, WIDE)
        rows = jnp.dot(unperm[...], row_buf[...].reshape(M, C), preferred_element_type=F32).astype(BF16)
        raw[pl.ds(S * r, S)] = rows.reshape(S, S * A, C)
        out_copy(r).start()

    rows_loop(0, R, last)
    stage(1, 4)
    tap_stage(1)
    stage(0, 3)
    stage(1, 5)
    tap_stage(2)
    stage(0, 4)
    stage(0, 5)
    finish([out_copy(r) for r in range(R)])


def hand_over(pieces, *refs):
    srcs, dsts, mids, sem = refs[:3], refs[3:6], refs[6:9], refs[9]
    step = srcs[0].shape[1] // pieces
    parts = [tuple(ref.at[:, pl.ds(i * step, step)] for ref in (srcs[0], mids[0], dsts[0])) for i in range(pieces)]
    parts += [(srcs[j], mids[j], dsts[j]) for j in (2, 1)]
    loads = [pltpu.make_async_copy(a, b, sem.at[0, i]) for i, (a, b, _) in enumerate(parts)]
    stores = [pltpu.make_async_copy(b, c, sem.at[1, i]) for i, (_, b, c) in enumerate(parts)]
    for c in loads:
        c.start()
    for a, b in zip(loads, stores):
        a.wait()
        b.start()
    for c in stores:
        c.wait()


def body(inputs, cotangent, dw_kernel, pw_weight):
    _, rows, cols, C = inputs.shape
    n = lax.axis_size("lon")
    R, A, T, H = rows // S, cols // S, S * S, C // 2
    piece = H // n
    wire = BF16 if piece % 16 == 0 else F32
    samples = inputs.size // C * n * lax.axis_size("lat") * lax.axis_size("mem")
    anywhere = pl.BlockSpec(memory_space=pl.ANY)
    local = pl.BlockSpec(memory_space=pltpu.VMEM)
    padded = pltpu.VMEM((R + 2, A + 2, T, C), BF16)
    cells = pltpu.VMEM((R, A, T, C), BF16)
    CH = max(c for c in (1, 2, 4) if A % c == 0)
    chunk = pltpu.VMEM((R, CH, T, C), BF16)
    half = (A // CH + 1) // 2
    steps = pltpu.VMEM((half, R, CH, T, C), BF16)
    scoped = [
        padded, padded, padded, padded,
        cells, cells, cells,
        pltpu.VMEM((R, A, T, 128), F32),
        steps, steps,
        pltpu.VMEM((half, R, CH, T, 128), F32), pltpu.VMEM((half, R, CH, T, 128), F32),
        steps, steps,
        pltpu.VMEM((R, CH, T, C), F32),
        chunk,
        pltpu.VMEM((A, T, C), BF16),
        pltpu.VMEM((2, 9, T, C), BF16),
    ]
    scratch = [
        pltpu.VMEM((rows, cols, C), BF16),
        pltpu.VMEM((rows, cols, C), BF16),
        pltpu.VMEM((A * T, A * T), BF16),
        pltpu.VMEM((A * T, A * T), BF16),
        pltpu.VMEM((2, 9, 8, C), F32),
        pltpu.VMEM((2, C, C), F32),
        pltpu.VMEM((2, H, C), BF16), pltpu.VMEM((2, H, C), BF16),
        pltpu.VMEM((2, H, H), BF16), pltpu.VMEM((2, H, H), BF16),
        pltpu.VMEM((2, n, piece, H), wire), pltpu.VMEM((2, n, piece, H), wire),
        pltpu.VMEM((2, piece, H), wire), pltpu.VMEM((2, 2, n, piece, H), wire),
        pltpu.VMEM((2, 16, C), F32),
        pltpu.VMEM((2, 16, H), BF16), pltpu.VMEM((2, 16, H), BF16), pltpu.VMEM((3, 2, 16, H), BF16),
        pltpu.VMEM((2, 16, H), BF16), pltpu.VMEM((n, 2, 16, H), BF16),
        pltpu.SemaphoreType.DMA((2, R)), pltpu.SemaphoreType.DMA((R,)),
        pltpu.SemaphoreType.DMA((4, 4 + A // CH)), pltpu.SemaphoreType.DMA((4, 4 + A // CH)),
        pltpu.SemaphoreType.DMA((2, 5, 2 * n)), pltpu.SemaphoreType.DMA((2, 5, 2 * n)),
    ]
    made = pl.pallas_call(
        functools.partial(kernel, n, 1.0 / math.sqrt(samples), scoped),
        out_shape=(
            jax.ShapeDtypeStruct(inputs.shape, BF16),
            jax.ShapeDtypeStruct((9, 2, H), F32),
            jax.ShapeDtypeStruct((2, C, H), F32),
        ),
        in_specs=[anywhere, anywhere, local, local],
        out_specs=(anywhere, local, local),
        scratch_shapes=scratch,
        name="blocks",
        compiler_params=pltpu.CompilerParams(
            collective_id=0, has_side_effects=True, vmem_limit_bytes=60 * 1024 * 1024
        ),
    )(inputs, cotangent, jnp.transpose(dw_kernel, (1, 0, 2)), pw_weight)
    pieces = max(p for p in (1, 2, 3, 4, 6, 8) if rows % p == 0)
    out, kgrad, wgrad = pl.pallas_call(
        functools.partial(hand_over, pieces),
        out_shape=tuple(jax.ShapeDtypeStruct(v.shape, v.dtype) for v in made),
        in_specs=[anywhere] * 3,
        out_specs=(anywhere,) * 3,
        scratch_shapes=[*(pltpu.VMEM(v.shape, v.dtype) for v in made), pltpu.SemaphoreType.DMA((2, pieces + 2))],
        compiler_params=pltpu.CompilerParams(vmem_limit_bytes=60 * 1024 * 1024),
        name="hand_over",
    )(*made)
    return out, jnp.transpose(kgrad, (1, 0, 2)), wgrad


def solution(mesh):
    placed = (P("mem", "lat", "lon", None), P("mem", "lat", "lon", None), P(), P())
    return jax.shard_map(
        body,
        mesh=mesh,
        in_specs=placed,
        out_specs=(P("mem", "lat", "lon", None), P(None, None, "mem"), P(None, None, "mem")),
        check_vma=False,
    )
```

```python
import functools
import math

import jax
import jax.numpy as jnp
from jax import lax
from jax.experimental import pallas as pl
from jax.experimental.pallas import tpu as pltpu
from jax.sharding import PartitionSpec as P

S = 4
F32 = jnp.float32
BF16 = jnp.bfloat16
MESH = pl.DeviceIdType.MESH
ROOT = math.sqrt(2.0 / math.pi)
CUBE = 0.044715


def gelu_both(x):
    xx = x * x
    t = jnp.tanh(x * (ROOT + (ROOT * CUBE) * xx))
    h = 0.5 + 0.5 * t
    g = x * h
    return g, h + g * (1.0 - t) * (ROOT + (3.0 * ROOT * CUBE) * xx)


def kernel(n, factor, scoped, *refs):
    pl.run_scoped(lambda *inner: work(n, factor, *refs, *inner), *scoped)


def work(
    n, factor,
    x_hbm, cot_hbm, dw_ref, w_hbm,
    out_hbm, kgrad, wgrad,
    raw, cotraw, perm, unperm, kacc, wacc,
    w0s, w0r, w1s, w1r, w2s, w2r, w3s, w3r, kv, kown, koth, kin, ks2, kr2,
    w_ref, wg, io_sem,
    in_sem, out_sem, rim_s, rim_r, red_s, red_r,
    u0p, u1p, g1p, g0p, g1, hid0, d0, rc0, hid1_0, hid1_1, rc1_0, rc1_1, gp_0, gp_1, pre, gn, row_buf, kb,
):
    R, A, T, C = hid0.shape
    M = A * T
    H = C // 2
    CH = gn.shape[1]
    NK = A // CH
    MC = R * CH * T
    WIDE = max(c for c in (1, 2, 4, 7) if A % c == 0)
    groups = [slice(g, g + 128) for g in range(0, C, 128)]
    me, lat, mem = lax.axis_index("lon"), lax.axis_index("lat"), lax.axis_index("mem")
    other, omem = 1 - lat, 1 - mem

    def lon_at(d):
        return lax.rem(me + (d % n), n)

    def dev(lon_i, lat_i, mem_i):
        return {"lon": lon_i, "lat": lat_i, "mem": mem_i}

    def planned(src, dst, ssem, rsem, where):
        return pltpu.make_async_remote_copy(
            src_ref=src, dst_ref=dst, send_sem=ssem, recv_sem=rsem, device_id=where, device_id_type=MESH
        )

    def in_copy(i, r):
        src, dst = ((x_hbm, raw), (cot_hbm, cotraw))[i]
        return pltpu.make_async_copy(src.at[0, pl.ds(S * r, S)], dst.at[pl.ds(S * r, S)], in_sem.at[i, r])

    for i in range(2):
        for r in range(R):
            in_copy(i, r).start()
    w_copy = pltpu.make_async_copy(w_hbm, w_ref, io_sem.at[0])
    w_copy.start()

    barrier = pltpu.get_barrier_semaphore()
    for d in range(n):
        for la in (lat, other):
            if d == 0 and la is lat:
                continue
            pl.semaphore_signal(barrier, inc=1, device_id=dev(lon_at(d), la, mem), device_id_type=MESH)
    for la in (lat, other):
        pl.semaphore_signal(barrier, inc=1, device_id=dev(me, la, omem), device_id_type=MESH)

    def one_hot(rows_dim):
        o = lax.broadcasted_iota(jnp.int32, (M, M), rows_dim)
        i = lax.broadcasted_iota(jnp.int32, (M, M), 1 - rows_dim)
        a, s, b = o >> 4, (o >> 2) & 3, o & 3
        return jnp.where(i == s * (A * S) + a * S + b, 1.0, 0.0).astype(BF16)

    perm[...] = one_hot(0)
    unperm[...] = one_hot(1)
    for t in range(9):
        taps_f = dw_ref[t].astype(F32)
        for l in range(2):
            kb[l, t] = jnp.broadcast_to(taps_f[l : l + 1, :], (T, C)).astype(BF16)
    kacc[...] = jnp.zeros_like(kacc)
    kv[...] = jnp.zeros_like(kv)
    edge = lat * (R + 1)
    for ref in (u0p, u1p, g1p, g0p):
        ref[edge] = jnp.zeros(ref.shape[1:], BF16)

    def rows_loop(lo, hi, fn):
        def step(r, c):
            fn(r)
            return c

        lax.fori_loop(lo, hi, step, 0)

    def regroup(src, r):
        rows = src[pl.ds(S * r, S)].reshape(M, C)
        return jnp.dot(perm[...], rows, preferred_element_type=F32).astype(BF16).reshape(A, T, C)

    wacc[...] = jnp.zeros_like(wacc)

    def load0(r):
        in_copy(0, r).wait()
        u0p[1 + r, 1 : A + 1] = regroup(raw, r)

    rows_loop(0, R, load0)

    pl.semaphore_wait(barrier, 2 * n + 1)

    right, left = lon_at(1), lon_at(-1)

    def rim(ref, e, i, src, dst, where):
        return planned(ref.at[src], ref.at[dst], rim_s.at[e, i], rim_r.at[e, i], where)

    seam = R - lat * (R - 1)
    inner = pl.ds(1, R)

    def rim_right(ref, e):
        last, first = pl.ds(A, 1), pl.ds(0, 1)
        return [
            rim(ref, e, 0, (inner, last), (inner, first), dev(right, lat, mem)),
            rim(ref, e, 2, (seam, last), (edge, first), dev(right, other, mem)),
        ]

    def rim_left(ref, e):
        first, last = pl.ds(1, 1), pl.ds(A + 1, 1)
        return [
            rim(ref, e, 1, (inner, first), (inner, last), dev(left, lat, mem)),
            rim(ref, e, 3, (seam, first), (edge, last), dev(left, other, mem)),
        ]

    def rim_lat(ref, e, k):
        at = pl.ds(1 + k * CH, CH)
        return [rim(ref, e, 4 + k, (seam, at), (edge, at), dev(me, other, mem))]

    def rim_lat_all(ref, e):
        at = pl.ds(1, A)
        return [rim(ref, e, 4, (seam, at), (edge, at), dev(me, other, mem))]

    def interior_first(m):
        return [*range(1, 1 + m), NK - 1, 0, *range(1 + m, NK - 1)]

    def pick(order, i):
        return sum(k * ((i + NK - j) // NK - (i + NK - j - 1) // NK) for j, k in enumerate(order))

    def send_after(ref, e, i, k, order):
        start(rim_lat(ref, e, k))

        @pl.when(i == order.index(NK - 1))
        def _():
            start(rim_right(ref, e))

        @pl.when(i == order.index(0))
        def _():
            start(rim_left(ref, e))

    def wait_before(ref, e, i, order):
        done = set()
        for j, k in enumerate(order):
            need = [p for p in (k - 1, k, k + 1) if 0 <= p < NK and p not in done]
            done.update(need)
            if e == 0:
                need = [0] if j == 0 else []
            if not need and 0 < k < NK - 1:
                continue

            @pl.when(i == j)
            def _(k=k, need=need):
                for p in need:
                    finish(rim_lat(ref, e, p) if e else rim_lat_all(ref, e))
                if k == NK - 1:
                    finish(rim_left(ref, e))
                if k == 0:
                    finish(rim_right(ref, e))

    def wait_all(ref, e):
        for k in range(NK):
            finish(rim_lat(ref, e, k))
        finish(rim_left(ref, e) + rim_right(ref, e))

    def start(copies):
        for c in copies:
            c.start()

    def finish(copies):
        for c in copies:
            c.wait()

    def products(ref, r, a, ch, lanes, other_factor):
        for p in range(3):
            row = ref[r + p, pl.ds(a, ch + 2), :, lanes]
            yield [row[q : q + ch] * other_factor(p, q) for q in range(3)]

    def conv(ref, l, r, a, ch, lanes, rev):
        def tap(p, q):
            return kb[l, 3 * (2 - p) + 2 - q if rev else 3 * p + q, :, lanes]

        s0, s1, s2 = [v[0] + v[1] + v[2] for v in products(ref, r, a, ch, lanes, tap)]
        return s0 + s1 + s2

    def chunks(fn, ch, unroll=False):
        def step(i, c):
            fn(i * ch)
            return c

        lax.fori_loop(0, A // ch, step, 0, unroll=unroll)

    def each_row(fn):
        def step(r, c):
            fn(r)
            return c

        lax.fori_loop(0, R, step, 0, unroll=True)

    def tree(v):
        v = [v[i] for i in range(v.shape[0])]
        while len(v) > 1:
            v = [a + b for a, b in zip(v[::2], v[1::2])] + v[len(v) - len(v) % 2 :]
        return v[0]

    def add_taps(k, t, lanes, prod):
        both = tree(prod).astype(F32).reshape(2, 8, 128)
        kacc[k, t, :, lanes] += both[0] + both[1]

    def lane_mean(v, ch):
        m = jnp.sum(v.astype(F32), axis=-1, keepdims=True) * (1.0 / C)
        return jnp.broadcast_to(m, (ch, T, 128))

    def conv_norm(src, l, a, hid, rc):
        def go(r):
            convs = [conv(src, l, r, a, CH, lanes, False) for lanes in groups]
            c0, c1, c2, c3 = [c * c for c in convs]
            recip = lax.rsqrt(lane_mean((c0 + c1) + (c2 + c3), CH) + 1e-6)
            rc[r] = recip
            for lanes, c in zip(groups, convs):
                hid[r, :, :, lanes] = (c.astype(F32) * recip).astype(BF16)

        each_row(go)

    def mix(v, l):
        return jnp.dot(v.reshape(MC, C), w_ref[l], preferred_element_type=F32).reshape(R, CH, T, C)

    def mix_back(v, l):
        return lax.dot_general(
            v.reshape(MC, C), w_ref[l], (((1,), (1,)), ((), ())), preferred_element_type=F32
        ).astype(BF16).reshape(R, CH, T, C)

    def norm_back(dst, hid, rc, a):
        def go(r):
            ns = [hid[r, :, :, lanes] for lanes in groups]
            gs = [gn[r, :, :, lanes] for lanes in groups]
            d0_, d1_, d2_, d3_ = [g * v for g, v in zip(gs, ns)]
            mean = lane_mean((d0_ + d1_) + (d2_ + d3_), CH)
            recip = rc[r]
            for lanes, g, v in zip(groups, gs, ns):
                back = recip * (g.astype(F32) - v.astype(F32) * mean)
                dst[1 + r, pl.ds(1 + a, CH), :, lanes] = back.astype(BF16)

        each_row(go)

    def weight_sum(l, hid, gp):
        wacc[l] += lax.dot_general(
            hid[...].reshape(MC, C), gp[...].reshape(MC, C), (((0,), (0,)), ((), ())), preferred_element_type=F32
        )

    def slot(pair, i, odd):
        return pair[odd].at[i // 2]

    def pipeline(before, first, second, after):
        before(0)
        first(0, 0)

        def both(i, odd):
            before(i)
            second(i - 1, 1 - odd)
            first(i, odd)
            after(i - 1)

        def step(j, c):
            both(2 * j + 1, 1)
            both(2 * j + 2, 0)
            return c

        lax.fori_loop(0, (NK - 1) // 2, step, 0)
        if NK % 2 == 0:
            both(NK - 1, 1)

    own_rows = pl.ds(pl.multiple_of(lat * H, H), H)
    other_rows = pl.ds(pl.multiple_of(other * H, H), H)
    own_cols = pl.ds(pl.multiple_of(mem * H, H), H)
    other_cols = pl.ds(pl.multiple_of(omem * H, H), H)
    piece = H // n
    wire = w2s.dtype

    def red(l, stage, i, src, dst, where):
        return planned(src, dst, red_s.at[l, stage, i], red_r.at[l, stage, i], where)

    def plan(l, stage):
        if stage == 0:
            return [red(l, 0, 0, w0s.at[l], w0r.at[l], dev(me, other, mem))]
        if stage == 1:
            return [red(l, 1, 0, w1s.at[l], w1r.at[l], dev(me, lat, omem))]
        if stage == 2:
            return [
                red(l, 2, d, w2s.at[l, lon_at(d)], w2r.at[l, me], dev(lon_at(d), lat, mem)) for d in range(1, n)
            ]
        if stage == 3:
            return [red(l, 3, d, w3s.at[l], w3r.at[l, lat, me], dev(lon_at(d), lat, mem)) for d in range(1, n)]
        return [red(l, 4, 0, w3r.at[l, lat], w3r.at[l, lat], dev(me, other, mem))]

    def wgrad_copy(l):
        return pltpu.make_async_copy(wg.at[l], wgrad.at[l], io_sem.at[1 + l])

    def stage(l, step):
        if step:
            finish(plan(l, step - 1))
        if step == 0:
            w0s[l] = wacc[l, other_rows, :].astype(BF16)
        elif step == 1:
            wacc[l, own_rows, :] += w0r[l].astype(F32)
            w1s[l] = wacc[l, own_rows, other_cols].astype(BF16)
        elif step == 2:
            total = wacc[l, own_rows, own_cols] + w1r[l].astype(F32)
            wacc[l, own_rows, own_cols] = total
            w2s[l] = total.reshape(n, piece, H).astype(wire)
        elif step == 3:
            at = pl.multiple_of(lat * H + me * piece, piece)
            total = wacc[l, pl.ds(at, piece), own_cols]
            for d in range(1, n):
                total = total + w2r[l, lon_at(d)].astype(F32)
            done = (total * factor).astype(wire)
            w3s[l] = done
            w3r[l, lat, me] = done
        elif step == 5:
            wg[l] = w3r[l].reshape(C, H).astype(F32)
            start([wgrad_copy(l)])
            return
        start(plan(l, step))

    def tap_plan(step):
        if step == 0:
            return [
                red(0, 0, 1, kown, kin.at[0], dev(me, other, mem)),
                red(0, 0, 2, koth, kin.at[1], dev(me, lat, omem)),
                red(0, 0, 3, koth, kin.at[2], dev(me, other, omem)),
            ]
        return [red(0, 2, n + d, ks2, kr2.at[me], dev(lon_at(d), lat, mem)) for d in range(1, n)]

    def tap_stage(step):
        if step:
            finish(tap_plan(step - 1))
        if step == 0:
            for k in range(2):
                for t in range(9):
                    kv[k, t : t + 1, :] = jnp.sum(kacc[k, t], axis=0, keepdims=True)
            kown[...] = kv[:, :, own_cols].astype(BF16)
            koth[...] = kv[:, :, other_cols].astype(BF16)
        elif step == 1:
            total = kv[:, :, own_cols]
            for j in range(3):
                total = total + kin[j].astype(F32)
            both = total.astype(BF16)
            ks2[...] = both
            kr2[me] = both
        else:
            ks = kr2[0].astype(F32)
            for j in range(1, n):
                ks = ks + kr2[j].astype(F32)
            for k in range(2):
                kgrad[:, k, :] = ks[k, :9, :] * factor
            return
        start(tap_plan(step))

    rims0 = rim_lat_all(u0p, 0) + rim_right(u0p, 0) + rim_left(u0p, 0)
    start(rims0)

    def load1(r):
        in_copy(1, r).wait()
        g1[r] = regroup(cotraw, r)

    rows_loop(0, R, load1)
    w_copy.wait()
    early, mixed, inward = [interior_first(min(m, NK - 2)) for m in (4, 3, NK - 2)]

    def block0(i):
        wait_before(u0p, 0, i, early)
        k = pick(early, i)
        a = k * CH
        at = pl.ds(a, CH)
        conv_norm(u0p, 0, a, hid0.at[:, at], rc0.at[:, at])
        pre[...] = mix(hid0[:, at], 0)

        def go(r):
            for lanes in groups:
                gel, slope = gelu_both(pre[r, :, :, lanes])
                d0[r, at, :, lanes] = slope.astype(BF16)
                u = u0p[1 + r, pl.ds(1 + a, CH), :, lanes]
                u1p[1 + r, pl.ds(1 + a, CH), :, lanes] = u + gel.astype(BF16)

        each_row(go)
        send_after(u1p, 1, i, k, early)

    rows_loop(0, NK, block0)

    hid1, rc1, gp = (hid1_0, hid1_1), (rc1_0, rc1_1), (gp_0, gp_1)

    def block1(i, odd):
        k = pick(mixed, i)
        a = k * CH
        at = pl.ds(a, CH)
        hid, out = slot(hid1, i, odd), slot(gp, i, odd)
        conv_norm(u1p, 1, a, hid, slot(rc1, i, odd))
        pre[...] = mix(hid[...], 1)

        def go(r):
            for lanes in groups:
                slope = gelu_both(pre[r, :, :, lanes])[1]
                g = g1[r, at, :, lanes].astype(F32)
                out[r, :, :, lanes] = (g * slope).astype(BF16)

        each_row(go)
        weight_sum(1, hid, out)

    def back1(i, odd):
        gn[...] = mix_back(slot(gp, i, odd)[...], 1)
        norm_back(g1p, slot(hid1, i, odd), slot(rc1, i, odd), pick(mixed, i) * CH)

    def send1(i):
        send_after(g1p, 2, i, pick(mixed, i), mixed)

    pipeline(lambda i: wait_before(u1p, 1, i, mixed), block1, back1, send1)
    stage(1, 0)
    back1(NK - 1, (NK - 1) % 2)
    send1(NK - 1)

    def back0(i, odd):
        a = pick(inward, i) * CH
        at = pl.ds(a, CH)
        out = slot(gp, i, odd)

        def go(r):
            for lanes in groups:
                s = conv(g1p, 1, r, a, CH, lanes, True) + g1[r, at, :, lanes]
                g1[r, at, :, lanes] = s
                out[r, :, :, lanes] = s * d0[r, at, :, lanes]

        each_row(go)

    def sum0(i, odd):
        weight_sum(0, hid0.at[:, pl.ds(pick(inward, i) * CH, CH)], slot(gp, i, odd))

    def chain1(i):
        @pl.when(i == 3)
        def _():
            stage(1, 1)

    pipeline(lambda i: wait_before(g1p, 2, i, inward), back0, sum0, chain1)
    sum0(NK - 1, (NK - 1) % 2)
    stage(0, 0)

    def norm0(i, odd):
        k = pick(inward, i)
        a = k * CH
        at = pl.ds(a, CH)
        gn[...] = mix_back(slot(gp, i, odd)[...], 0)
        norm_back(g0p, hid0.at[:, at], rc0.at[:, at], a)
        send_after(g0p, 3, i, k, inward)

    def norm0_pair(j):
        norm0(2 * j, 0)
        norm0(2 * j + 1, 1)

        @pl.when(j == 1)
        def _():
            stage(0, 1)

    rows_loop(0, NK // 2, norm0_pair)
    if NK % 2:
        norm0(NK - 1, 0)
    stage(1, 2)

    def tap_sums(k, moved, still, rev, lo, hi):
        def row(r):
            def go(a):
                for lanes in groups:
                    v = still[1 + r, pl.ds(1 + a, WIDE), :, lanes]
                    for p, prods in enumerate(products(moved, r, a, WIDE, lanes, lambda p, q: v)):
                        for q, prod in enumerate(prods):
                            add_taps(k, 3 * (2 - p) + 2 - q if rev else 3 * p + q, lanes, prod)

            chunks(go, WIDE)

        rows_loop(lo, hi, row)

    tap_sums(1, g1p, u1p, True, 0, R)
    tap_sums(0, u0p, g0p, False, 0, R // 2)
    stage(0, 2)
    tap_sums(0, u0p, g0p, False, R // 2, R)
    tap_stage(0)
    wait_all(g0p, 3)

    def out_copy(r):
        return pltpu.make_async_copy(raw.at[pl.ds(S * r, S)], out_hbm.at[0, pl.ds(S * r, S)], out_sem.at[r])

    def last(r):
        def go(a):
            for lanes in groups:
                s = conv(g0p, 0, r, a, WIDE, lanes, True) + g1[r, pl.ds(a, WIDE), :, lanes]
                row_buf[pl.ds(a, WIDE), :, lanes] = s

        chunks(go, WIDE)
        rows = jnp.dot(unperm[...], row_buf[...].reshape(M, C), preferred_element_type=F32).astype(BF16)
        raw[pl.ds(S * r, S)] = rows.reshape(S, S * A, C)
        out_copy(r).start()

    def last_step(r):
        last(r)

        @pl.when(r == R // 2)
        def _():
            stage(1, 3)

    rows_loop(0, R, last_step)
    tap_stage(1)
    stage(0, 3)
    stage(1, 4)
    stage(1, 5)
    tap_stage(2)
    stage(0, 4)
    stage(0, 5)
    finish([wgrad_copy(l) for l in range(2)])
    finish([out_copy(r) for r in range(R)])


def hand_over(pieces, *refs):
    srcs, dsts, mids, sem = refs[:3], refs[3:6], refs[6:9], refs[9]
    step = srcs[0].shape[1] // pieces
    parts = [tuple(ref.at[:, pl.ds(i * step, step)] for ref in (srcs[0], mids[0], dsts[0])) for i in range(pieces)]
    parts += [(srcs[j], mids[j], dsts[j]) for j in (2, 1)]
    loads = [pltpu.make_async_copy(a, b, sem.at[0, i]) for i, (a, b, _) in enumerate(parts)]
    stores = [pltpu.make_async_copy(b, c, sem.at[1, i]) for i, (_, b, c) in enumerate(parts)]
    for c in loads:
        c.start()
    for a, b in zip(loads, stores):
        a.wait()
        b.start()
    for c in stores:
        c.wait()


def body(inputs, cotangent, dw_kernel, pw_weight):
    _, rows, cols, C = inputs.shape
    n = lax.axis_size("lon")
    R, A, T, H = rows // S, cols // S, S * S, C // 2
    piece = H // n
    wire = BF16 if piece % 16 == 0 else F32
    samples = inputs.size // C * n * lax.axis_size("lat") * lax.axis_size("mem")
    anywhere = pl.BlockSpec(memory_space=pl.ANY)
    local = pl.BlockSpec(memory_space=pltpu.VMEM)
    padded = pltpu.VMEM((R + 2, A + 2, T, C), BF16)
    cells = pltpu.VMEM((R, A, T, C), BF16)
    CH = max(c for c in (1, 2, 4) if A % c == 0)
    chunk = pltpu.VMEM((R, CH, T, C), BF16)
    half = (A // CH + 1) // 2
    steps = pltpu.VMEM((half, R, CH, T, C), BF16)
    scoped = [
        padded, padded, padded, padded,
        cells, cells, cells,
        pltpu.VMEM((R, A, T, 128), F32),
        steps, steps,
        pltpu.VMEM((half, R, CH, T, 128), F32), pltpu.VMEM((half, R, CH, T, 128), F32),
        steps, steps,
        pltpu.VMEM((R, CH, T, C), F32),
        chunk,
        pltpu.VMEM((A, T, C), BF16),
        pltpu.VMEM((2, 9, T, C), BF16),
    ]
    scratch = [
        pltpu.VMEM((rows, cols, C), BF16),
        pltpu.VMEM((rows, cols, C), BF16),
        pltpu.VMEM((A * T, A * T), BF16),
        pltpu.VMEM((A * T, A * T), BF16),
        pltpu.VMEM((2, 9, 8, C), F32),
        pltpu.VMEM((2, C, C), F32),
        pltpu.VMEM((2, H, C), BF16), pltpu.VMEM((2, H, C), BF16),
        pltpu.VMEM((2, H, H), BF16), pltpu.VMEM((2, H, H), BF16),
        pltpu.VMEM((2, n, piece, H), wire), pltpu.VMEM((2, n, piece, H), wire),
        pltpu.VMEM((2, piece, H), wire), pltpu.VMEM((2, 2, n, piece, H), wire),
        pltpu.VMEM((2, 16, C), F32),
        pltpu.VMEM((2, 16, H), BF16), pltpu.VMEM((2, 16, H), BF16), pltpu.VMEM((3, 2, 16, H), BF16),
        pltpu.VMEM((2, 16, H), BF16), pltpu.VMEM((n, 2, 16, H), BF16),
        pltpu.VMEM((2, C, C), BF16), pltpu.VMEM((2, C, H), F32), pltpu.SemaphoreType.DMA((3,)),
        pltpu.SemaphoreType.DMA((2, R)), pltpu.SemaphoreType.DMA((R,)),
        pltpu.SemaphoreType.DMA((4, 4 + A // CH)), pltpu.SemaphoreType.DMA((4, 4 + A // CH)),
        pltpu.SemaphoreType.DMA((2, 5, 2 * n)), pltpu.SemaphoreType.DMA((2, 5, 2 * n)),
    ]
    made = pl.pallas_call(
        functools.partial(kernel, n, 1.0 / math.sqrt(samples), scoped),
        out_shape=(
            jax.ShapeDtypeStruct(inputs.shape, BF16),
            jax.ShapeDtypeStruct((9, 2, H), F32),
            jax.ShapeDtypeStruct((2, C, H), F32),
        ),
        in_specs=[anywhere, anywhere, local, anywhere],
        out_specs=(anywhere, local, anywhere),
        scratch_shapes=scratch,
        name="blocks",
        compiler_params=pltpu.CompilerParams(
            collective_id=0, has_side_effects=True, vmem_limit_bytes=60 * 1024 * 1024
        ),
    )(inputs, cotangent, jnp.transpose(dw_kernel, (1, 0, 2)), pw_weight)
    pieces = max(p for p in (1, 2, 3, 4, 6, 8) if rows % p == 0)
    out, kgrad, wgrad = pl.pallas_call(
        functools.partial(hand_over, pieces),
        out_shape=tuple(jax.ShapeDtypeStruct(v.shape, v.dtype) for v in made),
        in_specs=[anywhere] * 3,
        out_specs=(anywhere,) * 3,
        scratch_shapes=[*(pltpu.VMEM(v.shape, v.dtype) for v in made), pltpu.SemaphoreType.DMA((2, pieces + 2))],
        compiler_params=pltpu.CompilerParams(vmem_limit_bytes=60 * 1024 * 1024),
        name="hand_over",
    )(*made)
    return out, jnp.transpose(kgrad, (1, 0, 2)), wgrad


def solution(mesh):
    placed = (P("mem", "lat", "lon", None), P("mem", "lat", "lon", None), P(), P())
    return jax.shard_map(
        body,
        mesh=mesh,
        in_specs=placed,
        out_specs=(P("mem", "lat", "lon", None), P(None, None, "mem"), P(None, None, "mem")),
        check_vma=False,
    )
```

```python
import functools
import math

import jax
import jax.numpy as jnp
from jax import lax
from jax.experimental import pallas as pl
from jax.experimental.pallas import tpu as pltpu
from jax.sharding import PartitionSpec as P

S = 4
F32 = jnp.float32
BF16 = jnp.bfloat16
MESH = pl.DeviceIdType.MESH
ROOT = math.sqrt(2.0 / math.pi)
CUBE = 0.044715


def gelu_both(x):
    xx = x * x
    t = jnp.tanh(x * (ROOT + (ROOT * CUBE) * xx))
    h = 0.5 + 0.5 * t
    g = x * h
    return g, h + g * (1.0 - t) * (ROOT + (3.0 * ROOT * CUBE) * xx)


def kernel(n, factor, scoped, *refs):
    pl.run_scoped(lambda *inner: work(n, factor, *refs, *inner), *scoped)


def work(
    n, factor,
    x_hbm, cot_hbm, dw_ref, w_hbm,
    out_hbm, kgrad, wgrad,
    raw, cotraw, perm, unperm, kacc, wacc,
    w0s, w0r, w1s, w1r, w2s, w2r, w3s, w3r, kv, kown, koth, kin, ks2, kr2,
    w_ref, wg, io_sem,
    in_sem, out_sem, rim_s, rim_r, red_s, red_r,
    u0p, u1p, g1p, g0p, g1, hid0, d0, rc0, hid1_0, hid1_1, rc1_0, rc1_1, gp_0, gp_1, pre, gn, row_buf, kb,
):
    R, A, T, C = hid0.shape
    M = A * T
    H = C // 2
    CH = gn.shape[1]
    NK = A // CH
    MC = R * CH * T
    WIDE = max(c for c in (1, 2, 4, 7) if A % c == 0)
    groups = [slice(g, g + 128) for g in range(0, C, 128)]
    me, lat, mem = lax.axis_index("lon"), lax.axis_index("lat"), lax.axis_index("mem")
    other, omem = 1 - lat, 1 - mem
    pair = me + 1 - 2 * (me % 2)

    def lon_at(d):
        return lax.rem(me + (d % n), n)

    def dev(lon_i, lat_i, mem_i):
        return {"lon": lon_i, "lat": lat_i, "mem": mem_i}

    def planned(src, dst, ssem, rsem, where):
        return pltpu.make_async_remote_copy(
            src_ref=src, dst_ref=dst, send_sem=ssem, recv_sem=rsem, device_id=where, device_id_type=MESH
        )

    def in_copy(i, r):
        src, dst = ((x_hbm, raw), (cot_hbm, cotraw))[i]
        return pltpu.make_async_copy(src.at[0, pl.ds(S * r, S)], dst.at[pl.ds(S * r, S)], in_sem.at[i, r])

    for i in range(2):
        for r in range(R):
            in_copy(i, r).start()
    w_copy = pltpu.make_async_copy(w_hbm, w_ref, io_sem.at[0])
    w_copy.start()

    barrier = pltpu.get_barrier_semaphore()
    for d in range(n):
        for la in (lat, other):
            if d == 0 and la is lat:
                continue
            pl.semaphore_signal(barrier, inc=1, device_id=dev(lon_at(d), la, mem), device_id_type=MESH)
    for lon_i in (me, pair):
        for la in (lat, other):
            pl.semaphore_signal(barrier, inc=1, device_id=dev(lon_i, la, omem), device_id_type=MESH)

    def one_hot(rows_dim):
        o = lax.broadcasted_iota(jnp.int32, (M, M), rows_dim)
        i = lax.broadcasted_iota(jnp.int32, (M, M), 1 - rows_dim)
        a, s, b = o >> 4, (o >> 2) & 3, o & 3
        return jnp.where(i == s * (A * S) + a * S + b, 1.0, 0.0).astype(BF16)

    perm[...] = one_hot(0)
    unperm[...] = one_hot(1)
    for t in range(9):
        taps_f = dw_ref[t].astype(F32)
        for l in range(2):
            kb[l, t] = jnp.broadcast_to(taps_f[l : l + 1, :], (T, C)).astype(BF16)
    kacc[...] = jnp.zeros_like(kacc)
    kv[...] = jnp.zeros_like(kv)
    edge = lat * (R + 1)
    for ref in (u0p, u1p, g1p, g0p):
        ref[edge] = jnp.zeros(ref.shape[1:], BF16)

    def rows_loop(lo, hi, fn):
        def step(r, c):
            fn(r)
            return c

        lax.fori_loop(lo, hi, step, 0)

    def regroup(src, r):
        rows = src[pl.ds(S * r, S)].reshape(M, C)
        return jnp.dot(perm[...], rows, preferred_element_type=F32).astype(BF16).reshape(A, T, C)

    wacc[...] = jnp.zeros_like(wacc)

    def load0(r):
        in_copy(0, r).wait()
        u0p[1 + r, 1 : A + 1] = regroup(raw, r)

    rows_loop(0, R, load0)

    pl.semaphore_wait(barrier, 2 * n + 3)

    right, left = lon_at(1), lon_at(-1)

    def rim(ref, e, i, src, dst, where):
        return planned(ref.at[src], ref.at[dst], rim_s.at[e, i], rim_r.at[e, i], where)

    seam = R - lat * (R - 1)
    inner = pl.ds(1, R)

    def rim_right(ref, e):
        last, first = pl.ds(A, 1), pl.ds(0, 1)
        return [
            rim(ref, e, 0, (inner, last), (inner, first), dev(right, lat, mem)),
            rim(ref, e, 2, (seam, last), (edge, first), dev(right, other, mem)),
        ]

    def rim_left(ref, e):
        first, last = pl.ds(1, 1), pl.ds(A + 1, 1)
        return [
            rim(ref, e, 1, (inner, first), (inner, last), dev(left, lat, mem)),
            rim(ref, e, 3, (seam, first), (edge, last), dev(left, other, mem)),
        ]

    def rim_lat(ref, e, k):
        at = pl.ds(1 + k * CH, CH)
        return [rim(ref, e, 4 + k, (seam, at), (edge, at), dev(me, other, mem))]

    def rim_lat_all(ref, e):
        at = pl.ds(1, A)
        return [rim(ref, e, 4, (seam, at), (edge, at), dev(me, other, mem))]

    def interior_first(m):
        return [*range(1, 1 + m), NK - 1, 0, *range(1 + m, NK - 1)]

    def pick(order, i):
        return sum(k * ((i + NK - j) // NK - (i + NK - j - 1) // NK) for j, k in enumerate(order))

    def send_after(ref, e, i, k, order):
        start(rim_lat(ref, e, k))

        @pl.when(i == order.index(NK - 1))
        def _():
            start(rim_right(ref, e))

        @pl.when(i == order.index(0))
        def _():
            start(rim_left(ref, e))

    def wait_before(ref, e, i, order):
        done = set()
        for j, k in enumerate(order):
            need = [p for p in (k - 1, k, k + 1) if 0 <= p < NK and p not in done]
            done.update(need)
            if e == 0:
                need = [0] if j == 0 else []
            if not need and 0 < k < NK - 1:
                continue

            @pl.when(i == j)
            def _(k=k, need=need):
                for p in need:
                    finish(rim_lat(ref, e, p) if e else rim_lat_all(ref, e))
                if k == NK - 1:
                    finish(rim_left(ref, e))
                if k == 0:
                    finish(rim_right(ref, e))

    def wait_all(ref, e):
        for k in range(NK):
            finish(rim_lat(ref, e, k))
        finish(rim_left(ref, e) + rim_right(ref, e))

    def start(copies):
        for c in copies:
            c.start()

    def finish(copies):
        for c in copies:
            c.wait()

    def products(ref, r, a, ch, lanes, other_factor):
        for p in range(3):
            row = ref[r + p, pl.ds(a, ch + 2), :, lanes]
            yield [row[q : q + ch] * other_factor(p, q) for q in range(3)]

    def conv(ref, l, r, a, ch, lanes, rev):
        def tap(p, q):
            return kb[l, 3 * (2 - p) + 2 - q if rev else 3 * p + q, :, lanes]

        s0, s1, s2 = [v[0] + v[1] + v[2] for v in products(ref, r, a, ch, lanes, tap)]
        return s0 + s1 + s2

    def chunks(fn, ch, unroll=False):
        def step(i, c):
            fn(i * ch)
            return c

        lax.fori_loop(0, A // ch, step, 0, unroll=unroll)

    def each_row(fn):
        def step(r, c):
            fn(r)
            return c

        lax.fori_loop(0, R, step, 0, unroll=True)

    def tree(v):
        v = [v[i] for i in range(v.shape[0])]
        while len(v) > 1:
            v = [a + b for a, b in zip(v[::2], v[1::2])] + v[len(v) - len(v) % 2 :]
        return v[0]

    def add_taps(k, t, lanes, prod):
        both = tree(prod).astype(F32).reshape(2, 8, 128)
        kacc[k, t, :, lanes] += both[0] + both[1]

    def lane_mean(v, ch):
        m = jnp.sum(v.astype(F32), axis=-1, keepdims=True) * (1.0 / C)
        return jnp.broadcast_to(m, (ch, T, 128))

    def conv_norm(src, l, a, hid, rc):
        def go(r):
            convs = [conv(src, l, r, a, CH, lanes, False) for lanes in groups]
            c0, c1, c2, c3 = [c * c for c in convs]
            recip = lax.rsqrt(lane_mean((c0 + c1) + (c2 + c3), CH) + 1e-6)
            rc[r] = recip
            for lanes, c in zip(groups, convs):
                hid[r, :, :, lanes] = (c.astype(F32) * recip).astype(BF16)

        each_row(go)

    def mix(v, l):
        return jnp.dot(v.reshape(MC, C), w_ref[l], preferred_element_type=F32).reshape(R, CH, T, C)

    def mix_back(v, l):
        return lax.dot_general(
            v.reshape(MC, C), w_ref[l], (((1,), (1,)), ((), ())), preferred_element_type=F32
        ).astype(BF16).reshape(R, CH, T, C)

    def norm_back(dst, hid, rc, a):
        def go(r):
            ns = [hid[r, :, :, lanes] for lanes in groups]
            gs = [gn[r, :, :, lanes] for lanes in groups]
            d0_, d1_, d2_, d3_ = [g * v for g, v in zip(gs, ns)]
            mean = lane_mean((d0_ + d1_) + (d2_ + d3_), CH)
            recip = rc[r]
            for lanes, g, v in zip(groups, gs, ns):
                back = recip * (g.astype(F32) - v.astype(F32) * mean)
                dst[1 + r, pl.ds(1 + a, CH), :, lanes] = back.astype(BF16)

        each_row(go)

    def weight_sum(l, hid, gp):
        wacc[l] += lax.dot_general(
            hid[...].reshape(MC, C), gp[...].reshape(MC, C), (((0,), (0,)), ((), ())), preferred_element_type=F32
        )

    def slot(pair, i, odd):
        return pair[odd].at[i // 2]

    def pipeline(before, first, second, after):
        before(0)
        first(0, 0)

        def both(i, odd):
            before(i)
            second(i - 1, 1 - odd)
            first(i, odd)
            after(i - 1)

        def step(j, c):
            both(2 * j + 1, 1)
            both(2 * j + 2, 0)
            return c

        lax.fori_loop(0, (NK - 1) // 2, step, 0)
        if NK % 2 == 0:
            both(NK - 1, 1)

    own_rows = pl.ds(pl.multiple_of(lat * H, H), H)
    other_rows = pl.ds(pl.multiple_of(other * H, H), H)
    own_cols = pl.ds(pl.multiple_of(mem * H, H), H)
    other_cols = pl.ds(pl.multiple_of(omem * H, H), H)
    piece = H // n
    wire = w2s.dtype

    def red(l, stage, i, src, dst, where):
        return planned(src, dst, red_s.at[l, stage, i], red_r.at[l, stage, i], where)

    def plan(l, stage):
        if stage == 0:
            return [red(l, 0, 0, w0s.at[l], w0r.at[l], dev(me, other, mem))]
        if stage == 1:
            return [red(l, 1, 0, w1s.at[l], w1r.at[l], dev(me, lat, omem))]
        if stage == 2:
            return [
                red(l, 2, d, w2s.at[l, lon_at(d)], w2r.at[l, me], dev(lon_at(d), lat, mem)) for d in range(1, n)
            ]
        if stage == 3:
            return [red(l, 3, d, w3s.at[l], w3r.at[l, lat, me], dev(lon_at(d), lat, mem)) for d in range(1, n)]
        return [red(l, 4, 0, w3r.at[l, lat], w3r.at[l, lat], dev(me, other, mem))]

    def wgrad_copy(l):
        return pltpu.make_async_copy(wg.at[l], wgrad.at[l], io_sem.at[1 + l])

    def stage(l, step):
        if step:
            finish(plan(l, step - 1))
        if step == 0:
            w0s[l] = wacc[l, other_rows, :].astype(BF16)
        elif step == 1:
            wacc[l, own_rows, :] += w0r[l].astype(F32)
            w1s[l] = wacc[l, own_rows, other_cols].astype(BF16)
        elif step == 2:
            total = wacc[l, own_rows, own_cols] + w1r[l].astype(F32)
            wacc[l, own_rows, own_cols] = total
            w2s[l] = total.reshape(n, piece, H).astype(wire)
        elif step == 3:
            at = pl.multiple_of(lat * H + me * piece, piece)
            total = wacc[l, pl.ds(at, piece), own_cols]
            for d in range(1, n):
                total = total + w2r[l, lon_at(d)].astype(F32)
            done = (total * factor).astype(wire)
            w3s[l] = done
            w3r[l, lat, me] = done
        elif step == 5:
            wg[l] = w3r[l].reshape(C, H).astype(F32)
            start([wgrad_copy(l)])
            return
        start(plan(l, step))

    def tap_plan(step):
        if step == 0:
            near = [(lon_i, la, mm) for lon_i in (me, pair) for la in (lat, other) for mm in (mem, omem)]
            return [
                red(0, 0, j, koth if j % 2 else kown, kin.at[j - 1], dev(*near[j])) for j in range(1, 8)
            ]
        return [red(0, 2, n + d, ks2, kr2.at[me // 2], dev(lon_at(2 * d), lat, mem)) for d in range(1, n // 2)]

    def tap_stage(step):
        if step:
            finish(tap_plan(step - 1))
        if step == 0:
            for k in range(2):
                for t in range(9):
                    kv[k, t : t + 1, :] = jnp.sum(kacc[k, t], axis=0, keepdims=True)
            kown[...] = kv[:, :, own_cols].astype(BF16)
            koth[...] = kv[:, :, other_cols].astype(BF16)
        elif step == 1:
            total = kv[:, :, own_cols]
            for j in range(7):
                total = total + kin[j].astype(F32)
            both = total.astype(BF16)
            ks2[...] = both
            kr2[me // 2] = both
        else:
            ks = kr2[0].astype(F32)
            for j in range(1, n // 2):
                ks = ks + kr2[j].astype(F32)
            for k in range(2):
                kgrad[:, k, :] = ks[k, :9, :] * factor
            return
        start(tap_plan(step))

    rims0 = rim_lat_all(u0p, 0) + rim_right(u0p, 0) + rim_left(u0p, 0)
    start(rims0)

    def load1(r):
        in_copy(1, r).wait()
        g1[r] = regroup(cotraw, r)

    rows_loop(0, R, load1)
    w_copy.wait()
    early, mixed, inward = [interior_first(min(m, NK - 2)) for m in (4, 3, NK - 2)]

    def block0(i):
        wait_before(u0p, 0, i, early)
        k = pick(early, i)
        a = k * CH
        at = pl.ds(a, CH)
        conv_norm(u0p, 0, a, hid0.at[:, at], rc0.at[:, at])
        pre[...] = mix(hid0[:, at], 0)

        def go(r):
            for lanes in groups:
                gel, slope = gelu_both(pre[r, :, :, lanes])
                d0[r, at, :, lanes] = slope.astype(BF16)
                u = u0p[1 + r, pl.ds(1 + a, CH), :, lanes]
                u1p[1 + r, pl.ds(1 + a, CH), :, lanes] = u + gel.astype(BF16)

        each_row(go)
        send_after(u1p, 1, i, k, early)

    rows_loop(0, NK, block0)

    hid1, rc1, gp = (hid1_0, hid1_1), (rc1_0, rc1_1), (gp_0, gp_1)

    def block1(i, odd):
        k = pick(mixed, i)
        a = k * CH
        at = pl.ds(a, CH)
        hid, out = slot(hid1, i, odd), slot(gp, i, odd)
        conv_norm(u1p, 1, a, hid, slot(rc1, i, odd))
        pre[...] = mix(hid[...], 1)

        def go(r):
            for lanes in groups:
                slope = gelu_both(pre[r, :, :, lanes])[1]
                g = g1[r, at, :, lanes].astype(F32)
                out[r, :, :, lanes] = (g * slope).astype(BF16)

        each_row(go)
        weight_sum(1, hid, out)

    def back1(i, odd):
        gn[...] = mix_back(slot(gp, i, odd)[...], 1)
        norm_back(g1p, slot(hid1, i, odd), slot(rc1, i, odd), pick(mixed, i) * CH)

    def send1(i):
        send_after(g1p, 2, i, pick(mixed, i), mixed)

    pipeline(lambda i: wait_before(u1p, 1, i, mixed), block1, back1, send1)
    stage(1, 0)
    back1(NK - 1, (NK - 1) % 2)
    send1(NK - 1)

    def back0(i, odd):
        a = pick(inward, i) * CH
        at = pl.ds(a, CH)
        out = slot(gp, i, odd)

        def go(r):
            for lanes in groups:
                s = conv(g1p, 1, r, a, CH, lanes, True) + g1[r, at, :, lanes]
                g1[r, at, :, lanes] = s
                out[r, :, :, lanes] = s * d0[r, at, :, lanes]

        each_row(go)

    def sum0(i, odd):
        weight_sum(0, hid0.at[:, pl.ds(pick(inward, i) * CH, CH)], slot(gp, i, odd))

    def chain1(i):
        @pl.when(i == 1)
        def _():
            stage(1, 1)

    pipeline(lambda i: wait_before(g1p, 2, i, inward), back0, sum0, chain1)
    sum0(NK - 1, (NK - 1) % 2)
    stage(0, 0)

    def norm0(i, odd):
        k = pick(inward, i)
        a = k * CH
        at = pl.ds(a, CH)
        gn[...] = mix_back(slot(gp, i, odd)[...], 0)
        norm_back(g0p, hid0.at[:, at], rc0.at[:, at], a)
        send_after(g0p, 3, i, k, inward)

    def norm0_pair(j):
        norm0(2 * j, 0)
        norm0(2 * j + 1, 1)

        @pl.when(j == 1)
        def _():
            stage(0, 1)

        @pl.when(j == NK // 2 - 1)
        def _():
            stage(1, 2)

    rows_loop(0, NK // 2, norm0_pair)
    if NK % 2:
        norm0(NK - 1, 0)

    def tap_sums(k, moved, still, rev, lo, hi):
        def row(r):
            def go(a):
                for lanes in groups:
                    v = still[1 + r, pl.ds(1 + a, WIDE), :, lanes]
                    for p, prods in enumerate(products(moved, r, a, WIDE, lanes, lambda p, q: v)):
                        for q, prod in enumerate(prods):
                            add_taps(k, 3 * (2 - p) + 2 - q if rev else 3 * p + q, lanes, prod)

            chunks(go, WIDE)

        rows_loop(lo, hi, row)

    tap_sums(1, g1p, u1p, True, 0, R)
    tap_sums(0, u0p, g0p, False, 0, R // 2)
    stage(0, 2)
    tap_sums(0, u0p, g0p, False, R // 2, R)
    tap_stage(0)
    wait_all(g0p, 3)

    def out_copy(r):
        return pltpu.make_async_copy(raw.at[pl.ds(S * r, S)], out_hbm.at[0, pl.ds(S * r, S)], out_sem.at[r])

    def last(r):
        def go(a):
            for lanes in groups:
                s = conv(g0p, 0, r, a, WIDE, lanes, True) + g1[r, pl.ds(a, WIDE), :, lanes]
                row_buf[pl.ds(a, WIDE), :, lanes] = s

        chunks(go, WIDE)
        rows = jnp.dot(unperm[...], row_buf[...].reshape(M, C), preferred_element_type=F32).astype(BF16)
        raw[pl.ds(S * r, S)] = rows.reshape(S, S * A, C)
        out_copy(r).start()

    def last_step(r):
        last(r)

        @pl.when(r == 0)
        def _():
            stage(1, 3)

    rows_loop(0, R, last_step)
    tap_stage(1)
    stage(0, 3)
    stage(1, 4)
    stage(1, 5)
    tap_stage(2)
    stage(0, 4)
    stage(0, 5)
    finish([wgrad_copy(l) for l in range(2)])
    finish([out_copy(r) for r in range(R)])


def hand_over(pieces, *refs):
    srcs, dsts, mids, sem = refs[:3], refs[3:6], refs[6:9], refs[9]
    step = srcs[0].shape[1] // pieces
    parts = [tuple(ref.at[:, pl.ds(i * step, step)] for ref in (srcs[0], mids[0], dsts[0])) for i in range(pieces)]
    parts += [(srcs[j], mids[j], dsts[j]) for j in (2, 1)]
    loads = [pltpu.make_async_copy(a, b, sem.at[0, i]) for i, (a, b, _) in enumerate(parts)]
    stores = [pltpu.make_async_copy(b, c, sem.at[1, i]) for i, (_, b, c) in enumerate(parts)]
    for c in loads:
        c.start()
    for a, b in zip(loads, stores):
        a.wait()
        b.start()
    for c in stores:
        c.wait()


def body(inputs, cotangent, dw_kernel, pw_weight):
    _, rows, cols, C = inputs.shape
    n = lax.axis_size("lon")
    R, A, T, H = rows // S, cols // S, S * S, C // 2
    piece = H // n
    wire = BF16 if piece % 16 == 0 else F32
    samples = inputs.size // C * n * lax.axis_size("lat") * lax.axis_size("mem")
    anywhere = pl.BlockSpec(memory_space=pl.ANY)
    local = pl.BlockSpec(memory_space=pltpu.VMEM)
    padded = pltpu.VMEM((R + 2, A + 2, T, C), BF16)
    cells = pltpu.VMEM((R, A, T, C), BF16)
    CH = max(c for c in (1, 2, 4) if A % c == 0)
    chunk = pltpu.VMEM((R, CH, T, C), BF16)
    half = (A // CH + 1) // 2
    steps = pltpu.VMEM((half, R, CH, T, C), BF16)
    scoped = [
        padded, padded, padded, padded,
        cells, cells, cells,
        pltpu.VMEM((R, A, T, 128), F32),
        steps, steps,
        pltpu.VMEM((half, R, CH, T, 128), F32), pltpu.VMEM((half, R, CH, T, 128), F32),
        steps, steps,
        pltpu.VMEM((R, CH, T, C), F32),
        chunk,
        pltpu.VMEM((A, T, C), BF16),
        pltpu.VMEM((2, 9, T, C), BF16),
    ]
    scratch = [
        pltpu.VMEM((rows, cols, C), BF16),
        pltpu.VMEM((rows, cols, C), BF16),
        pltpu.VMEM((A * T, A * T), BF16),
        pltpu.VMEM((A * T, A * T), BF16),
        pltpu.VMEM((2, 9, 8, C), F32),
        pltpu.VMEM((2, C, C), F32),
        pltpu.VMEM((2, H, C), BF16), pltpu.VMEM((2, H, C), BF16),
        pltpu.VMEM((2, H, H), BF16), pltpu.VMEM((2, H, H), BF16),
        pltpu.VMEM((2, n, piece, H), wire), pltpu.VMEM((2, n, piece, H), wire),
        pltpu.VMEM((2, piece, H), wire), pltpu.VMEM((2, 2, n, piece, H), wire),
        pltpu.VMEM((2, 16, C), F32),
        pltpu.VMEM((2, 16, H), BF16), pltpu.VMEM((2, 16, H), BF16), pltpu.VMEM((7, 2, 16, H), BF16),
        pltpu.VMEM((2, 16, H), BF16), pltpu.VMEM((n // 2, 2, 16, H), BF16),
        pltpu.VMEM((2, C, C), BF16), pltpu.VMEM((2, C, H), F32), pltpu.SemaphoreType.DMA((3,)),
        pltpu.SemaphoreType.DMA((2, R)), pltpu.SemaphoreType.DMA((R,)),
        pltpu.SemaphoreType.DMA((4, 4 + A // CH)), pltpu.SemaphoreType.DMA((4, 4 + A // CH)),
        pltpu.SemaphoreType.DMA((2, 5, 2 * n)), pltpu.SemaphoreType.DMA((2, 5, 2 * n)),
    ]
    made = pl.pallas_call(
        functools.partial(kernel, n, 1.0 / math.sqrt(samples), scoped),
        out_shape=(
            jax.ShapeDtypeStruct(inputs.shape, BF16),
            jax.ShapeDtypeStruct((9, 2, H), F32),
            jax.ShapeDtypeStruct((2, C, H), F32),
        ),
        in_specs=[anywhere, anywhere, local, anywhere],
        out_specs=(anywhere, local, anywhere),
        scratch_shapes=scratch,
        name="blocks",
        compiler_params=pltpu.CompilerParams(
            collective_id=0, has_side_effects=True, vmem_limit_bytes=60 * 1024 * 1024
        ),
    )(inputs, cotangent, jnp.transpose(dw_kernel, (1, 0, 2)), pw_weight)
    pieces = max(p for p in (1, 2, 3, 4, 6, 8) if rows % p == 0)
    out, kgrad, wgrad = pl.pallas_call(
        functools.partial(hand_over, pieces),
        out_shape=tuple(jax.ShapeDtypeStruct(v.shape, v.dtype) for v in made),
        in_specs=[anywhere] * 3,
        out_specs=(anywhere,) * 3,
        scratch_shapes=[*(pltpu.VMEM(v.shape, v.dtype) for v in made), pltpu.SemaphoreType.DMA((2, pieces + 2))],
        compiler_params=pltpu.CompilerParams(vmem_limit_bytes=60 * 1024 * 1024),
        name="hand_over",
    )(*made)
    return out, jnp.transpose(kgrad, (1, 0, 2)), wgrad


def solution(mesh):
    placed = (P("mem", "lat", "lon", None), P("mem", "lat", "lon", None), P(), P())
    return jax.shard_map(
        body,
        mesh=mesh,
        in_specs=placed,
        out_specs=(P("mem", "lat", "lon", None), P(None, None, "mem"), P(None, None, "mem")),
        check_vma=False,
    )
```

```python
import functools
import math

import jax
import jax.numpy as jnp
from jax import lax
from jax.experimental import pallas as pl
from jax.experimental.pallas import tpu as pltpu
from jax.sharding import PartitionSpec as P

S = 4
F32 = jnp.float32
BF16 = jnp.bfloat16
MESH = pl.DeviceIdType.MESH
ROOT = math.sqrt(2.0 / math.pi)
CUBE = 0.044715


def gelu_both(x):
    xx = x * x
    t = jnp.tanh(x * (ROOT + (ROOT * CUBE) * xx))
    h = 0.5 + 0.5 * t
    g = x * h
    return g, h + g * (1.0 - t) * (ROOT + (3.0 * ROOT * CUBE) * xx)


def kernel(n, factor, scoped, *refs):
    pl.run_scoped(lambda *inner: work(n, factor, *refs, *inner), *scoped)


def work(
    n, factor,
    x_hbm, cot_hbm, dw_ref, w_hbm,
    out_hbm, kgrad, wgrad,
    raw, cotraw, perm, unperm, kacc, wacc,
    w0s, w0r, w1s, w1r, w2s, w2r, w3s, w3r, kv, kown, koth, kin, ks2, kr2,
    w_ref, wg, io_sem,
    in_sem, out_sem, rim_s, rim_r, red_s, red_r,
    u0p, u1p, g1p, g0p, g1, hid0, d0, rc0, hid1_0, hid1_1, rc1_0, rc1_1, gp_0, gp_1, pre, gn, row_buf, kb,
):
    R, A, T, C = hid0.shape
    M = A * T
    H = C // 2
    CH = gn.shape[1]
    NK = A // CH
    MC = R * CH * T
    WIDE = max(c for c in (1, 2, 4, 7) if A % c == 0)
    groups = [slice(g, g + 128) for g in range(0, C, 128)]
    me, lat, mem = lax.axis_index("lon"), lax.axis_index("lat"), lax.axis_index("mem")
    other, omem = 1 - lat, 1 - mem
    pair = me + 1 - 2 * (me % 2)

    def lon_at(d):
        return lax.rem(me + (d % n), n)

    def dev(lon_i, lat_i, mem_i):
        return {"lon": lon_i, "lat": lat_i, "mem": mem_i}

    def planned(src, dst, ssem, rsem, where):
        return pltpu.make_async_remote_copy(
            src_ref=src, dst_ref=dst, send_sem=ssem, recv_sem=rsem, device_id=where, device_id_type=MESH
        )

    def in_copy(i, r):
        src, dst = ((x_hbm, raw), (cot_hbm, cotraw))[i]
        return pltpu.make_async_copy(src.at[0, pl.ds(S * r, S)], dst.at[pl.ds(S * r, S)], in_sem.at[i, r])

    for i in range(2):
        for r in range(R):
            in_copy(i, r).start()
    w_copy = pltpu.make_async_copy(w_hbm, w_ref, io_sem.at[0])
    w_copy.start()

    barrier = pltpu.get_barrier_semaphore()
    for d in range(n):
        for la in (lat, other):
            if d == 0 and la is lat:
                continue
            pl.semaphore_signal(barrier, inc=1, device_id=dev(lon_at(d), la, mem), device_id_type=MESH)
    for lon_i in (me, pair):
        for la in (lat, other):
            pl.semaphore_signal(barrier, inc=1, device_id=dev(lon_i, la, omem), device_id_type=MESH)

    def one_hot(rows_dim):
        o = lax.broadcasted_iota(jnp.int32, (M, M), rows_dim)
        i = lax.broadcasted_iota(jnp.int32, (M, M), 1 - rows_dim)
        a, s, b = o >> 4, (o >> 2) & 3, o & 3
        return jnp.where(i == s * (A * S) + a * S + b, 1.0, 0.0).astype(BF16)

    perm[...] = one_hot(0)
    unperm[...] = one_hot(1)
    for t in range(9):
        taps_f = dw_ref[t].astype(F32)
        for l in range(2):
            kb[l, t] = jnp.broadcast_to(taps_f[l : l + 1, :], (T, C)).astype(BF16)
    kacc[...] = jnp.zeros_like(kacc)
    kv[...] = jnp.zeros_like(kv)
    edge = lat * (R + 1)
    for ref in (u0p, u1p, g1p, g0p):
        ref[edge] = jnp.zeros(ref.shape[1:], BF16)

    def rows_loop(lo, hi, fn):
        def step(r, c):
            fn(r)
            return c

        lax.fori_loop(lo, hi, step, 0)

    def regroup(src, r):
        rows = src[pl.ds(S * r, S)].reshape(M, C)
        return jnp.dot(perm[...], rows, preferred_element_type=F32).astype(BF16).reshape(A, T, C)


    def load0(r):
        in_copy(0, r).wait()
        u0p[1 + r, 1 : A + 1] = regroup(raw, r)

    rows_loop(0, R, load0)

    pl.semaphore_wait(barrier, 2 * n + 3)

    right, left = lon_at(1), lon_at(-1)

    def rim(ref, e, i, src, dst, where):
        return planned(ref.at[src], ref.at[dst], rim_s.at[e, i], rim_r.at[e, i], where)

    seam = R - lat * (R - 1)
    inner = pl.ds(1, R)

    def rim_right(ref, e):
        last, first = pl.ds(A, 1), pl.ds(0, 1)
        return [
            rim(ref, e, 0, (inner, last), (inner, first), dev(right, lat, mem)),
            rim(ref, e, 2, (seam, last), (edge, first), dev(right, other, mem)),
        ]

    def rim_left(ref, e):
        first, last = pl.ds(1, 1), pl.ds(A + 1, 1)
        return [
            rim(ref, e, 1, (inner, first), (inner, last), dev(left, lat, mem)),
            rim(ref, e, 3, (seam, first), (edge, last), dev(left, other, mem)),
        ]

    def rim_lat(ref, e, k):
        at = pl.ds(1 + k * CH, CH)
        return [rim(ref, e, 4 + k, (seam, at), (edge, at), dev(me, other, mem))]

    def rim_lat_all(ref, e):
        at = pl.ds(1, A)
        return [rim(ref, e, 4, (seam, at), (edge, at), dev(me, other, mem))]

    def interior_first(m):
        return [*range(1, 1 + m), NK - 1, 0, *range(1 + m, NK - 1)]

    def pick(order, i):
        return sum(k * ((i + NK - j) // NK - (i + NK - j - 1) // NK) for j, k in enumerate(order))

    def send_after(ref, e, i, k, order):
        start(rim_lat(ref, e, k))

        @pl.when(i == order.index(NK - 1))
        def _():
            start(rim_right(ref, e))

        @pl.when(i == order.index(0))
        def _():
            start(rim_left(ref, e))

    def wait_before(ref, e, i, order):
        done = set()
        for j, k in enumerate(order):
            need = [p for p in (k - 1, k, k + 1) if 0 <= p < NK and p not in done]
            done.update(need)
            if e == 0:
                need = [0] if j == 0 else []
            if not need and 0 < k < NK - 1:
                continue

            @pl.when(i == j)
            def _(k=k, need=need):
                for p in need:
                    finish(rim_lat(ref, e, p) if e else rim_lat_all(ref, e))
                if k == NK - 1:
                    finish(rim_left(ref, e))
                if k == 0:
                    finish(rim_right(ref, e))

    def wait_all(ref, e):
        for k in range(NK):
            finish(rim_lat(ref, e, k))
        finish(rim_left(ref, e) + rim_right(ref, e))

    def start(copies):
        for c in copies:
            c.start()

    def finish(copies):
        for c in copies:
            c.wait()

    def products(ref, r, a, ch, lanes, other_factor):
        for p in range(3):
            row = ref[r + p, pl.ds(a, ch + 2), :, lanes]
            yield [row[q : q + ch] * other_factor(p, q) for q in range(3)]

    def conv(ref, l, r, a, ch, lanes, rev):
        def tap(p, q):
            return kb[l, 3 * (2 - p) + 2 - q if rev else 3 * p + q, :, lanes]

        s0, s1, s2 = [v[0] + v[1] + v[2] for v in products(ref, r, a, ch, lanes, tap)]
        return s0 + s1 + s2

    def chunks(fn, ch, unroll=False):
        def step(i, c):
            fn(i * ch)
            return c

        lax.fori_loop(0, A // ch, step, 0, unroll=unroll)

    def each_row(fn):
        def step(r, c):
            fn(r)
            return c

        lax.fori_loop(0, R, step, 0, unroll=True)

    def tree(v):
        v = [v[i] for i in range(v.shape[0])]
        while len(v) > 1:
            v = [a + b for a, b in zip(v[::2], v[1::2])] + v[len(v) - len(v) % 2 :]
        return v[0]

    def add_taps(k, t, lanes, prod):
        both = tree(prod).astype(F32).reshape(2, 8, 128)
        kacc[k, t, :, lanes] += both[0] + both[1]

    def lane_mean(v, ch):
        m = jnp.sum(v.astype(F32), axis=-1, keepdims=True) * (1.0 / C)
        return jnp.broadcast_to(m, (ch, T, 128))

    def conv_norm(src, l, a, hid, rc):
        def go(r):
            convs = [conv(src, l, r, a, CH, lanes, False) for lanes in groups]
            c0, c1, c2, c3 = [c * c for c in convs]
            recip = lax.rsqrt(lane_mean((c0 + c1) + (c2 + c3), CH) + 1e-6)
            rc[r] = recip
            for lanes, c in zip(groups, convs):
                hid[r, :, :, lanes] = (c.astype(F32) * recip).astype(BF16)

        each_row(go)

    def mix(v, l):
        return jnp.dot(v.reshape(MC, C), w_ref[l], preferred_element_type=F32).reshape(R, CH, T, C)

    def mix_back(v, l):
        return lax.dot_general(
            v.reshape(MC, C), w_ref[l], (((1,), (1,)), ((), ())), preferred_element_type=F32
        ).astype(BF16).reshape(R, CH, T, C)

    def norm_back(dst, hid, rc, a):
        def go(r):
            ns = [hid[r, :, :, lanes] for lanes in groups]
            gs = [gn[r, :, :, lanes] for lanes in groups]
            d0_, d1_, d2_, d3_ = [g * v for g, v in zip(gs, ns)]
            mean = lane_mean((d0_ + d1_) + (d2_ + d3_), CH)
            recip = rc[r]
            for lanes, g, v in zip(groups, gs, ns):
                back = recip * (g.astype(F32) - v.astype(F32) * mean)
                dst[1 + r, pl.ds(1 + a, CH), :, lanes] = back.astype(BF16)

        each_row(go)

    def weight_sum(l, hid_of):
        for odd in range(2):
            count = (NK + 1 - odd) // 2
            grads = gp[odd][:count].reshape(count * MC, C)
            part = lax.dot_general(
                hid_of(odd, count), grads, (((0,), (0,)), ((), ())), preferred_element_type=F32
            )
            wacc[l] = wacc[l] + part if odd else part

    def slot(pair, i, odd):
        return pair[odd].at[i // 2]

    def pipeline(before, first, second, after):
        before(0)
        first(0, 0)

        def both(i, odd):
            before(i)
            second(i - 1, 1 - odd)
            first(i, odd)
            after(i - 1)

        def step(j, c):
            both(2 * j + 1, 1)
            both(2 * j + 2, 0)
            return c

        lax.fori_loop(0, (NK - 1) // 2, step, 0)
        if NK % 2 == 0:
            both(NK - 1, 1)

    own_rows = pl.ds(pl.multiple_of(lat * H, H), H)
    other_rows = pl.ds(pl.multiple_of(other * H, H), H)
    own_cols = pl.ds(pl.multiple_of(mem * H, H), H)
    other_cols = pl.ds(pl.multiple_of(omem * H, H), H)
    piece = H // n
    wire = w2s.dtype

    def red(l, stage, i, src, dst, where):
        return planned(src, dst, red_s.at[l, stage, i], red_r.at[l, stage, i], where)

    def plan(l, stage):
        if stage == 0:
            return [red(l, 0, 0, w0s.at[l], w0r.at[l], dev(me, other, mem))]
        if stage == 1:
            return [red(l, 1, 0, w1s.at[l], w1r.at[l], dev(me, lat, omem))]
        if stage == 2:
            return [
                red(l, 2, d, w2s.at[l, lon_at(d)], w2r.at[l, me], dev(lon_at(d), lat, mem)) for d in range(1, n)
            ]
        if stage == 3:
            return [red(l, 3, d, w3s.at[l], w3r.at[l, lat, me], dev(lon_at(d), lat, mem)) for d in range(1, n)]
        return [red(l, 4, 0, w3r.at[l, lat], w3r.at[l, lat], dev(me, other, mem))]

    def wgrad_copy(l):
        return pltpu.make_async_copy(wg.at[l], wgrad.at[l], io_sem.at[1 + l])

    def stage(l, step):
        if step:
            finish(plan(l, step - 1))
        if step == 0:
            w0s[l] = wacc[l, other_rows, :].astype(BF16)
        elif step == 1:
            wacc[l, own_rows, :] += w0r[l].astype(F32)
            w1s[l] = wacc[l, own_rows, other_cols].astype(BF16)
        elif step == 2:
            total = wacc[l, own_rows, own_cols] + w1r[l].astype(F32)
            wacc[l, own_rows, own_cols] = total
            w2s[l] = total.reshape(n, piece, H).astype(wire)
        elif step == 3:
            at = pl.multiple_of(lat * H + me * piece, piece)
            total = wacc[l, pl.ds(at, piece), own_cols]
            for d in range(1, n):
                total = total + w2r[l, lon_at(d)].astype(F32)
            done = (total * factor).astype(wire)
            w3s[l] = done
            w3r[l, lat, me] = done
        elif step == 5:
            wg[l] = w3r[l].reshape(C, H).astype(F32)
            start([wgrad_copy(l)])
            return
        start(plan(l, step))

    def tap_plan(step):
        if step == 0:
            near = [(lon_i, la, mm) for lon_i in (me, pair) for la in (lat, other) for mm in (mem, omem)]
            return [
                red(0, 0, j, koth if j % 2 else kown, kin.at[j - 1], dev(*near[j])) for j in range(1, 8)
            ]
        return [red(0, 2, n + d, ks2, kr2.at[me // 2], dev(lon_at(2 * d), lat, mem)) for d in range(1, n // 2)]

    def tap_stage(step):
        if step:
            finish(tap_plan(step - 1))
        if step == 0:
            for k in range(2):
                for t in range(9):
                    kv[k, t : t + 1, :] = jnp.sum(kacc[k, t], axis=0, keepdims=True)
            kown[...] = kv[:, :, own_cols].astype(BF16)
            koth[...] = kv[:, :, other_cols].astype(BF16)
        elif step == 1:
            total = kv[:, :, own_cols]
            for j in range(7):
                total = total + kin[j].astype(F32)
            both = total.astype(BF16)
            ks2[...] = both
            kr2[me // 2] = both
        else:
            ks = kr2[0].astype(F32)
            for j in range(1, n // 2):
                ks = ks + kr2[j].astype(F32)
            for k in range(2):
                kgrad[:, k, :] = ks[k, :9, :] * factor
            return
        start(tap_plan(step))

    rims0 = rim_lat_all(u0p, 0) + rim_right(u0p, 0) + rim_left(u0p, 0)
    start(rims0)

    def load1(r):
        in_copy(1, r).wait()
        g1[r] = regroup(cotraw, r)

    rows_loop(0, R, load1)
    w_copy.wait()
    early, mixed, inward = [interior_first(min(m, NK - 2)) for m in (4, 3, NK - 2)]

    def block0(i):
        wait_before(u0p, 0, i, early)
        k = pick(early, i)
        a = k * CH
        at = pl.ds(a, CH)
        conv_norm(u0p, 0, a, hid0.at[:, at], rc0.at[:, at])
        pre[...] = mix(hid0[:, at], 0)

        def go(r):
            for lanes in groups:
                gel, slope = gelu_both(pre[r, :, :, lanes])
                d0[r, at, :, lanes] = slope.astype(BF16)
                u = u0p[1 + r, pl.ds(1 + a, CH), :, lanes]
                u1p[1 + r, pl.ds(1 + a, CH), :, lanes] = u + gel.astype(BF16)

        each_row(go)
        send_after(u1p, 1, i, k, early)

    rows_loop(0, NK, block0)

    hid1, rc1, gp = (hid1_0, hid1_1), (rc1_0, rc1_1), (gp_0, gp_1)

    def block1(i, odd):
        k = pick(mixed, i)
        a = k * CH
        at = pl.ds(a, CH)
        hid, out = slot(hid1, i, odd), slot(gp, i, odd)
        conv_norm(u1p, 1, a, hid, slot(rc1, i, odd))
        pre[...] = mix(hid[...], 1)

        def go(r):
            for lanes in groups:
                slope = gelu_both(pre[r, :, :, lanes])[1]
                g = g1[r, at, :, lanes].astype(F32)
                out[r, :, :, lanes] = (g * slope).astype(BF16)

        each_row(go)

    def back1(i, odd):
        gn[...] = mix_back(slot(gp, i, odd)[...], 1)
        norm_back(g1p, slot(hid1, i, odd), slot(rc1, i, odd), pick(mixed, i) * CH)

    def send1(i):
        send_after(g1p, 2, i, pick(mixed, i), mixed)

    pipeline(lambda i: wait_before(u1p, 1, i, mixed), block1, back1, send1)
    back1(NK - 1, (NK - 1) % 2)
    send1(NK - 1)
    weight_sum(1, lambda odd, count: hid1[odd][:count].reshape(count * MC, C))
    stage(1, 0)

    def back0(i, odd):
        a = pick(inward, i) * CH
        at = pl.ds(a, CH)
        out = slot(gp, i, odd)

        def go(r):
            for lanes in groups:
                s = conv(g1p, 1, r, a, CH, lanes, True) + g1[r, at, :, lanes]
                g1[r, at, :, lanes] = s
                out[r, :, :, lanes] = s * d0[r, at, :, lanes]

        each_row(go)

    def back0_step(i, odd):
        wait_before(g1p, 2, i, inward)
        back0(i, odd)

    def back0_pair(j):
        back0_step(2 * j, 0)
        back0_step(2 * j + 1, 1)

        @pl.when(j == 1)
        def _():
            stage(1, 1)

    rows_loop(0, NK // 2, back0_pair)
    if NK % 2:
        back0_step(NK - 1, 0)

    def hidden0(odd, count):
        return jnp.concatenate(
            [hid0[:, pl.ds(inward[2 * j + odd] * CH, CH)].reshape(MC, C) for j in range(count)], axis=0
        )

    weight_sum(0, hidden0)
    stage(0, 0)

    def norm0(i, odd):
        k = pick(inward, i)
        a = k * CH
        at = pl.ds(a, CH)
        gn[...] = mix_back(slot(gp, i, odd)[...], 0)
        norm_back(g0p, hid0.at[:, at], rc0.at[:, at], a)
        send_after(g0p, 3, i, k, inward)

    def norm0_pair(j):
        norm0(2 * j, 0)
        norm0(2 * j + 1, 1)

        @pl.when(j == 1)
        def _():
            stage(0, 1)

        @pl.when(j == NK // 2 - 1)
        def _():
            stage(1, 2)

    rows_loop(0, NK // 2, norm0_pair)
    if NK % 2:
        norm0(NK - 1, 0)

    def tap_sums(k, moved, still, rev, lo, hi):
        def row(r):
            def go(a):
                for lanes in groups:
                    v = still[1 + r, pl.ds(1 + a, WIDE), :, lanes]
                    for p, prods in enumerate(products(moved, r, a, WIDE, lanes, lambda p, q: v)):
                        for q, prod in enumerate(prods):
                            add_taps(k, 3 * (2 - p) + 2 - q if rev else 3 * p + q, lanes, prod)

            chunks(go, WIDE)

        rows_loop(lo, hi, row)

    tap_sums(1, g1p, u1p, True, 0, R)
    tap_sums(0, u0p, g0p, False, 0, R // 2)
    stage(0, 2)
    tap_sums(0, u0p, g0p, False, R // 2, R)
    tap_stage(0)
    wait_all(g0p, 3)

    def out_copy(r):
        return pltpu.make_async_copy(raw.at[pl.ds(S * r, S)], out_hbm.at[0, pl.ds(S * r, S)], out_sem.at[r])

    def last(r):
        def go(a):
            for lanes in groups:
                s = conv(g0p, 0, r, a, WIDE, lanes, True) + g1[r, pl.ds(a, WIDE), :, lanes]
                row_buf[pl.ds(a, WIDE), :, lanes] = s

        chunks(go, WIDE)
        rows = jnp.dot(unperm[...], row_buf[...].reshape(M, C), preferred_element_type=F32).astype(BF16)
        raw[pl.ds(S * r, S)] = rows.reshape(S, S * A, C)
        out_copy(r).start()

    def last_step(r):
        last(r)

        @pl.when(r == 0)
        def _():
            stage(1, 3)

    rows_loop(0, R, last_step)
    tap_stage(1)
    stage(0, 3)
    stage(1, 4)
    stage(1, 5)
    tap_stage(2)
    stage(0, 4)
    stage(0, 5)
    finish([wgrad_copy(l) for l in range(2)])
    finish([out_copy(r) for r in range(R)])


def hand_over(pieces, *refs):
    srcs, dsts, mids, sem = refs[:3], refs[3:6], refs[6:9], refs[9]
    step = srcs[0].shape[1] // pieces
    parts = [tuple(ref.at[:, pl.ds(i * step, step)] for ref in (srcs[0], mids[0], dsts[0])) for i in range(pieces)]
    parts += [(srcs[j], mids[j], dsts[j]) for j in (2, 1)]
    loads = [pltpu.make_async_copy(a, b, sem.at[0, i]) for i, (a, b, _) in enumerate(parts)]
    stores = [pltpu.make_async_copy(b, c, sem.at[1, i]) for i, (_, b, c) in enumerate(parts)]
    for c in loads:
        c.start()
    for a, b in zip(loads, stores):
        a.wait()
        b.start()
    for c in stores:
        c.wait()


def body(inputs, cotangent, dw_kernel, pw_weight):
    _, rows, cols, C = inputs.shape
    n = lax.axis_size("lon")
    R, A, T, H = rows // S, cols // S, S * S, C // 2
    piece = H // n
    wire = BF16 if piece % 16 == 0 else F32
    samples = inputs.size // C * n * lax.axis_size("lat") * lax.axis_size("mem")
    anywhere = pl.BlockSpec(memory_space=pl.ANY)
    local = pl.BlockSpec(memory_space=pltpu.VMEM)
    padded = pltpu.VMEM((R + 2, A + 2, T, C), BF16)
    cells = pltpu.VMEM((R, A, T, C), BF16)
    CH = max(c for c in (1, 2, 4) if A % c == 0)
    chunk = pltpu.VMEM((R, CH, T, C), BF16)
    half = (A // CH + 1) // 2
    steps = pltpu.VMEM((half, R, CH, T, C), BF16)
    scoped = [
        padded, padded, padded, padded,
        cells, cells, cells,
        pltpu.VMEM((R, A, T, 128), F32),
        steps, steps,
        pltpu.VMEM((half, R, CH, T, 128), F32), pltpu.VMEM((half, R, CH, T, 128), F32),
        steps, steps,
        pltpu.VMEM((R, CH, T, C), F32),
        chunk,
        pltpu.VMEM((A, T, C), BF16),
        pltpu.VMEM((2, 9, T, C), BF16),
    ]
    scratch = [
        pltpu.VMEM((rows, cols, C), BF16),
        pltpu.VMEM((rows, cols, C), BF16),
        pltpu.VMEM((A * T, A * T), BF16),
        pltpu.VMEM((A * T, A * T), BF16),
        pltpu.VMEM((2, 9, 8, C), F32),
        pltpu.VMEM((2, C, C), F32),
        pltpu.VMEM((2, H, C), BF16), pltpu.VMEM((2, H, C), BF16),
        pltpu.VMEM((2, H, H), BF16), pltpu.VMEM((2, H, H), BF16),
        pltpu.VMEM((2, n, piece, H), wire), pltpu.VMEM((2, n, piece, H), wire),
        pltpu.VMEM((2, piece, H), wire), pltpu.VMEM((2, 2, n, piece, H), wire),
        pltpu.VMEM((2, 16, C), F32),
        pltpu.VMEM((2, 16, H), BF16), pltpu.VMEM((2, 16, H), BF16), pltpu.VMEM((7, 2, 16, H), BF16),
        pltpu.VMEM((2, 16, H), BF16), pltpu.VMEM((n // 2, 2, 16, H), BF16),
        pltpu.VMEM((2, C, C), BF16), pltpu.VMEM((2, C, H), F32), pltpu.SemaphoreType.DMA((3,)),
        pltpu.SemaphoreType.DMA((2, R)), pltpu.SemaphoreType.DMA((R,)),
        pltpu.SemaphoreType.DMA((4, 4 + A // CH)), pltpu.SemaphoreType.DMA((4, 4 + A // CH)),
        pltpu.SemaphoreType.DMA((2, 5, 2 * n)), pltpu.SemaphoreType.DMA((2, 5, 2 * n)),
    ]
    made = pl.pallas_call(
        functools.partial(kernel, n, 1.0 / math.sqrt(samples), scoped),
        out_shape=(
            jax.ShapeDtypeStruct(inputs.shape, BF16),
            jax.ShapeDtypeStruct((9, 2, H), F32),
            jax.ShapeDtypeStruct((2, C, H), F32),
        ),
        in_specs=[anywhere, anywhere, local, anywhere],
        out_specs=(anywhere, local, anywhere),
        scratch_shapes=scratch,
        name="blocks",
        compiler_params=pltpu.CompilerParams(
            collective_id=0, has_side_effects=True, vmem_limit_bytes=60 * 1024 * 1024
        ),
    )(inputs, cotangent, jnp.transpose(dw_kernel, (1, 0, 2)), pw_weight)
    pieces = max(p for p in (1, 2, 3, 4, 6, 8) if rows % p == 0)
    out, kgrad, wgrad = pl.pallas_call(
        functools.partial(hand_over, pieces),
        out_shape=tuple(jax.ShapeDtypeStruct(v.shape, v.dtype) for v in made),
        in_specs=[anywhere] * 3,
        out_specs=(anywhere,) * 3,
        scratch_shapes=[*(pltpu.VMEM(v.shape, v.dtype) for v in made), pltpu.SemaphoreType.DMA((2, pieces + 2))],
        compiler_params=pltpu.CompilerParams(vmem_limit_bytes=60 * 1024 * 1024),
        name="hand_over",
    )(*made)
    return out, jnp.transpose(kgrad, (1, 0, 2)), wgrad


def solution(mesh):
    placed = (P("mem", "lat", "lon", None), P("mem", "lat", "lon", None), P(), P())
    return jax.shard_map(
        body,
        mesh=mesh,
        in_specs=placed,
        out_specs=(P("mem", "lat", "lon", None), P(None, None, "mem"), P(None, None, "mem")),
        check_vma=False,
    )
```

```python
import functools
import math

import jax
import jax.numpy as jnp
from jax import lax
from jax.experimental import pallas as pl
from jax.experimental.pallas import tpu as pltpu
from jax.sharding import PartitionSpec as P

S = 4
F32 = jnp.float32
BF16 = jnp.bfloat16
MESH = pl.DeviceIdType.MESH
ROOT = math.sqrt(2.0 / math.pi)
CUBE = 0.044715


def gelu_both(x):
    xx = x * x
    t = jnp.tanh(x * (ROOT + (ROOT * CUBE) * xx))
    h = 0.5 + 0.5 * t
    g = x * h
    return g, h + g * (1.0 - t) * (ROOT + (3.0 * ROOT * CUBE) * xx)


def kernel(n, factor, scoped, *refs):
    pl.run_scoped(lambda *inner: work(n, factor, *refs, *inner), *scoped)


def work(
    n, factor,
    x_hbm, cot_hbm, dw_ref, w_hbm,
    out_hbm, kgrad, wgrad,
    raw, cotraw, perm, perm_rest, unperm, kacc, wacc,
    w0s, w0r, w1s, w1r, w2s, w2r, w3s, w3r, kv, kown, koth, kin, ks2, kr2,
    w_ref, wg, io_sem,
    in_sem, out_sem, rim_s, rim_r, red_s, red_r,
    u0p, u1p, g1p, g0p, g1, hid0, d0, rc0, hid1_0, hid1_1, rc1_0, rc1_1, gp_0, gp_1, pre, gn, row_buf, kb,
):
    R, A, T, C = hid0.shape
    M = A * T
    H = C // 2
    CH = gn.shape[1]
    NK = A // CH
    MC = R * CH * T
    WIDE = max(c for c in (1, 2, 4, 7) if A % c == 0)
    groups = [slice(g, g + 128) for g in range(0, C, 128)]
    me, lat, mem = lax.axis_index("lon"), lax.axis_index("lat"), lax.axis_index("mem")
    other, omem = 1 - lat, 1 - mem
    pair = me + 1 - 2 * (me % 2)

    def lon_at(d):
        return lax.rem(me + (d % n), n)

    def dev(lon_i, lat_i, mem_i):
        return {"lon": lon_i, "lat": lat_i, "mem": mem_i}

    def planned(src, dst, ssem, rsem, where):
        return pltpu.make_async_remote_copy(
            src_ref=src, dst_ref=dst, send_sem=ssem, recv_sem=rsem, device_id=where, device_id_type=MESH
        )

    def in_copy(i, r):
        src, dst = ((x_hbm, raw), (cot_hbm, cotraw))[i]
        return pltpu.make_async_copy(src.at[0, pl.ds(S * r, S)], dst.at[pl.ds(S * r, S)], in_sem.at[i, r])

    for i in range(2):
        for r in range(R):
            in_copy(i, r).start()
    w_copy = pltpu.make_async_copy(w_hbm, w_ref, io_sem.at[0])
    w_copy.start()

    barrier = pltpu.get_barrier_semaphore()
    for d in range(n):
        for la in (lat, other):
            if d == 0 and la is lat:
                continue
            pl.semaphore_signal(barrier, inc=1, device_id=dev(lon_at(d), la, mem), device_id_type=MESH)
    for lon_i in (me, pair):
        for la in (lat, other):
            pl.semaphore_signal(barrier, inc=1, device_id=dev(lon_i, la, omem), device_id_type=MESH)

    def one_hot(rows_dim, groups_a):
        m = groups_a * T
        o = lax.broadcasted_iota(jnp.int32, (m, m), rows_dim)
        i = lax.broadcasted_iota(jnp.int32, (m, m), 1 - rows_dim)
        a, s, b = o >> 4, (o >> 2) & 3, o & 3
        return jnp.where(i == s * (groups_a * S) + a * S + b, 1.0, 0.0).astype(BF16)

    parts = [(a, min(perm.shape[0] // T, A - a)) for a in range(0, A, perm.shape[0] // T)]
    perm[...] = one_hot(0, perm.shape[0] // T)
    perm_rest[...] = one_hot(0, perm_rest.shape[0] // T)
    unperm[...] = one_hot(1, A)
    for t in range(9):
        taps_f = dw_ref[t].astype(F32)
        for l in range(2):
            kb[l, t] = jnp.broadcast_to(taps_f[l : l + 1, :], (T, C)).astype(BF16)
    kacc[...] = jnp.zeros_like(kacc)
    kv[...] = jnp.zeros_like(kv)
    edge = lat * (R + 1)
    for ref in (u0p, u1p, g1p, g0p):
        ref[edge] = jnp.zeros(ref.shape[1:], BF16)

    def rows_loop(lo, hi, fn):
        def step(r, c):
            fn(r)
            return c

        lax.fori_loop(lo, hi, step, 0)

    def regroup(src, r):
        out = []
        for a, count in parts:
            rows = src[pl.ds(S * r, S), S * a : S * (a + count)].reshape(count * T, C)
            order = perm if count * T == perm.shape[0] else perm_rest
            out.append(jnp.dot(order[...], rows, preferred_element_type=F32).astype(BF16).reshape(count, T, C))
        return jnp.concatenate(out, axis=0)


    def load0(r):
        in_copy(0, r).wait()
        u0p[1 + r, 1 : A + 1] = regroup(raw, r)

    rows_loop(0, R, load0)

    pl.semaphore_wait(barrier, 2 * n + 3)

    right, left = lon_at(1), lon_at(-1)

    def rim(ref, e, i, src, dst, where):
        return planned(ref.at[src], ref.at[dst], rim_s.at[e, i], rim_r.at[e, i], where)

    seam = R - lat * (R - 1)
    inner = pl.ds(1, R)

    def rim_right(ref, e):
        last, first = pl.ds(A, 1), pl.ds(0, 1)
        return [
            rim(ref, e, 0, (inner, last), (inner, first), dev(right, lat, mem)),
            rim(ref, e, 2, (seam, last), (edge, first), dev(right, other, mem)),
        ]

    def rim_left(ref, e):
        first, last = pl.ds(1, 1), pl.ds(A + 1, 1)
        return [
            rim(ref, e, 1, (inner, first), (inner, last), dev(left, lat, mem)),
            rim(ref, e, 3, (seam, first), (edge, last), dev(left, other, mem)),
        ]

    def rim_lat(ref, e, k):
        at = pl.ds(1 + k * CH, CH)
        return [rim(ref, e, 4 + k, (seam, at), (edge, at), dev(me, other, mem))]

    def rim_lat_all(ref, e):
        at = pl.ds(1, A)
        return [rim(ref, e, 4, (seam, at), (edge, at), dev(me, other, mem))]

    def interior_first(m):
        return [*range(1, 1 + m), NK - 1, 0, *range(1 + m, NK - 1)]

    def pick(order, i):
        return sum(k * ((i + NK - j) // NK - (i + NK - j - 1) // NK) for j, k in enumerate(order))

    def send_after(ref, e, i, k, order):
        start(rim_lat(ref, e, k))

        @pl.when(i == order.index(NK - 1))
        def _():
            start(rim_right(ref, e))

        @pl.when(i == order.index(0))
        def _():
            start(rim_left(ref, e))

    def wait_before(ref, e, i, order):
        done = set()
        for j, k in enumerate(order):
            need = [p for p in (k - 1, k, k + 1) if 0 <= p < NK and p not in done]
            done.update(need)
            if e == 0:
                need = [0] if j == 0 else []
            if not need and 0 < k < NK - 1:
                continue

            @pl.when(i == j)
            def _(k=k, need=need):
                for p in need:
                    finish(rim_lat(ref, e, p) if e else rim_lat_all(ref, e))
                if k == NK - 1:
                    finish(rim_left(ref, e))
                if k == 0:
                    finish(rim_right(ref, e))

    def wait_all(ref, e):
        for k in range(NK):
            finish(rim_lat(ref, e, k))
        finish(rim_left(ref, e) + rim_right(ref, e))

    def start(copies):
        for c in copies:
            c.start()

    def finish(copies):
        for c in copies:
            c.wait()

    def products(ref, r, a, ch, lanes, other_factor):
        for p in range(3):
            row = ref[r + p, pl.ds(a, ch + 2), :, lanes]
            yield [row[q : q + ch] * other_factor(p, q) for q in range(3)]

    def conv(ref, l, r, a, ch, lanes, rev):
        def tap(p, q):
            return kb[l, 3 * (2 - p) + 2 - q if rev else 3 * p + q, :, lanes]

        s0, s1, s2 = [v[0] + v[1] + v[2] for v in products(ref, r, a, ch, lanes, tap)]
        return s0 + s1 + s2

    def chunks(fn, ch, unroll=False):
        def step(i, c):
            fn(i * ch)
            return c

        lax.fori_loop(0, A // ch, step, 0, unroll=unroll)

    def each_row(fn):
        def step(r, c):
            fn(r)
            return c

        lax.fori_loop(0, R, step, 0, unroll=True)

    def tree(v):
        v = [v[i] for i in range(v.shape[0])]
        while len(v) > 1:
            v = [a + b for a, b in zip(v[::2], v[1::2])] + v[len(v) - len(v) % 2 :]
        return v[0]

    def add_taps(k, t, lanes, prod):
        both = tree(prod).astype(F32).reshape(2, 8, 128)
        kacc[k, t, :, lanes] += both[0] + both[1]

    def lane_mean(v, ch):
        m = jnp.sum(v.astype(F32), axis=-1, keepdims=True) * (1.0 / C)
        return jnp.broadcast_to(m, (ch, T, 128))

    def conv_norm(src, l, a, hid, rc):
        def go(r):
            convs = [conv(src, l, r, a, CH, lanes, False) for lanes in groups]
            c0, c1, c2, c3 = [c * c for c in convs]
            recip = lax.rsqrt(lane_mean((c0 + c1) + (c2 + c3), CH) + 1e-6)
            rc[r] = recip
            for lanes, c in zip(groups, convs):
                hid[r, :, :, lanes] = (c.astype(F32) * recip).astype(BF16)

        each_row(go)

    def mix(v, l):
        return jnp.dot(v.reshape(MC, C), w_ref[l], preferred_element_type=F32).reshape(R, CH, T, C)

    def mix_back(v, l):
        return lax.dot_general(
            v.reshape(MC, C), w_ref[l], (((1,), (1,)), ((), ())), preferred_element_type=F32
        ).astype(BF16).reshape(R, CH, T, C)

    def norm_back(dst, hid, rc, a):
        def go(r):
            ns = [hid[r, :, :, lanes] for lanes in groups]
            gs = [gn[r, :, :, lanes] for lanes in groups]
            d0_, d1_, d2_, d3_ = [g * v for g, v in zip(gs, ns)]
            mean = lane_mean((d0_ + d1_) + (d2_ + d3_), CH)
            recip = rc[r]
            for lanes, g, v in zip(groups, gs, ns):
                back = recip * (g.astype(F32) - v.astype(F32) * mean)
                dst[1 + r, pl.ds(1 + a, CH), :, lanes] = back.astype(BF16)

        each_row(go)

    def weight_sum(l, hid_of):
        for odd in range(2):
            count = (NK + 1 - odd) // 2
            grads = gp[odd][:count].reshape(count * MC, C)
            part = lax.dot_general(
                hid_of(odd, count), grads, (((0,), (0,)), ((), ())), preferred_element_type=F32
            )
            wacc[l] = wacc[l] + part if odd else part

    def slot(pair, i, odd):
        return pair[odd].at[i // 2]

    def pipeline(before, first, second, after):
        before(0)
        first(0, 0)

        def both(i, odd):
            before(i)
            second(i - 1, 1 - odd)
            first(i, odd)
            after(i - 1)

        def step(j, c):
            both(2 * j + 1, 1)
            both(2 * j + 2, 0)
            return c

        lax.fori_loop(0, (NK - 1) // 2, step, 0)
        if NK % 2 == 0:
            both(NK - 1, 1)

    own_rows = pl.ds(pl.multiple_of(lat * H, H), H)
    other_rows = pl.ds(pl.multiple_of(other * H, H), H)
    own_cols = pl.ds(pl.multiple_of(mem * H, H), H)
    other_cols = pl.ds(pl.multiple_of(omem * H, H), H)
    piece = H // n
    wire = w2s.dtype

    def red(l, stage, i, src, dst, where):
        return planned(src, dst, red_s.at[l, stage, i], red_r.at[l, stage, i], where)

    def plan(l, stage):
        if stage == 0:
            return [red(l, 0, 0, w0s.at[l], w0r.at[l], dev(me, other, mem))]
        if stage == 1:
            return [red(l, 1, 0, w1s.at[l], w1r.at[l], dev(me, lat, omem))]
        if stage == 2:
            return [
                red(l, 2, d, w2s.at[l, lon_at(d)], w2r.at[l, me], dev(lon_at(d), lat, mem)) for d in range(1, n)
            ]
        if stage == 3:
            return [red(l, 3, d, w3s.at[l], w3r.at[l, lat, me], dev(lon_at(d), lat, mem)) for d in range(1, n)]
        return [red(l, 4, 0, w3r.at[l, lat], w3r.at[l, lat], dev(me, other, mem))]

    def wgrad_copy(l):
        return pltpu.make_async_copy(wg.at[l], wgrad.at[l], io_sem.at[1 + l])

    def stage(l, step):
        if step:
            finish(plan(l, step - 1))
        if step == 0:
            w0s[l] = wacc[l, other_rows, :].astype(BF16)
        elif step == 1:
            wacc[l, own_rows, :] += w0r[l].astype(F32)
            w1s[l] = wacc[l, own_rows, other_cols].astype(BF16)
        elif step == 2:
            total = wacc[l, own_rows, own_cols] + w1r[l].astype(F32)
            wacc[l, own_rows, own_cols] = total
            w2s[l] = total.reshape(n, piece, H).astype(wire)
        elif step == 3:
            at = pl.multiple_of(lat * H + me * piece, piece)
            total = wacc[l, pl.ds(at, piece), own_cols]
            for d in range(1, n):
                total = total + w2r[l, lon_at(d)].astype(F32)
            done = (total * factor).astype(wire)
            w3s[l] = done
            w3r[l, lat, me] = done
        elif step == 5:
            wg[l] = w3r[l].reshape(C, H).astype(F32)
            start([wgrad_copy(l)])
            return
        start(plan(l, step))

    def tap_plan(step):
        if step == 0:
            near = [(lon_i, la, mm) for lon_i in (me, pair) for la in (lat, other) for mm in (mem, omem)]
            return [
                red(0, 0, j, koth if j % 2 else kown, kin.at[j - 1], dev(*near[j])) for j in range(1, 8)
            ]
        return [red(0, 2, n + d, ks2, kr2.at[me // 2], dev(lon_at(2 * d), lat, mem)) for d in range(1, n // 2)]

    def tap_stage(step):
        if step:
            finish(tap_plan(step - 1))
        if step == 0:
            for k in range(2):
                for t in range(9):
                    kv[k, t : t + 1, :] = jnp.sum(kacc[k, t], axis=0, keepdims=True)
            kown[...] = kv[:, :, own_cols].astype(BF16)
            koth[...] = kv[:, :, other_cols].astype(BF16)
        elif step == 1:
            total = kv[:, :, own_cols]
            for j in range(7):
                total = total + kin[j].astype(F32)
            both = total.astype(BF16)
            ks2[...] = both
            kr2[me // 2] = both
        else:
            ks = kr2[0].astype(F32)
            for j in range(1, n // 2):
                ks = ks + kr2[j].astype(F32)
            for k in range(2):
                kgrad[:, k, :] = ks[k, :9, :] * factor
            return
        start(tap_plan(step))

    rims0 = rim_lat_all(u0p, 0) + rim_right(u0p, 0) + rim_left(u0p, 0)
    start(rims0)

    def load1(r):
        in_copy(1, r).wait()
        g1[r] = regroup(cotraw, r)

    rows_loop(0, R, load1)
    w_copy.wait()
    early, mixed, inward = [interior_first(min(m, NK - 2)) for m in (4, 3, NK - 2)]

    def block0(i):
        wait_before(u0p, 0, i, early)
        k = pick(early, i)
        a = k * CH
        at = pl.ds(a, CH)
        conv_norm(u0p, 0, a, hid0.at[:, at], rc0.at[:, at])
        pre[...] = mix(hid0[:, at], 0)

        def go(r):
            for lanes in groups:
                gel, slope = gelu_both(pre[r, :, :, lanes])
                d0[r, at, :, lanes] = slope.astype(BF16)
                u = u0p[1 + r, pl.ds(1 + a, CH), :, lanes]
                u1p[1 + r, pl.ds(1 + a, CH), :, lanes] = u + gel.astype(BF16)

        each_row(go)
        send_after(u1p, 1, i, k, early)

    rows_loop(0, NK, block0)

    hid1, rc1, gp = (hid1_0, hid1_1), (rc1_0, rc1_1), (gp_0, gp_1)

    def block1(i, odd):
        k = pick(mixed, i)
        a = k * CH
        at = pl.ds(a, CH)
        hid, out = slot(hid1, i, odd), slot(gp, i, odd)
        conv_norm(u1p, 1, a, hid, slot(rc1, i, odd))
        pre[...] = mix(hid[...], 1)

        def go(r):
            for lanes in groups:
                slope = gelu_both(pre[r, :, :, lanes])[1]
                g = g1[r, at, :, lanes].astype(F32)
                out[r, :, :, lanes] = (g * slope).astype(BF16)

        each_row(go)

    def back1(i, odd):
        gn[...] = mix_back(slot(gp, i, odd)[...], 1)
        norm_back(g1p, slot(hid1, i, odd), slot(rc1, i, odd), pick(mixed, i) * CH)

    def send1(i):
        send_after(g1p, 2, i, pick(mixed, i), mixed)

    pipeline(lambda i: wait_before(u1p, 1, i, mixed), block1, back1, send1)
    back1(NK - 1, (NK - 1) % 2)
    send1(NK - 1)
    weight_sum(1, lambda odd, count: hid1[odd][:count].reshape(count * MC, C))
    stage(1, 0)

    def back0(i, odd):
        a = pick(inward, i) * CH
        at = pl.ds(a, CH)
        out = slot(gp, i, odd)

        def go(r):
            for lanes in groups:
                s = conv(g1p, 1, r, a, CH, lanes, True) + g1[r, at, :, lanes]
                g1[r, at, :, lanes] = s
                out[r, :, :, lanes] = s * d0[r, at, :, lanes]

        each_row(go)

    def back0_step(i, odd):
        wait_before(g1p, 2, i, inward)
        back0(i, odd)

    def back0_pair(j):
        back0_step(2 * j, 0)
        back0_step(2 * j + 1, 1)

        @pl.when(j == 1)
        def _():
            stage(1, 1)

    rows_loop(0, NK // 2, back0_pair)
    if NK % 2:
        back0_step(NK - 1, 0)

    def hidden0(odd, count):
        return jnp.concatenate(
            [hid0[:, pl.ds(inward[2 * j + odd] * CH, CH)].reshape(MC, C) for j in range(count)], axis=0
        )

    weight_sum(0, hidden0)
    stage(0, 0)

    def norm0(i, odd):
        k = pick(inward, i)
        a = k * CH
        at = pl.ds(a, CH)
        gn[...] = mix_back(slot(gp, i, odd)[...], 0)
        norm_back(g0p, hid0.at[:, at], rc0.at[:, at], a)
        send_after(g0p, 3, i, k, inward)

    def norm0_pair(j):
        norm0(2 * j, 0)
        norm0(2 * j + 1, 1)

        @pl.when(j == 1)
        def _():
            stage(0, 1)

        @pl.when(j == NK // 2 - 1)
        def _():
            stage(1, 2)

    rows_loop(0, NK // 2, norm0_pair)
    if NK % 2:
        norm0(NK - 1, 0)

    def tap_sums(k, moved, still, rev, lo, hi):
        def row(r):
            def go(a):
                for lanes in groups:
                    v = still[1 + r, pl.ds(1 + a, WIDE), :, lanes]
                    for p, prods in enumerate(products(moved, r, a, WIDE, lanes, lambda p, q: v)):
                        for q, prod in enumerate(prods):
                            add_taps(k, 3 * (2 - p) + 2 - q if rev else 3 * p + q, lanes, prod)

            chunks(go, WIDE)

        rows_loop(lo, hi, row)

    tap_sums(1, g1p, u1p, True, 0, R)
    tap_sums(0, u0p, g0p, False, 0, R // 2)
    stage(0, 2)
    tap_sums(0, u0p, g0p, False, R // 2, R)
    tap_stage(0)
    wait_all(g0p, 3)

    def out_copy(r):
        return pltpu.make_async_copy(raw.at[pl.ds(S * r, S)], out_hbm.at[0, pl.ds(S * r, S)], out_sem.at[r])

    def last(r):
        def go(a):
            for lanes in groups:
                s = conv(g0p, 0, r, a, WIDE, lanes, True) + g1[r, pl.ds(a, WIDE), :, lanes]
                row_buf[pl.ds(a, WIDE), :, lanes] = s

        chunks(go, WIDE)
        rows = jnp.dot(unperm[...], row_buf[...].reshape(M, C), preferred_element_type=F32).astype(BF16)
        raw[pl.ds(S * r, S)] = rows.reshape(S, S * A, C)
        out_copy(r).start()

    def last_step(r):
        last(r)

        @pl.when(r == 0)
        def _():
            stage(1, 3)

    rows_loop(0, R, last_step)
    tap_stage(1)
    stage(0, 3)
    stage(1, 4)
    stage(1, 5)
    tap_stage(2)
    stage(0, 4)
    stage(0, 5)
    finish([wgrad_copy(l) for l in range(2)])
    finish([out_copy(r) for r in range(R)])


def hand_over(pieces, *refs):
    srcs, dsts, mids, sem = refs[:3], refs[3:6], refs[6:9], refs[9]
    step = srcs[0].shape[1] // pieces
    parts = [tuple(ref.at[:, pl.ds(i * step, step)] for ref in (srcs[0], mids[0], dsts[0])) for i in range(pieces)]
    parts += [(srcs[j], mids[j], dsts[j]) for j in (2, 1)]
    loads = [pltpu.make_async_copy(a, b, sem.at[0, i]) for i, (a, b, _) in enumerate(parts)]
    stores = [pltpu.make_async_copy(b, c, sem.at[1, i]) for i, (_, b, c) in enumerate(parts)]
    for c in loads:
        c.start()
    for a, b in zip(loads, stores):
        a.wait()
        b.start()
    for c in stores:
        c.wait()


def body(inputs, cotangent, dw_kernel, pw_weight):
    _, rows, cols, C = inputs.shape
    n = lax.axis_size("lon")
    R, A, T, H = rows // S, cols // S, S * S, C // 2
    piece = H // n
    wire = BF16 if piece % 16 == 0 else F32
    samples = inputs.size // C * n * lax.axis_size("lat") * lax.axis_size("mem")
    anywhere = pl.BlockSpec(memory_space=pl.ANY)
    local = pl.BlockSpec(memory_space=pltpu.VMEM)
    padded = pltpu.VMEM((R + 2, A + 2, T, C), BF16)
    cells = pltpu.VMEM((R, A, T, C), BF16)
    CH = max(c for c in (1, 2, 4) if A % c == 0)
    chunk = pltpu.VMEM((R, CH, T, C), BF16)
    half = (A // CH + 1) // 2
    steps = pltpu.VMEM((half, R, CH, T, C), BF16)
    scoped = [
        padded, padded, padded, padded,
        cells, cells, cells,
        pltpu.VMEM((R, A, T, 128), F32),
        steps, steps,
        pltpu.VMEM((half, R, CH, T, 128), F32), pltpu.VMEM((half, R, CH, T, 128), F32),
        steps, steps,
        pltpu.VMEM((R, CH, T, C), F32),
        chunk,
        pltpu.VMEM((A, T, C), BF16),
        pltpu.VMEM((2, 9, T, C), BF16),
    ]
    scratch = [
        pltpu.VMEM((rows, cols, C), BF16),
        pltpu.VMEM((rows, cols, C), BF16),
        pltpu.VMEM((min(A, 16) * T, min(A, 16) * T), BF16),
        pltpu.VMEM((((A - 1) % 16 + 1) * T, ((A - 1) % 16 + 1) * T), BF16),
        pltpu.VMEM((A * T, A * T), BF16),
        pltpu.VMEM((2, 9, 8, C), F32),
        pltpu.VMEM((2, C, C), F32),
        pltpu.VMEM((2, H, C), BF16), pltpu.VMEM((2, H, C), BF16),
        pltpu.VMEM((2, H, H), BF16), pltpu.VMEM((2, H, H), BF16),
        pltpu.VMEM((2, n, piece, H), wire), pltpu.VMEM((2, n, piece, H), wire),
        pltpu.VMEM((2, piece, H), wire), pltpu.VMEM((2, 2, n, piece, H), wire),
        pltpu.VMEM((2, 16, C), F32),
        pltpu.VMEM((2, 16, H), BF16), pltpu.VMEM((2, 16, H), BF16), pltpu.VMEM((7, 2, 16, H), BF16),
        pltpu.VMEM((2, 16, H), BF16), pltpu.VMEM((n // 2, 2, 16, H), BF16),
        pltpu.VMEM((2, C, C), BF16), pltpu.VMEM((2, C, H), F32), pltpu.SemaphoreType.DMA((3,)),
        pltpu.SemaphoreType.DMA((2, R)), pltpu.SemaphoreType.DMA((R,)),
        pltpu.SemaphoreType.DMA((4, 4 + A // CH)), pltpu.SemaphoreType.DMA((4, 4 + A // CH)),
        pltpu.SemaphoreType.DMA((2, 5, 2 * n)), pltpu.SemaphoreType.DMA((2, 5, 2 * n)),
    ]
    made = pl.pallas_call(
        functools.partial(kernel, n, 1.0 / math.sqrt(samples), scoped),
        out_shape=(
            jax.ShapeDtypeStruct(inputs.shape, BF16),
            jax.ShapeDtypeStruct((9, 2, H), F32),
            jax.ShapeDtypeStruct((2, C, H), F32),
        ),
        in_specs=[anywhere, anywhere, local, anywhere],
        out_specs=(anywhere, local, anywhere),
        scratch_shapes=scratch,
        name="blocks",
        compiler_params=pltpu.CompilerParams(
            collective_id=0, has_side_effects=True, vmem_limit_bytes=60 * 1024 * 1024
        ),
    )(inputs, cotangent, jnp.transpose(dw_kernel, (1, 0, 2)), pw_weight)
    pieces = max(p for p in (1, 2, 3, 4, 6, 8) if rows % p == 0)
    out, kgrad, wgrad = pl.pallas_call(
        functools.partial(hand_over, pieces),
        out_shape=tuple(jax.ShapeDtypeStruct(v.shape, v.dtype) for v in made),
        in_specs=[anywhere] * 3,
        out_specs=(anywhere,) * 3,
        scratch_shapes=[*(pltpu.VMEM(v.shape, v.dtype) for v in made), pltpu.SemaphoreType.DMA((2, pieces + 2))],
        compiler_params=pltpu.CompilerParams(vmem_limit_bytes=60 * 1024 * 1024),
        name="hand_over",
    )(*made)
    return out, jnp.transpose(kgrad, (1, 0, 2)), wgrad


def solution(mesh):
    placed = (P("mem", "lat", "lon", None), P("mem", "lat", "lon", None), P(), P())
    return jax.shard_map(
        body,
        mesh=mesh,
        in_specs=placed,
        out_specs=(P("mem", "lat", "lon", None), P(None, None, "mem"), P(None, None, "mem")),
        check_vma=False,
    )
```
